32 devices in a mesh: head: 2 (over core), seq: 16 (over z, y, x).
Axes of the slice: x: 2, y: 2, z: 4, core: 2. Of those that a mesh axis runs over, the one named last changes fastest.
Arguments:
- queries: bfloat16 [8192, 5120], P(('seq', 'head')), may hold values from -8 to 8
- key_states: bfloat16 [8192, 5120], P(('seq', 'head')), may hold values from -8 to 8
- value_states: bfloat16 [8192, 5120], P(('seq', 'head')), may hold values from -6 to 6
- cluster_perm: int32 [40, 8192], P('head', 'seq'), may hold values from 0 to 8191, as said below
- block_mask: int32 [40, 64, 64], P('head', 'seq'), may hold values from 0 to 1, as said below
Outputs:
- attention_out: bfloat16 [8192, 5120], P(('seq', 'head'))
The draws below stay inside these ranges and needn't reach their ends.
Inputs may be any that keep to these rules, and one draw needn't show every extreme that they name: `cluster_perm`: for each head, positions k * 512 to (k + 1) * 512 - 1 list the tokens k * 512 to (k + 1) * 512 - 1, each once. `block_mask`: for each head and each aligned run of 4 query blocks, the key blocks used by some query block of the run number exactly 1. For such a run and the 20 heads g * 20 to (g + 1) * 20 - 1, the (head, key block) pairs so used that lie in one aligned run of 4 key blocks number at most 2, and exactly 2 in some run. Every query block uses 1 to 1 key blocks, and some query block of every run uses 1, for every head.
All inputs are finite; a program needn't handle non-finite values.
Results may differ from the reference program's by a relative error of at most 0.0049.
Values may be sent and summed in bfloat16 or wider, within the bound.
A program may use at most 128 MiB of HBM per device.

```python
import math
import jax
import jax.numpy as jnp
from jax import lax

HEADS = 40
HEAD_DIM = 128
BLOCK = 128
ROWS_SEQ = 512
TOKENS = 8192
BLOCKS = 64
PICKS = 1
LIVE = 1
CAP = 2
N_HEAD = 2
N_SEQ = 16


def draw_queries(key, part):
    gaussian = jax.random.truncated_normal(jax.random.fold_in(key, 11), -6.0, 6.0, (TOKENS, HEADS, HEAD_DIM), jnp.float32)
    return gaussian.reshape(TOKENS, HEADS * HEAD_DIM).astype(jnp.bfloat16)


def draw_key_states(key, part):
    gaussian = jax.random.truncated_normal(jax.random.fold_in(key, 21), -6.0, 6.0, (TOKENS, HEADS, HEAD_DIM), jnp.float32)
    return gaussian.reshape(TOKENS, HEADS * HEAD_DIM).astype(jnp.bfloat16)


def draw_cluster_perm(key, part):
    random_bits = jax.random.bits(jax.random.fold_in(key, 31), (HEADS, N_SEQ, ROWS_SEQ))
    local_order = jnp.argsort(random_bits, axis=-1, stable=True).astype(jnp.int32)
    offsets = (jnp.arange(N_SEQ, dtype=jnp.int32) * ROWS_SEQ)[None, :, None]
    return (local_order + offsets).reshape(HEADS, TOKENS)


def draw_block_mask(key, part):
    heads_group = HEADS // N_HEAD
    shard_blocks = ROWS_SEQ // BLOCK
    slot_count = N_SEQ * CAP
    filled_count = heads_group * PICKS
    slot_owner = jnp.arange(slot_count, dtype=jnp.int32) // CAP
    slot_index = jnp.arange(slot_count, dtype=jnp.int32) % CAP
    star_owner = jax.random.randint(jax.random.fold_in(key, 41), (N_HEAD, N_SEQ), 0, N_SEQ)
    jitter = jax.random.randint(jax.random.fold_in(key, 42), (N_HEAD, N_SEQ, slot_count), 0, 1 << 20)
    priority = jitter + jnp.where(slot_owner[None, None, :] == star_owner[:, :, None], 0, 1 << 21)
    ranking = jnp.argsort(priority, axis=-1, stable=True)
    position = jnp.argsort(ranking, axis=-1, stable=True).astype(jnp.int32)
    is_filled = (position < filled_count).astype(jnp.int32)
    head_local = position % heads_group
    rotate = jax.random.randint(jax.random.fold_in(key, 43), (N_HEAD, N_SEQ, N_SEQ * heads_group), 0, shard_blocks)
    rot_pick = jnp.take_along_axis(rotate, slot_owner[None, None, :] * heads_group + head_local, axis=-1)
    key_block = slot_owner[None, None, :] * shard_blocks + (slot_index[None, None, :] + rot_pick) % shard_blocks
    group_ids = jnp.arange(N_HEAD, dtype=jnp.int32)[:, None, None]
    shard_ids = jnp.arange(N_SEQ, dtype=jnp.int32)[None, :, None]
    needed = jnp.zeros((N_HEAD, N_SEQ, heads_group, BLOCKS), jnp.int32)
    needed = needed.at[group_ids, shard_ids, head_local, key_block].max(is_filled)
    prefix = (jnp.cumsum(needed, axis=-1) - needed).astype(jnp.int32)
    chosen = (needed[..., None] == 1) & (prefix[..., None] == jnp.arange(PICKS, dtype=jnp.int32))
    picked = jnp.sum(jnp.where(chosen, jnp.arange(BLOCKS, dtype=jnp.int32)[:, None], 0), axis=-2).astype(jnp.int32)
    pick_ids = jnp.arange(PICKS, dtype=jnp.int32)
    query_ids = jnp.arange(shard_blocks, dtype=jnp.int32)
    home_bits = pick_ids[None, :] % shard_blocks == query_ids[:, None]
    home_count = jnp.sum(home_bits, axis=1).astype(jnp.int32)
    target = jax.random.randint(jax.random.fold_in(key, 44), (N_HEAD, N_SEQ, heads_group, shard_blocks), 1, LIVE + 1)
    star_query = jax.random.randint(jax.random.fold_in(key, 45), (N_HEAD, N_SEQ, heads_group), 0, shard_blocks)
    target = jnp.where(query_ids == star_query[..., None], LIVE, target)
    target = jnp.maximum(target, home_count)
    draw_scores = jax.random.randint(jax.random.fold_in(key, 46), (N_HEAD, N_SEQ, heads_group, shard_blocks, PICKS), 0, 1 << 20)
    draw_scores = jnp.where(home_bits, 1 << 21, draw_scores)
    extra_rank = jnp.argsort(jnp.argsort(draw_scores, axis=-1, stable=True), axis=-1, stable=True).astype(jnp.int32)
    live_bits = (home_bits | (extra_rank < (target - home_count)[..., None])).astype(jnp.int32)
    mask_grid = jnp.zeros((N_HEAD, N_SEQ, heads_group, shard_blocks, BLOCKS), jnp.int32)
    mask_grid = mask_grid.at[jnp.arange(N_HEAD)[:, None, None, None, None], jnp.arange(N_SEQ)[None, :, None, None, None], jnp.arange(heads_group)[None, None, :, None, None], query_ids[None, None, None, :, None], picked[:, :, :, None, :]].max(live_bits)
    return mask_grid.transpose(0, 2, 1, 3, 4).reshape(HEADS, BLOCKS, BLOCKS)


def level_of(stream_key, shape, cuts, low, high):
    def one(dim, shards_of):
        draws = jax.random.uniform(jax.random.fold_in(jax.random.fold_in(stream_key, 6), dim), (shards_of,), jnp.float32, low / len(cuts), high / len(cuts))
        return jnp.repeat(jnp.exp(draws), shape[dim] // shards_of).reshape((-1,) + (1,) * (len(shape) - dim - 1))

    gain = one(*cuts[0])
    for cut in cuts[1:]:
        gain = gain * one(*cut)
    return gain


def scatter_about(stream_key, shape, deviation, bound, split=(), kind=jnp.bfloat16):
    gain = level_of(stream_key, shape, split, -0.22, 0.18) if split else 1.0
    array = jax.random.normal(stream_key, shape, jnp.float32) * deviation * gain
    return jnp.minimum(jnp.maximum(array, -bound), bound).astype(kind)


def setup_inputs(seed: int = 0) -> dict:
    seeds = jax.random.split(jax.random.key(seed), 6)
    return {
        "queries": draw_queries(jax.random.fold_in(seeds[5], 71), 0),
        "key_states": draw_key_states(jax.random.fold_in(seeds[5], 71), 0),
        "value_states": scatter_about(seeds[2], (TOKENS, HEADS * HEAD_DIM), 1.0, 6.0, ((0, 32),)),
        "cluster_perm": draw_cluster_perm(jax.random.fold_in(seeds[5], 71), 0),
        "block_mask": draw_block_mask(jax.random.fold_in(seeds[5], 71), 0),
    }


def reference(queries, key_states, value_states, cluster_perm, block_mask):

    def cluster_order(flat_rows):
        grid_view = flat_rows.reshape(TOKENS, HEADS, HEAD_DIM).transpose(1, 0, 2)
        return jnp.take_along_axis(grid_view, cluster_perm[:, :, None].astype(jnp.int32), axis=1)
    query_sorted = cluster_order(queries)
    key_sorted = cluster_order(key_states)
    value_sorted = cluster_order(value_states)
    score_scale = 1.0 / math.sqrt(HEAD_DIM)
    slot_ids = jnp.arange(LIVE, dtype=jnp.int32)
    block_ids = jnp.arange(BLOCKS, dtype=jnp.int32)

    def one_head(operands):
        query_head, key_head, value_head, mask_head = operands
        prefix = (jnp.cumsum(mask_head, axis=1) - mask_head).astype(jnp.int32)
        chosen = (mask_head[:, :, None] == 1) & (prefix[:, :, None] == slot_ids[None, None, :])
        which_block = lax.optimization_barrier(jnp.sum(jnp.where(chosen, block_ids[None, :, None], 0), axis=1)).astype(jnp.int32)
        usable = jnp.any(chosen, axis=1)
        key_sel = jnp.take(key_head.reshape(BLOCKS, BLOCK, HEAD_DIM), which_block, axis=0)
        value_sel = jnp.take(value_head.reshape(BLOCKS, BLOCK, HEAD_DIM), which_block, axis=0)
        query_blocks = query_head.reshape(BLOCKS, BLOCK, HEAD_DIM).astype(jnp.float32)
        scores = jnp.einsum('nid,nljd->nilj', query_blocks, key_sel.astype(jnp.float32), precision=lax.Precision.HIGHEST) * score_scale
        scores = jnp.where(usable[:, None, :, None], scores, -jnp.inf)
        row_top = lax.optimization_barrier(jnp.max(scores, axis=(2, 3), keepdims=True))
        exponent = jnp.exp(scores - row_top)
        row_total = lax.optimization_barrier(jnp.sum(exponent, axis=(2, 3), keepdims=True))
        weights = (exponent / row_total).astype(jnp.bfloat16)
        attended = jnp.einsum('nilj,nljd->nid', weights.astype(jnp.float32), value_sel.astype(jnp.float32), precision=lax.Precision.HIGHEST)
        return attended.astype(jnp.bfloat16).reshape(TOKENS, HEAD_DIM)
    attended = lax.map(one_head, (query_sorted, key_sorted, value_sorted, block_mask))
    restored = jnp.zeros((HEADS, TOKENS, HEAD_DIM), jnp.bfloat16)
    restored = restored.at[jnp.arange(HEADS, dtype=jnp.int32)[:, None], cluster_perm.astype(jnp.int32)].set(attended)
    return restored.transpose(1, 0, 2).reshape(TOKENS, HEADS * HEAD_DIM)
```

```python
import functools
import math

import jax
import jax.numpy as jnp
from jax import lax
from jax.experimental import pallas as pl
from jax.experimental.pallas import tpu as pltpu
from jax.sharding import PartitionSpec as P

HEAD_DIM = 128
BLOCK = 128
MESH = pl.DeviceIdType.MESH
HIGHEST = lax.Precision.HIGHEST


def iota(shape, dim):
    return lax.broadcasted_iota(jnp.int32, shape, dim)


def partner_of(me, step, count):
    if count & (count - 1):
        raise ValueError("seq size")
    peer = 0
    bit = 1
    while bit < count:
        peer = peer + bit * (((me // bit) + (step // bit)) % 2)
        bit *= 2
    return peer


def route(shard_blocks, capacity, picks, mask_ref, req_ref, pos_ref):
    heads, _, blocks = mask_ref.shape
    seq_count = blocks // shard_blocks
    needed = jnp.max(mask_ref[...], axis=1).astype(jnp.float32)
    row, col = iota((blocks, blocks), 0), iota((blocks, blocks), 1)
    same = (row // shard_blocks) == (col // shard_blocks)
    dot = functools.partial(jnp.dot, precision=HIGHEST, preferred_element_type=jnp.float32)
    ones = lambda flag: flag.astype(jnp.float32)
    by_owner = dot(needed, ones(same))
    before_in_owner = dot(needed, ones(same & (row < col)))
    before_all = dot(needed, ones(row < col))
    lower = ones(iota((heads, heads), 1) < iota((heads, heads), 0))
    rank = dot(lower, by_owner) + before_in_owner
    head_ids, block_ids = iota((heads, blocks), 0), iota((heads, blocks), 1)
    pair = (block_ids % shard_blocks * heads + head_ids).astype(jnp.float32)
    slot_row = iota((128, blocks), 0)
    sums = jnp.zeros((128, blocks), jnp.float32)
    for c in range(capacity):
        hit = jnp.where((rank == c) & (needed > 0.5), pair, 0.0)
        sums = jnp.where(slot_row == 2 * c, jnp.sum(hit, axis=0, keepdims=True), sums)
        hit = jnp.where((rank == c) & (needed > 0.5), head_ids.astype(jnp.float32), 0.0)
        sums = jnp.where(slot_row == 2 * c + 1, jnp.sum(hit, axis=0, keepdims=True), sums)
    owner_t = ones(iota((seq_count, blocks), 1) // shard_blocks == iota((seq_count, blocks), 0))
    asked = lax.dot_general(
        owner_t, sums, (((1,), (1,)), ((), ())), precision=HIGHEST,
        preferred_element_type=jnp.float32,
    )
    req_ref[...] = (asked + 0.5).astype(jnp.int32)[:, None, :]
    position = (block_ids // shard_blocks * capacity).astype(jnp.float32) + rank
    lane = iota((heads, 128), 1)
    table = jnp.zeros((heads, 128), jnp.float32)
    for p in range(picks):
        here = jnp.where((before_all == p) & (needed > 0.5), position, 0.0)
        table = jnp.where(lane == p, jnp.sum(here, axis=1, keepdims=True), table)
    pos_ref[...] = (table + 0.5).astype(jnp.int32)


def order(i, me, count):
    top, next_bit = (me // (count // 2)) % 2, (me // (count // 4)) % 2
    end = (top + next_bit + 1) % 2
    return end * (1 + (i + count // 4 - 1) % (count - 1)) + (1 - end) * (count - 1 - i)


def exchange_kernel(
    seq_count, capacity, shard_blocks, picks,
    key_ref, value_ref, query_ref, perm_ref, mask_ref, got_ref, pos_ref, pos_out, query_out,
    near_key, near_value, far_key, far_value, req_ref, asked_ref, asked, send_ref, rows_ref, blocks_ref,
    load_sem, swap_send, swap_recv, req_send, req_recv, misc_sem,
    sends, recvs, relay_send, relay_recv,
):
    group, me = lax.axis_index("head"), lax.axis_index("seq")
    other = 1 - group
    near_kv, far_kv = (near_key, near_value), (far_key, far_value)
    heads, rows = near_key.shape[:2]
    barrier = pltpu.get_barrier_semaphore()
    pl.semaphore_signal(barrier, inc=1, device_id={"head": other}, device_id_type=MESH)

    def greet(step, carry):
        pl.semaphore_signal(
            barrier, inc=1, device_id={"seq": partner_of(me, step, seq_count)}, device_id_type=MESH
        )
        return carry

    lax.fori_loop(1, seq_count, greet, 0)
    loads = []
    for number, src in enumerate((key_ref, value_ref)):
        for head in range(heads):
            start_at = pl.multiple_of((group * heads + head) * HEAD_DIM, HEAD_DIM)
            loads.append(
                pltpu.make_async_copy(
                    src.at[:, pl.ds(start_at, HEAD_DIM)], near_kv[number].at[head],
                    load_sem.at[number * heads + head],
                )
            )
    for copy in loads:
        copy.start()
    pl.semaphore_wait(barrier, seq_count)

    swaps = []
    for number, src in enumerate((key_ref, value_ref)):
        for head in range(heads):
            start_at = pl.multiple_of((other * heads + head) * HEAD_DIM, HEAD_DIM)
            at = number * heads + head
            swaps.append(
                pltpu.make_async_remote_copy(
                    src_ref=src.at[:, pl.ds(start_at, HEAD_DIM)], dst_ref=far_kv[number].at[head],
                    send_sem=swap_send.at[at], recv_sem=swap_recv.at[at],
                    device_id={"head": other}, device_id_type=MESH,
                )
            )
    for copy in swaps:
        copy.start()
    route(shard_blocks, capacity, picks, mask_ref, req_ref, pos_ref)
    for b in range(shard_blocks):
        blocks_ref[b * heads : (b + 1) * heads] = perm_ref[:, b * BLOCK : (b + 1) * BLOCK][:, None, :]
    rows_ref[...] = jnp.zeros_like(rows_ref)

    def ask(step, landing):
        peer = partner_of(me, step, seq_count)
        return pltpu.make_async_remote_copy(
            src_ref=req_ref.at[peer], dst_ref=asked_ref.at[peer if landing else me],
            send_sem=req_send.at[step], recv_sem=req_recv.at[step],
            device_id={"seq": peer}, device_id_type=MESH,
        )

    def start_ask(step, carry):
        ask(step, False).start()
        return carry

    lax.fori_loop(1, seq_count, start_ask, 0)
    tell = pltpu.make_async_remote_copy(
        src_ref=pos_ref, dst_ref=pos_out, send_sem=misc_sem.at[0], recv_sem=misc_sem.at[1],
        device_id={"head": other}, device_id_type=MESH,
    )
    tell.start()
    stay = pltpu.make_async_copy(query_ref, query_out, misc_sem.at[6])
    stay.start()
    keep = pltpu.make_async_copy(req_ref.at[me], asked_ref.at[me], misc_sem.at[2])
    keep.start()
    keep.wait()

    def finish_ask(step, carry):
        ask(step, True).wait()
        return carry

    lax.fori_loop(1, seq_count, finish_ask, 0)
    to_scalar = pltpu.make_async_copy(asked_ref, asked, misc_sem.at[3])
    to_scalar.start()
    to_scalar.wait()
    base = me * (2 * rows)
    token = iota((BLOCK, rows), 1)
    near = token + (base + group * rows)
    far = token + (base + other * rows)

    def gather(which, peer):
        chosen = []
        for c in range(capacity):
            pair = jnp.clip(asked[peer, 0, 2 * c], 0, heads * shard_blocks - 1)
            rows_ref[c : c + 1, :] = blocks_ref[pair]
            chosen.append(jnp.clip(asked[peer, 0, 2 * c + 1], 0, heads - 1))
        turned = rows_ref[...].T
        for c, head in enumerate(chosen):
            column = turned[:, c : c + 1]
            near_table = (column == near).astype(jnp.float32).astype(jnp.bfloat16)
            far_table = (column == far).astype(jnp.float32).astype(jnp.bfloat16)
            got = jnp.dot(near_table, near_kv[which][head], preferred_element_type=jnp.float32)
            got += jnp.dot(far_table, far_kv[which][head], preferred_element_type=jnp.float32)
            send_ref[which, peer, c] = got.astype(jnp.bfloat16)

    def deliver(which, step, landing):
        peer = partner_of(me, step, seq_count)
        return pltpu.make_async_remote_copy(
            src_ref=send_ref.at[which, peer],
            dst_ref=got_ref.at[0, which, peer if landing else me],
            send_sem=sends.at[which, step], recv_sem=recvs.at[which, step],
            device_id={"seq": peer}, device_id_type=MESH,
        )

    def relay(which, step):
        peer = partner_of(me, step, seq_count)
        return pltpu.make_async_remote_copy(
            src_ref=got_ref.at[0, which, peer], dst_ref=got_ref.at[1, which, peer],
            send_sem=relay_send.at[which, step], recv_sem=relay_recv.at[which, step],
            device_id={"head": other}, device_id_type=MESH,
        )

    for which in range(2):
        for copy in loads[which * heads : (which + 1) * heads]:
            copy.wait()
        for copy in swaps[which * heads : (which + 1) * heads]:
            copy.wait()
        gather(which, partner_of(me, order(0, me, seq_count), seq_count))

        def produce(i, carry, which=which):
            gather(which, partner_of(me, order(i, me, seq_count), seq_count))
            deliver(which, order(i - 1, me, seq_count), False).start()
            return carry

        lax.fori_loop(1, seq_count - 1, produce, 0)
        gather(which, me)
        deliver(which, order(seq_count - 2, me, seq_count), False).start()

    locals_ = []
    for which in range(2):
        mine = pltpu.make_async_copy(
            send_ref.at[which, me], got_ref.at[0, which, me], misc_sem.at[4 + which]
        )
        share = pltpu.make_async_remote_copy(
            src_ref=send_ref.at[which, me], dst_ref=got_ref.at[1, which, me],
            send_sem=relay_send.at[which, 0], recv_sem=relay_recv.at[which, 0],
            device_id={"head": other}, device_id_type=MESH,
        )
        mine.start()
        share.start()
        locals_.extend((mine, share))

    for which in range(2):

        def pass_on(i, carry, which=which):
            step = order(i, me, seq_count)
            deliver(which, step, True).wait_recv()
            relay(which, step).start()
            return carry

        lax.fori_loop(0, seq_count - 1, pass_on, 0)

    def finish(step, carry):
        for which in range(2):
            deliver(which, step, True).wait_send()
            relay(which, step).wait()
        return carry

    lax.fori_loop(1, seq_count, finish, 0)
    for copy in locals_:
        copy.wait()
    tell.wait()
    stay.wait()


def fused_kernel(
    seq_count, capacity, shard_blocks, picks,
    key_ref, value_ref, query_hbm, perm_ref, mask_ref, out_ref,
    keys, values, query_ref, send_ref, got_ref, stage_ref,
    req_ref, far_req_ref, asked_ref, pos_ref, far_pos_ref, rows_ref, blocks_ref,
    own_tab, far_tab, asked_near, asked, own_pos, far_pos,
    load_sem, swap_send, swap_recv, req_send, req_recv, misc_sem, tab_sem,
    near_sends, near_recvs, sends, recvs, relay_send, relay_recv, step_sem,
):
    group, me = lax.axis_index("head"), lax.axis_index("seq")
    other = 1 - group
    heads = perm_ref.shape[0]
    rows, columns = out_ref.shape
    half = heads * HEAD_DIM
    peer_of = lambda step: partner_of(me, step, seq_count)
    top, low = (me // 8) % 2, (me // 4) % 2
    edge = (top + low + 1) % 2

    def near_step(i):
        far = (3 - i) // 2
        return 8 * far + 4 * (edge * ((i + 1) % 2) + (1 - edge) * ((i + 1) // 2))

    def rest_step(i):
        q = i // 3
        first, second = (3 - q) // 2, ((q + 1) // 2) % 2
        plane = edge * (4 * first + 8 * second) + (1 - edge) * (8 * first + 4 * second)
        return plane + 1 + i % 3

    def times(count, body):
        lax.fori_loop(0, count, lambda i, carry: (body(i), carry)[1], 0)

    barrier = pltpu.get_barrier_semaphore()
    pl.semaphore_signal(barrier, inc=1, device_id={"head": other}, device_id_type=MESH)
    for step in (4, 8, 12, 1, 2):
        pl.semaphore_signal(barrier, inc=1, device_id={"seq": peer_of(step)}, device_id_type=MESH)

    loads, swaps = [], []
    parts = load_sem.shape[1]
    span = half // parts
    here = pl.ds(pl.multiple_of(group * rows, rows), rows)
    for number, (src, dst) in enumerate(((key_ref, keys), (value_ref, values))):
        for part in range(parts):
            at = pl.ds(part * span, span)
            mine = pl.ds(pl.multiple_of(group * half + part * span, HEAD_DIM), span)
            theirs = pl.ds(pl.multiple_of(other * half + part * span, HEAD_DIM), span)
            loads.append(
                pltpu.make_async_copy(
                    src.at[:, mine], dst.at[here, at], load_sem.at[number, part]
                )
            )
            swaps.append(
                pltpu.make_async_remote_copy(
                    src_ref=src.at[:, theirs], dst_ref=dst.at[here, at],
                    send_sem=swap_send.at[number, part], recv_sem=swap_recv.at[number, part],
                    device_id={"head": other}, device_id_type=MESH,
                )
            )
    for copy in loads:
        copy.start()
    take = pltpu.make_async_copy(query_hbm, query_ref, misc_sem.at[0])
    take.start()
    route(shard_blocks, capacity, picks, mask_ref, req_ref, pos_ref)
    for b in range(shard_blocks):
        blocks_ref[b * heads : (b + 1) * heads] = perm_ref[:, b * BLOCK : (b + 1) * BLOCK][:, None, :]
    rows_ref[...] = jnp.zeros_like(rows_ref)
    pl.semaphore_wait(barrier, 6)

    def ask(step, landing):
        peer = peer_of(step)
        return pltpu.make_async_remote_copy(
            src_ref=req_ref.at[peer], dst_ref=asked_ref.at[peer if landing else me],
            send_sem=req_send.at[step], recv_sem=req_recv.at[step],
            device_id={"seq": peer}, device_id_type=MESH,
        )

    times(3, lambda i: ask(near_step(i), False).start())
    for copy in swaps:
        copy.start()
    for number, step in enumerate((1, 2)):
        pl.semaphore_signal(
            step_sem.at[number], inc=1, device_id={"seq": peer_of(step)}, device_id_type=MESH
        )
    tells = []
    for number, (src, dst) in enumerate(((req_ref, far_req_ref), (pos_ref, far_pos_ref))):
        tells.append(
            pltpu.make_async_remote_copy(
                src_ref=src, dst_ref=dst,
                send_sem=misc_sem.at[1 + number], recv_sem=misc_sem.at[3 + number],
                device_id={"head": other}, device_id_type=MESH,
            )
        )
    for copy in tells:
        copy.start()
    keep = pltpu.make_async_copy(req_ref.at[me], asked_ref.at[me], misc_sem.at[5])
    keep.start()
    own_tabs = [
        pltpu.make_async_copy(req_ref, own_tab, tab_sem.at[0]),
        pltpu.make_async_copy(pos_ref, own_pos, tab_sem.at[1]),
    ]
    for copy in own_tabs:
        copy.start()
    pl.semaphore_wait(step_sem.at[0], 1)
    pl.semaphore_wait(step_sem.at[1], 1)
    pl.semaphore_signal(step_sem.at[2], inc=1, device_id={"seq": peer_of(2)}, device_id_type=MESH)
    pl.semaphore_wait(step_sem.at[2], 1)
    times(12, lambda i: ask(rest_step(i), False).start())

    def near_scalar(i):
        peer = peer_of(4 * i + 4)
        return pltpu.make_async_copy(asked_ref.at[peer], asked_near.at[peer], tab_sem.at[5 + i])

    for i in range(3):
        ask(4 * i + 4, True).wait_recv()
        near_scalar(i).start()
    for i in range(3):
        near_scalar(i).wait()

    token = iota((BLOCK, 2 * rows), 1) + me * (2 * rows)
    sides = (keys, values)

    def gather(table_ref, peer, whiches, put):
        chosen = []
        for c in range(capacity):
            pair = jnp.clip(table_ref[peer, 0, 2 * c], 0, heads * shard_blocks - 1)
            rows_ref[c : c + 1, :] = blocks_ref[pair]
            head = jnp.clip(table_ref[peer, 0, 2 * c + 1], 0, heads - 1)
            chosen.append(head * HEAD_DIM)
        turned = rows_ref[...].T
        for c, start_at in enumerate(chosen):
            table = (turned[:, c : c + 1] == token).astype(jnp.float32).astype(jnp.bfloat16)
            for which in whiches:
                got = jnp.dot(
                    table, sides[which][:, pl.ds(start_at, HEAD_DIM)],
                    preferred_element_type=jnp.float32,
                )
                put(which, c, got.astype(jnp.bfloat16))

    def to_send(peer):
        def put(which, c, got):
            send_ref[peer, which, c] = got

        return put

    def near_deliver(which, step, landing):
        peer = peer_of(step)
        return pltpu.make_async_remote_copy(
            src_ref=send_ref.at[peer, which], dst_ref=got_ref.at[0, peer if landing else me, which],
            send_sem=near_sends.at[which, step], recv_sem=near_recvs.at[which, step],
            device_id={"seq": peer}, device_id_type=MESH,
        )

    def deliver(step, landing):
        peer = peer_of(step)
        return pltpu.make_async_remote_copy(
            src_ref=send_ref.at[peer], dst_ref=got_ref.at[0, peer if landing else me],
            send_sem=sends.at[step], recv_sem=recvs.at[step],
            device_id={"seq": peer}, device_id_type=MESH,
        )

    def relay(step, landing):
        peer = peer_of(step)
        return pltpu.make_async_remote_copy(
            src_ref=got_ref.at[0, peer], dst_ref=got_ref.at[1, peer],
            send_sem=relay_send.at[step], recv_sem=relay_recv.at[step],
            device_id={"head": other}, device_id_type=MESH,
        )

    for which in range(2):
        for copy in loads[which * parts : (which + 1) * parts]:
            copy.wait()
        for copy in swaps[which * parts : (which + 1) * parts]:
            copy.wait()

        def serve(i, which=which):
            step = near_step(i)
            peer = peer_of(step)
            gather(asked_near, peer, (which,), to_send(peer))
            near_deliver(which, step, False).start()

        times(3, serve)
    for copy in own_tabs:
        copy.wait()

    keep.wait()
    times(12, lambda i: ask(rest_step(i), True).wait_recv())
    to_scalar = pltpu.make_async_copy(asked_ref, asked, tab_sem.at[4])
    to_scalar.start()
    to_scalar.wait()

    def produce(i):
        step = rest_step(i)
        peer = peer_of(step)
        gather(asked, peer, (0, 1), to_send(peer))
        deliver(step, False).start()

    times(12, produce)

    def to_got(which, c, got):
        got_ref[0, me, which, c] = got

    gather(own_tab, me, (0, 1), to_got)
    relay(0, False).start()
    for copy in tells:
        copy.wait()
    far_tabs = [
        pltpu.make_async_copy(far_req_ref, far_tab, tab_sem.at[2]),
        pltpu.make_async_copy(far_pos_ref, far_pos, tab_sem.at[3]),
    ]
    for copy in far_tabs:
        copy.start()
    for copy in far_tabs:
        copy.wait()
    take.wait()

    scale = math.log2(math.e) / math.sqrt(HEAD_DIM)
    ones = jnp.ones((BLOCK, HEAD_DIM), jnp.bfloat16)

    def attend(items):
        scores = []
        for rel, peer, c in items:
            tab, base = ((own_tab, group), (far_tab, other))[rel]
            head = base * heads + jnp.clip(tab[peer, 0, 2 * c + 1], 0, heads - 1)
            query = query_ref[:, pl.ds(head * HEAD_DIM, HEAD_DIM)]
            scores.append(
                lax.dot_general(
                    query, got_ref[rel, peer, 0, c], (((1,), (1,)), ((), ())),
                    preferred_element_type=jnp.float32,
                )
            )
        weights = []
        for score in scores:
            peak = jnp.max(score, axis=1, keepdims=True)
            weights.append(jnp.exp2((score - peak) * scale).astype(jnp.bfloat16))
        for (rel, peer, c), weight in zip(items, weights):
            mixed = jnp.dot(
                weight, jnp.concatenate([got_ref[rel, peer, 1, c], ones], axis=1),
                preferred_element_type=jnp.float32,
            )
            stage_ref[rel, peer * capacity + c] = (mixed[:, :HEAD_DIM] / mixed[:, HEAD_DIM:]).astype(jnp.bfloat16)

    slots = lambda rel, peer: [(rel, peer, c) for c in range(capacity)]
    attend(slots(0, me))
    relay(0, True).wait_recv()
    attend(slots(1, me))

    def near_take(i):
        step = near_step(i)
        for which in range(2):
            near_deliver(which, step, True).wait_recv()
        relay(step, False).start()

    times(3, near_take)

    def near_use(i):
        step = near_step(i)
        peer = peer_of(step)
        relay(step, True).wait_recv()
        attend(slots(0, peer) + slots(1, peer))

    times(3, near_use)

    def use(step, before):
        deliver(step, True).wait_recv()
        relay(step, False).start()
        if before is None:
            attend(slots(0, peer_of(step)))
        else:
            relay(before, True).wait_recv()
            attend(slots(0, peer_of(step)) + slots(1, peer_of(before)))

    close = lambda j: 1 + j + j // 3
    away = lambda k: 9 + k // 2 + 4 * (k % 2)
    use(close(0), None)
    times(5, lambda j: use(close(j + 1), close(j)))
    use(away(0), close(5))
    times(5, lambda k: use(away(k + 1), away(k)))
    relay(away(5), True).wait_recv()
    attend(slots(1, peer_of(away(5))))

    for rel, (tab, base) in enumerate(((own_pos, group), (far_pos, other))):

        def place(local, rel=rel, tab=tab, base=base):
            slot = jnp.clip(tab[local, 0], 0, seq_count * capacity - 1)
            at = pl.multiple_of((base * heads + local) * HEAD_DIM, HEAD_DIM)
            out_ref[:, pl.ds(at, HEAD_DIM)] = stage_ref[rel, slot]

        times(heads, place)

    def finish_near(i):
        step = near_step(i)
        ask(step, True).wait_send()
        for which in range(2):
            near_deliver(which, step, True).wait_send()
        relay(step, True).wait_send()

    times(3, finish_near)

    def finish(i):
        step = rest_step(i)
        ask(step, True).wait_send()
        deliver(step, True).wait_send()
        relay(step, True).wait_send()

    times(12, finish)
    relay(0, True).wait_send()


def fused(key_states, value_states, queries, cluster_perm, block_mask, capacity, picks):
    heads, shard_rows = cluster_perm.shape
    shard_blocks = shard_rows // BLOCK
    seq_count = lax.axis_size("seq")
    rows, columns = queries.shape
    vmem = pl.BlockSpec(memory_space=pltpu.VMEM)
    anywhere = pl.BlockSpec(memory_space=pltpu.HBM)
    bf16, i32 = jnp.bfloat16, jnp.int32
    dma = pltpu.SemaphoreType.DMA
    table = (seq_count, 1, 128)
    parts = 4
    return pl.pallas_call(
        functools.partial(fused_kernel, seq_count, capacity, shard_blocks, picks),
        out_shape=pltpu.VMEM((rows, columns), bf16),
        in_specs=[anywhere, anywhere, anywhere, vmem, vmem],
        out_specs=vmem,
        scratch_shapes=[
            pltpu.VMEM((shard_rows, heads * HEAD_DIM), bf16),
            pltpu.VMEM((shard_rows, heads * HEAD_DIM), bf16),
            pltpu.VMEM((rows, columns), bf16),
            pltpu.VMEM((seq_count, 2, capacity, BLOCK, HEAD_DIM), bf16),
            pltpu.VMEM((2, seq_count, 2, capacity, BLOCK, HEAD_DIM), bf16),
            pltpu.VMEM((2, seq_count * capacity, rows, HEAD_DIM), bf16),
            pltpu.VMEM(table, i32), pltpu.VMEM(table, i32), pltpu.VMEM(table, i32),
            pltpu.VMEM((heads, 128), i32), pltpu.VMEM((heads, 128), i32),
            pltpu.VMEM((8 * -(-capacity // 8), 128), i32),
            pltpu.VMEM((shard_blocks * heads, 1, BLOCK), i32),
            pltpu.SMEM(table, i32), pltpu.SMEM(table, i32), pltpu.SMEM(table, i32),
            pltpu.SMEM(table, i32),
            pltpu.SMEM((heads, 128), i32), pltpu.SMEM((heads, 128), i32),
            dma((2, parts)), dma((2, parts)), dma((2, parts)),
            dma((seq_count,)), dma((seq_count,)), dma((6,)), dma((8,)),
            dma((2, seq_count)), dma((2, seq_count)),
            dma((seq_count,)), dma((seq_count,)), dma((seq_count,)), dma((seq_count,)),
            pltpu.SemaphoreType.REGULAR((3,)),
        ],
        compiler_params=pltpu.CompilerParams(
            collective_id=1, has_side_effects=True, vmem_limit_bytes=40 * 1024 * 1024
        ),
        name="fused",
    )(key_states, value_states, queries, cluster_perm, block_mask)


def attend_kernel(heads, picks, width, capacity, masked, pos_own, pos_far, *refs):
    if masked:
        query_ref, kv_ref, allow_ref, out_ref, stage, sems = refs
    else:
        query_ref, kv_ref, out_ref, stage, sems = refs
    group = lax.axis_index("head")
    scale = math.log2(math.e) / math.sqrt(HEAD_DIM)
    ones = jnp.ones((BLOCK, HEAD_DIM), jnp.bfloat16)
    span = width * HEAD_DIM
    batches = query_ref.shape[1] // span

    def put(batch, buffer):
        return pltpu.make_async_copy(
            stage.at[buffer],
            out_ref.at[:, pl.ds(pl.multiple_of(batch * span, span), span)],
            sems.at[buffer],
        )

    def one(batch, carry):
        where_, scores = [], []
        for w in range(width):
            head = batch * width + w
            away = (head // heads) != group
            local = head % heads
            query = query_ref[:, pl.ds(pl.multiple_of(head * HEAD_DIM, HEAD_DIM), HEAD_DIM)]
            for p in range(picks):
                slot = jnp.where(away, pos_far[local, p], pos_own[local, p])
                spot = (slot // capacity, slot % capacity)
                rel = away.astype(jnp.int32)
                where_.append((rel, spot))
                score = lax.dot_general(
                    query, kv_ref[rel, 0, spot[0], spot[1]], (((1,), (1,)), ((), ())),
                    preferred_element_type=jnp.float32,
                )
                if masked:
                    score = jnp.where(allow_ref[head, :, p : p + 1] > 0, score, -jnp.inf)
                scores.append(score)
        weights = []
        for w in range(width):
            own = scores[w * picks : (w + 1) * picks]
            top = jnp.max(functools.reduce(jnp.maximum, own), axis=1, keepdims=True)
            weights.extend([jnp.exp2((s - top) * scale).astype(jnp.bfloat16) for s in own])
        buffer = batch % 2

        @pl.when(batch >= 2)
        def _():
            put(batch - 2, buffer).wait()

        for w in range(width):
            parts = []
            for p in range(picks):
                rel, spot = where_[w * picks + p]
                parts.append(
                    jnp.dot(
                        weights[w * picks + p],
                        jnp.concatenate([kv_ref[rel, 1, spot[0], spot[1]], ones], axis=1),
                        preferred_element_type=jnp.float32,
                    )
                )
            mixed = functools.reduce(jnp.add, parts)
            stage[buffer, :, w * HEAD_DIM : (w + 1) * HEAD_DIM] = (
                mixed[:, :HEAD_DIM] / mixed[:, HEAD_DIM:]
            ).astype(jnp.bfloat16)
        put(batch, buffer).start()
        return carry

    lax.fori_loop(0, batches, one, 0)
    for batch in range(max(0, batches - 2), batches):
        put(batch, batch % 2).wait()


def token_allow(cluster_perm, block_mask, picks, me, shard_rows):
    needed = jnp.max(block_mask, axis=1)
    prefix = jnp.cumsum(needed, axis=1) - needed
    chosen = (needed[:, :, None] == 1) & (prefix[:, :, None] == jnp.arange(picks)[None, None, :])
    live = jnp.einsum(
        "hqb,hbp->hqp", block_mask.astype(jnp.float32), chosen.astype(jnp.float32)
    )
    group_heads = cluster_perm.shape[0]
    local = cluster_perm - me * shard_rows
    place = jnp.zeros((group_heads, shard_rows), jnp.int32)
    place = place.at[jnp.arange(group_heads)[:, None], local].set(
        jnp.broadcast_to(jnp.arange(shard_rows, dtype=jnp.int32) // BLOCK, local.shape)
    )
    by_token = jnp.take_along_axis(live, place[:, :, None], axis=1).astype(jnp.float32)
    return lax.all_to_all(by_token, "head", split_axis=1, concat_axis=0, tiled=True)


def shards(queries, key_states, value_states, cluster_perm, block_mask):
    group_heads, shard_rows = cluster_perm.shape
    shard_blocks = shard_rows // BLOCK
    seq_count = lax.axis_size("seq")
    block_total = block_mask.shape[2]
    picks = max(1, block_total // 64)
    capacity = max(
        1, min(shard_blocks, (group_heads * picks * 8 + 5 * seq_count - 1) // (5 * seq_count))
    )
    rows, columns = queries.shape
    me = lax.axis_index("seq")
    if picks == 1 and seq_count == 16:
        return fused(
            key_states, value_states, queries, cluster_perm, block_mask, capacity, picks
        )
    vmem = pl.BlockSpec(memory_space=pltpu.VMEM)
    anywhere = pl.BlockSpec(memory_space=pltpu.HBM)
    struct = jax.ShapeDtypeStruct
    bf16, i32 = jnp.bfloat16, jnp.int32

    dma = pltpu.SemaphoreType.DMA
    kv_half = pltpu.VMEM((group_heads, rows, HEAD_DIM), bf16)
    table = struct((group_heads, 128), i32)
    resident = 2 * (4 * seq_count * capacity * BLOCK * HEAD_DIM + rows * columns)
    grant = 67043328 - resident - 256 * 1024
    got, positions, pos_far, near_queries = pl.pallas_call(
        functools.partial(exchange_kernel, seq_count, capacity, shard_blocks, picks),
        out_shape=(
            pltpu.VMEM((2, 2, seq_count, capacity, BLOCK, HEAD_DIM), bf16), table, table,
            pltpu.VMEM((rows, columns), bf16),
        ),
        in_specs=[anywhere, anywhere, anywhere, vmem, vmem],
        out_specs=(vmem, vmem, vmem, vmem),
        scratch_shapes=[
            kv_half, kv_half, kv_half, kv_half,
            pltpu.VMEM((seq_count, 1, 128), i32),
            pltpu.VMEM((seq_count, 1, 128), i32),
            pltpu.SMEM((seq_count, 1, 128), i32),
            pltpu.VMEM((2, seq_count, capacity, BLOCK, HEAD_DIM), bf16),
            pltpu.VMEM((8 * -(-capacity // 8), 128), i32),
            pltpu.VMEM((shard_blocks * group_heads, 1, BLOCK), i32),
            dma((2 * group_heads,)), dma((2 * group_heads,)), dma((2 * group_heads,)),
            dma((seq_count,)), dma((seq_count,)), dma((7,)),
        ] + [dma((2, seq_count)) for _ in range(4)],
        compiler_params=pltpu.CompilerParams(
            collective_id=0, has_side_effects=True, vmem_limit_bytes=grant
        ),
        name="exchange",
    )(key_states, value_states, queries, cluster_perm, block_mask)

    masked = picks > 1
    total_heads = columns // HEAD_DIM
    width = 8 if total_heads % 8 == 0 else 1
    operands = [near_queries, got]
    if masked:
        operands.append(token_allow(cluster_perm, block_mask, picks, me, shard_rows))
    smem = pl.BlockSpec(memory_space=pltpu.SMEM)
    return pl.pallas_call(
        functools.partial(attend_kernel, group_heads, picks, width, capacity, masked),
        out_shape=struct((rows, columns), bf16),
        in_specs=[smem, smem] + [vmem] * len(operands),
        out_specs=anywhere,
        scratch_shapes=[pltpu.VMEM((2, rows, width * HEAD_DIM), bf16), dma((2,))],
        compiler_params=pltpu.CompilerParams(vmem_limit_bytes=24 * 1024 * 1024),
        name="attend",
    )(positions, pos_far, *operands)


def solution(mesh):
    rows = P(("seq", "head"), None)
    placed = (rows, rows, rows, P("head", "seq"), P("head", "seq", None))
    return jax.shard_map(shards, mesh=mesh, in_specs=placed, out_specs=rows, check_vma=False)
```

```python
import functools
import math

import jax
import jax.numpy as jnp
from jax import lax
from jax.experimental import pallas as pl
from jax.experimental.pallas import tpu as pltpu
from jax.sharding import PartitionSpec as P

HEAD_DIM = 128
BLOCK = 128
MESH = pl.DeviceIdType.MESH
HIGHEST = lax.Precision.HIGHEST


def iota(shape, dim):
    return lax.broadcasted_iota(jnp.int32, shape, dim)


def partner_of(me, step, count):
    if count & (count - 1):
        raise ValueError("seq size")
    peer = 0
    bit = 1
    while bit < count:
        peer = peer + bit * (((me // bit) + (step // bit)) % 2)
        bit *= 2
    return peer


def route(shard_blocks, capacity, picks, mask_ref, req_ref, pos_ref):
    heads, _, blocks = mask_ref.shape
    seq_count = blocks // shard_blocks
    needed = jnp.max(mask_ref[...], axis=1).astype(jnp.float32)
    row, col = iota((blocks, blocks), 0), iota((blocks, blocks), 1)
    same = (row // shard_blocks) == (col // shard_blocks)
    dot = functools.partial(jnp.dot, precision=HIGHEST, preferred_element_type=jnp.float32)
    ones = lambda flag: flag.astype(jnp.float32)
    by_owner = dot(needed, ones(same))
    before_in_owner = dot(needed, ones(same & (row < col)))
    before_all = dot(needed, ones(row < col))
    lower = ones(iota((heads, heads), 1) < iota((heads, heads), 0))
    rank = dot(lower, by_owner) + before_in_owner
    head_ids, block_ids = iota((heads, blocks), 0), iota((heads, blocks), 1)
    pair = (block_ids % shard_blocks * heads + head_ids).astype(jnp.float32)
    slot_row = iota((128, blocks), 0)
    sums = jnp.zeros((128, blocks), jnp.float32)
    for c in range(capacity):
        hit = jnp.where((rank == c) & (needed > 0.5), pair, 0.0)
        sums = jnp.where(slot_row == 2 * c, jnp.sum(hit, axis=0, keepdims=True), sums)
        hit = jnp.where((rank == c) & (needed > 0.5), head_ids.astype(jnp.float32), 0.0)
        sums = jnp.where(slot_row == 2 * c + 1, jnp.sum(hit, axis=0, keepdims=True), sums)
    owner_t = ones(iota((seq_count, blocks), 1) // shard_blocks == iota((seq_count, blocks), 0))
    asked = lax.dot_general(
        owner_t, sums, (((1,), (1,)), ((), ())), precision=HIGHEST,
        preferred_element_type=jnp.float32,
    )
    req_ref[...] = (asked + 0.5).astype(jnp.int32)[:, None, :]
    position = (block_ids // shard_blocks * capacity).astype(jnp.float32) + rank
    lane = iota((heads, 128), 1)
    table = jnp.zeros((heads, 128), jnp.float32)
    for p in range(picks):
        here = jnp.where((before_all == p) & (needed > 0.5), position, 0.0)
        table = jnp.where(lane == p, jnp.sum(here, axis=1, keepdims=True), table)
    pos_ref[...] = (table + 0.5).astype(jnp.int32)


def order(i, me, count):
    top, next_bit = (me // (count // 2)) % 2, (me // (count // 4)) % 2
    end = (top + next_bit + 1) % 2
    return end * (1 + (i + count // 4 - 1) % (count - 1)) + (1 - end) * (count - 1 - i)


def exchange_kernel(
    seq_count, capacity, shard_blocks, picks,
    key_ref, value_ref, query_ref, perm_ref, mask_ref, got_ref, pos_ref, pos_out, query_out,
    near_key, near_value, far_key, far_value, req_ref, asked_ref, asked, send_ref, rows_ref, blocks_ref,
    load_sem, swap_send, swap_recv, req_send, req_recv, misc_sem,
    sends, recvs, relay_send, relay_recv,
):
    group, me = lax.axis_index("head"), lax.axis_index("seq")
    other = 1 - group
    near_kv, far_kv = (near_key, near_value), (far_key, far_value)
    heads, rows = near_key.shape[:2]
    barrier = pltpu.get_barrier_semaphore()
    pl.semaphore_signal(barrier, inc=1, device_id={"head": other}, device_id_type=MESH)

    def greet(step, carry):
        pl.semaphore_signal(
            barrier, inc=1, device_id={"seq": partner_of(me, step, seq_count)}, device_id_type=MESH
        )
        return carry

    lax.fori_loop(1, seq_count, greet, 0)
    loads = []
    for number, src in enumerate((key_ref, value_ref)):
        for head in range(heads):
            start_at = pl.multiple_of((group * heads + head) * HEAD_DIM, HEAD_DIM)
            loads.append(
                pltpu.make_async_copy(
                    src.at[:, pl.ds(start_at, HEAD_DIM)], near_kv[number].at[head],
                    load_sem.at[number * heads + head],
                )
            )
    for copy in loads:
        copy.start()
    pl.semaphore_wait(barrier, seq_count)

    swaps = []
    for number, src in enumerate((key_ref, value_ref)):
        for head in range(heads):
            start_at = pl.multiple_of((other * heads + head) * HEAD_DIM, HEAD_DIM)
            at = number * heads + head
            swaps.append(
                pltpu.make_async_remote_copy(
                    src_ref=src.at[:, pl.ds(start_at, HEAD_DIM)], dst_ref=far_kv[number].at[head],
                    send_sem=swap_send.at[at], recv_sem=swap_recv.at[at],
                    device_id={"head": other}, device_id_type=MESH,
                )
            )
    for copy in swaps:
        copy.start()
    route(shard_blocks, capacity, picks, mask_ref, req_ref, pos_ref)
    for b in range(shard_blocks):
        blocks_ref[b * heads : (b + 1) * heads] = perm_ref[:, b * BLOCK : (b + 1) * BLOCK][:, None, :]
    rows_ref[...] = jnp.zeros_like(rows_ref)

    def ask(step, landing):
        peer = partner_of(me, step, seq_count)
        return pltpu.make_async_remote_copy(
            src_ref=req_ref.at[peer], dst_ref=asked_ref.at[peer if landing else me],
            send_sem=req_send.at[step], recv_sem=req_recv.at[step],
            device_id={"seq": peer}, device_id_type=MESH,
        )

    def start_ask(step, carry):
        ask(step, False).start()
        return carry

    lax.fori_loop(1, seq_count, start_ask, 0)
    tell = pltpu.make_async_remote_copy(
        src_ref=pos_ref, dst_ref=pos_out, send_sem=misc_sem.at[0], recv_sem=misc_sem.at[1],
        device_id={"head": other}, device_id_type=MESH,
    )
    tell.start()
    stay = pltpu.make_async_copy(query_ref, query_out, misc_sem.at[6])
    stay.start()
    keep = pltpu.make_async_copy(req_ref.at[me], asked_ref.at[me], misc_sem.at[2])
    keep.start()
    keep.wait()

    def finish_ask(step, carry):
        ask(step, True).wait()
        return carry

    lax.fori_loop(1, seq_count, finish_ask, 0)
    to_scalar = pltpu.make_async_copy(asked_ref, asked, misc_sem.at[3])
    to_scalar.start()
    to_scalar.wait()
    base = me * (2 * rows)
    token = iota((BLOCK, rows), 1)
    near = token + (base + group * rows)
    far = token + (base + other * rows)

    def gather(which, peer):
        chosen = []
        for c in range(capacity):
            pair = jnp.clip(asked[peer, 0, 2 * c], 0, heads * shard_blocks - 1)
            rows_ref[c : c + 1, :] = blocks_ref[pair]
            chosen.append(jnp.clip(asked[peer, 0, 2 * c + 1], 0, heads - 1))
        turned = rows_ref[...].T
        for c, head in enumerate(chosen):
            column = turned[:, c : c + 1]
            near_table = (column == near).astype(jnp.float32).astype(jnp.bfloat16)
            far_table = (column == far).astype(jnp.float32).astype(jnp.bfloat16)
            got = jnp.dot(near_table, near_kv[which][head], preferred_element_type=jnp.float32)
            got += jnp.dot(far_table, far_kv[which][head], preferred_element_type=jnp.float32)
            send_ref[which, peer, c] = got.astype(jnp.bfloat16)

    def deliver(which, step, landing):
        peer = partner_of(me, step, seq_count)
        return pltpu.make_async_remote_copy(
            src_ref=send_ref.at[which, peer],
            dst_ref=got_ref.at[0, which, peer if landing else me],
            send_sem=sends.at[which, step], recv_sem=recvs.at[which, step],
            device_id={"seq": peer}, device_id_type=MESH,
        )

    def relay(which, step):
        peer = partner_of(me, step, seq_count)
        return pltpu.make_async_remote_copy(
            src_ref=got_ref.at[0, which, peer], dst_ref=got_ref.at[1, which, peer],
            send_sem=relay_send.at[which, step], recv_sem=relay_recv.at[which, step],
            device_id={"head": other}, device_id_type=MESH,
        )

    for which in range(2):
        for copy in loads[which * heads : (which + 1) * heads]:
            copy.wait()
        for copy in swaps[which * heads : (which + 1) * heads]:
            copy.wait()
        gather(which, partner_of(me, order(0, me, seq_count), seq_count))

        def produce(i, carry, which=which):
            gather(which, partner_of(me, order(i, me, seq_count), seq_count))
            deliver(which, order(i - 1, me, seq_count), False).start()
            return carry

        lax.fori_loop(1, seq_count - 1, produce, 0)
        gather(which, me)
        deliver(which, order(seq_count - 2, me, seq_count), False).start()

    locals_ = []
    for which in range(2):
        mine = pltpu.make_async_copy(
            send_ref.at[which, me], got_ref.at[0, which, me], misc_sem.at[4 + which]
        )
        share = pltpu.make_async_remote_copy(
            src_ref=send_ref.at[which, me], dst_ref=got_ref.at[1, which, me],
            send_sem=relay_send.at[which, 0], recv_sem=relay_recv.at[which, 0],
            device_id={"head": other}, device_id_type=MESH,
        )
        mine.start()
        share.start()
        locals_.extend((mine, share))

    for which in range(2):

        def pass_on(i, carry, which=which):
            step = order(i, me, seq_count)
            deliver(which, step, True).wait_recv()
            relay(which, step).start()
            return carry

        lax.fori_loop(0, seq_count - 1, pass_on, 0)

    def finish(step, carry):
        for which in range(2):
            deliver(which, step, True).wait_send()
            relay(which, step).wait()
        return carry

    lax.fori_loop(1, seq_count, finish, 0)
    for copy in locals_:
        copy.wait()
    tell.wait()
    stay.wait()


def fused_kernel(
    seq_count, capacity, shard_blocks, picks,
    key_ref, value_ref, query_hbm, perm_hbm, mask_hbm, out_ref,
    perm_ref, mask_ref, keys, values, query_ref, send_ref, got_ref, stage_ref,
    req_ref, far_req_ref, asked_ref, pos_ref, far_pos_ref, rows_ref, blocks_ref,
    own_tab, far_tab, asked_near, asked, own_pos, far_pos,
    load_sem, swap_send, swap_recv, req_send, req_recv, misc_sem, tab_sem,
    near_sends, near_recvs, sends, recvs, relay_send, relay_recv, step_sem,
):
    group, me = lax.axis_index("head"), lax.axis_index("seq")
    other = 1 - group
    heads = perm_ref.shape[0]
    rows, columns = out_ref.shape
    half = heads * HEAD_DIM
    peer_of = lambda step: partner_of(me, step, seq_count)
    top, low = (me // 8) % 2, (me // 4) % 2
    edge = (top + low + 1) % 2

    def near_step(i):
        far = (3 - i) // 2
        return 8 * far + 4 * (edge * ((i + 1) % 2) + (1 - edge) * ((i + 1) // 2))

    def far_step(k):
        return 9 + k // 2 + 4 * (edge * ((k + 1) % 2) + (1 - edge) * (k % 2))

    def all_rest(body):
        times(3, lambda k: body(1 + k))
        times(3, lambda k: body(5 + k))
        times(6, lambda k: body(far_step(k)))

    def times(count, body):
        lax.fori_loop(0, count, lambda i, carry: (body(i), carry)[1], 0)

    barrier = pltpu.get_barrier_semaphore()
    pl.semaphore_signal(barrier, inc=1, device_id={"head": other}, device_id_type=MESH)
    for step in (4, 8, 12, 1, 2):
        pl.semaphore_signal(barrier, inc=1, device_id={"seq": peer_of(step)}, device_id_type=MESH)

    masks = pltpu.make_async_copy(mask_hbm, mask_ref, misc_sem.at[6])
    masks.start()
    perms = pltpu.make_async_copy(perm_hbm, perm_ref, misc_sem.at[7])
    perms.start()
    loads, swaps = [], []
    parts = load_sem.shape[1]
    span = half // parts
    here = pl.ds(pl.multiple_of(group * rows, rows), rows)
    for number, (src, dst) in enumerate(((key_ref, keys), (value_ref, values))):
        for part in range(parts):
            at = pl.ds(part * span, span)
            mine = pl.ds(pl.multiple_of(group * half + part * span, HEAD_DIM), span)
            theirs = pl.ds(pl.multiple_of(other * half + part * span, HEAD_DIM), span)
            loads.append(
                pltpu.make_async_copy(
                    src.at[:, mine], dst.at[here, at], load_sem.at[number, part]
                )
            )
            swaps.append(
                pltpu.make_async_remote_copy(
                    src_ref=src.at[:, theirs], dst_ref=dst.at[here, at],
                    send_sem=swap_send.at[number, part], recv_sem=swap_recv.at[number, part],
                    device_id={"head": other}, device_id_type=MESH,
                )
            )
    for copy in loads:
        copy.start()
    take = pltpu.make_async_copy(query_hbm, query_ref, misc_sem.at[0])
    take.start()
    masks.wait()
    route(shard_blocks, capacity, picks, mask_ref, req_ref, pos_ref)
    perms.wait()
    for b in range(shard_blocks):
        blocks_ref[b * heads : (b + 1) * heads] = perm_ref[:, b * BLOCK : (b + 1) * BLOCK][:, None, :]
    rows_ref[...] = jnp.zeros_like(rows_ref)
    pl.semaphore_wait(barrier, 6)

    def ask(step, landing):
        peer = peer_of(step)
        return pltpu.make_async_remote_copy(
            src_ref=req_ref.at[peer], dst_ref=asked_ref.at[peer if landing else me],
            send_sem=req_send.at[step], recv_sem=req_recv.at[step],
            device_id={"seq": peer}, device_id_type=MESH,
        )

    times(3, lambda i: ask(near_step(i), False).start())
    for copy in swaps:
        copy.start()
    for number, step in enumerate((1, 2)):
        pl.semaphore_signal(
            step_sem.at[number], inc=1, device_id={"seq": peer_of(step)}, device_id_type=MESH
        )
    tells = []
    for number, (src, dst) in enumerate(((req_ref, far_req_ref), (pos_ref, far_pos_ref))):
        tells.append(
            pltpu.make_async_remote_copy(
                src_ref=src, dst_ref=dst,
                send_sem=misc_sem.at[1 + number], recv_sem=misc_sem.at[3 + number],
                device_id={"head": other}, device_id_type=MESH,
            )
        )
    for copy in tells:
        copy.start()
    keep = pltpu.make_async_copy(req_ref.at[me], asked_ref.at[me], misc_sem.at[5])
    keep.start()
    own_tabs = [
        pltpu.make_async_copy(req_ref, own_tab, tab_sem.at[0]),
        pltpu.make_async_copy(pos_ref, own_pos, tab_sem.at[1]),
    ]
    for copy in own_tabs:
        copy.start()
    pl.semaphore_wait(step_sem.at[0], 1)
    pl.semaphore_wait(step_sem.at[1], 1)
    pl.semaphore_signal(step_sem.at[2], inc=1, device_id={"seq": peer_of(2)}, device_id_type=MESH)
    pl.semaphore_wait(step_sem.at[2], 1)
    all_rest(lambda step: ask(step, False).start())

    def near_scalar(i):
        peer = peer_of(4 * i + 4)
        return pltpu.make_async_copy(asked_ref.at[peer], asked_near.at[peer], tab_sem.at[5 + i])

    for i in range(3):
        ask(4 * i + 4, True).wait_recv()
        near_scalar(i).start()
    for i in range(3):
        near_scalar(i).wait()

    token = iota((BLOCK, 2 * rows), 1) + me * (2 * rows)
    sides = (keys, values)

    def gather(table_ref, peer, whiches, put):
        chosen = []
        for c in range(capacity):
            pair = jnp.clip(table_ref[peer, 0, 2 * c], 0, heads * shard_blocks - 1)
            rows_ref[c : c + 1, :] = blocks_ref[pair]
            head = jnp.clip(table_ref[peer, 0, 2 * c + 1], 0, heads - 1)
            chosen.append(head * HEAD_DIM)
        turned = rows_ref[...].T
        for c, start_at in enumerate(chosen):
            table = (turned[:, c : c + 1] == token).astype(jnp.float32).astype(jnp.bfloat16)
            for which in whiches:
                got = jnp.dot(
                    table, sides[which][:, pl.ds(start_at, HEAD_DIM)],
                    preferred_element_type=jnp.float32,
                )
                put(which, c, got.astype(jnp.bfloat16))

    def to_send(peer):
        def put(which, c, got):
            send_ref[peer, which, c] = got

        return put

    def near_deliver(which, step, landing):
        peer = peer_of(step)
        return pltpu.make_async_remote_copy(
            src_ref=send_ref.at[peer, which], dst_ref=got_ref.at[0, peer if landing else me, which],
            send_sem=near_sends.at[which, step], recv_sem=near_recvs.at[which, step],
            device_id={"seq": peer}, device_id_type=MESH,
        )

    def deliver(step, landing):
        peer = peer_of(step)
        return pltpu.make_async_remote_copy(
            src_ref=send_ref.at[peer], dst_ref=got_ref.at[0, peer if landing else me],
            send_sem=sends.at[step], recv_sem=recvs.at[step],
            device_id={"seq": peer}, device_id_type=MESH,
        )

    def relay(step, landing):
        peer = peer_of(step)
        return pltpu.make_async_remote_copy(
            src_ref=got_ref.at[0, peer], dst_ref=got_ref.at[1, peer],
            send_sem=relay_send.at[step], recv_sem=relay_recv.at[step],
            device_id={"head": other}, device_id_type=MESH,
        )

    for which in range(2):
        for copy in loads[which * parts : (which + 1) * parts]:
            copy.wait()
        for copy in swaps[which * parts : (which + 1) * parts]:
            copy.wait()

        def serve(i, which=which):
            step = near_step(i)
            peer = peer_of(step)
            gather(asked_near, peer, (which,), to_send(peer))
            near_deliver(which, step, False).start()

        times(3, serve)
    for copy in own_tabs:
        copy.wait()

    keep.wait()
    all_rest(lambda step: ask(step, True).wait_recv())
    to_scalar = pltpu.make_async_copy(asked_ref, asked, tab_sem.at[4])
    to_scalar.start()
    to_scalar.wait()

    def produce(step):
        peer = peer_of(step)
        gather(asked, peer, (0, 1), to_send(peer))
        deliver(step, False).start()

    def produce_at(i):
        far = edge * ((i + 6) // 9) + (1 - edge) * ((14 - i) // 9)
        at = i - 3 * edge + 9 * (1 - far)
        produce(far * far_step(at % 9) + (1 - far) * (5 + (at + 9 * edge) % 3))

    times(9, produce_at)
    times(3, lambda k: produce(1 + k))

    def to_got(which, c, got):
        got_ref[0, me, which, c] = got

    gather(own_tab, me, (0, 1), to_got)
    relay(0, False).start()
    for copy in tells:
        copy.wait()
    far_tabs = [
        pltpu.make_async_copy(far_req_ref, far_tab, tab_sem.at[2]),
        pltpu.make_async_copy(far_pos_ref, far_pos, tab_sem.at[3]),
    ]
    for copy in far_tabs:
        copy.start()
    for copy in far_tabs:
        copy.wait()
    take.wait()

    scale = math.log2(math.e) / math.sqrt(HEAD_DIM)
    ones = jnp.ones((BLOCK, HEAD_DIM), jnp.bfloat16)

    def attend(items):
        scores = []
        for rel, peer, c in items:
            tab, base = ((own_tab, group), (far_tab, other))[rel]
            head = base * heads + jnp.clip(tab[peer, 0, 2 * c + 1], 0, heads - 1)
            query = query_ref[:, pl.ds(head * HEAD_DIM, HEAD_DIM)]
            scores.append(
                lax.dot_general(
                    query, got_ref[rel, peer, 0, c], (((1,), (1,)), ((), ())),
                    preferred_element_type=jnp.float32,
                )
            )
        weights = []
        for score in scores:
            peak = jnp.max(score, axis=1, keepdims=True)
            weights.append(jnp.exp2((score - peak) * scale).astype(jnp.bfloat16))
        for (rel, peer, c), weight in zip(items, weights):
            mixed = jnp.dot(
                weight, jnp.concatenate([got_ref[rel, peer, 1, c], ones], axis=1),
                preferred_element_type=jnp.float32,
            )
            stage_ref[rel, peer * capacity + c] = (mixed[:, :HEAD_DIM] / mixed[:, HEAD_DIM:]).astype(jnp.bfloat16)

    slots = lambda rel, peer: [(rel, peer, c) for c in range(capacity)]
    attend(slots(0, me))
    relay(0, True).wait_recv()
    attend(slots(1, me))

    def near_take(i):
        step = near_step(i)
        for which in range(2):
            near_deliver(which, step, True).wait_recv()
        relay(step, False).start()

    times(3, near_take)

    def near_use(i):
        step = near_step(i)
        peer = peer_of(step)
        relay(step, True).wait_recv()
        attend(slots(0, peer) + slots(1, peer))

    times(3, near_use)

    def use(step, before):
        deliver(step, True).wait_recv()
        relay(step, False).start()
        if before is None:
            attend(slots(0, peer_of(step)))
        else:
            relay(before, True).wait_recv()
            attend(slots(0, peer_of(step)) + slots(1, peer_of(before)))

    close = lambda j: 1 + j + j // 3
    away = lambda k: 9 + k // 2 + 4 * (k % 2)
    use(close(0), None)
    times(5, lambda j: use(close(j + 1), close(j)))
    use(away(0), close(5))
    times(5, lambda k: use(away(k + 1), away(k)))
    relay(away(5), True).wait_recv()
    attend(slots(1, peer_of(away(5))))

    for rel, (tab, base) in enumerate(((own_pos, group), (far_pos, other))):

        def place(local, rel=rel, tab=tab, base=base):
            slot = jnp.clip(tab[local, 0], 0, seq_count * capacity - 1)
            at = pl.multiple_of((base * heads + local) * HEAD_DIM, HEAD_DIM)
            out_ref[:, pl.ds(at, HEAD_DIM)] = stage_ref[rel, slot]

        times(heads, place)

    def finish_near(i):
        step = near_step(i)
        ask(step, True).wait_send()
        for which in range(2):
            near_deliver(which, step, True).wait_send()
        relay(step, True).wait_send()

    times(3, finish_near)

    def finish(step):
        ask(step, True).wait_send()
        deliver(step, True).wait_send()
        relay(step, True).wait_send()

    all_rest(finish)
    relay(0, True).wait_send()


def fused(key_states, value_states, queries, cluster_perm, block_mask, capacity, picks):
    heads, shard_rows = cluster_perm.shape
    shard_blocks = shard_rows // BLOCK
    seq_count = lax.axis_size("seq")
    rows, columns = queries.shape
    vmem = pl.BlockSpec(memory_space=pltpu.VMEM)
    anywhere = pl.BlockSpec(memory_space=pltpu.HBM)
    bf16, i32 = jnp.bfloat16, jnp.int32
    dma = pltpu.SemaphoreType.DMA
    table = (seq_count, 1, 128)
    parts = 4
    return pl.pallas_call(
        functools.partial(fused_kernel, seq_count, capacity, shard_blocks, picks),
        out_shape=pltpu.VMEM((rows, columns), bf16),
        in_specs=[anywhere] * 5,
        out_specs=vmem,
        scratch_shapes=[
            pltpu.VMEM(cluster_perm.shape, i32), pltpu.VMEM(block_mask.shape, i32),
            pltpu.VMEM((shard_rows, heads * HEAD_DIM), bf16),
            pltpu.VMEM((shard_rows, heads * HEAD_DIM), bf16),
            pltpu.VMEM((rows, columns), bf16),
            pltpu.VMEM((seq_count, 2, capacity, BLOCK, HEAD_DIM), bf16),
            pltpu.VMEM((2, seq_count, 2, capacity, BLOCK, HEAD_DIM), bf16),
            pltpu.VMEM((2, seq_count * capacity, rows, HEAD_DIM), bf16),
            pltpu.VMEM(table, i32), pltpu.VMEM(table, i32), pltpu.VMEM(table, i32),
            pltpu.VMEM((heads, 128), i32), pltpu.VMEM((heads, 128), i32),
            pltpu.VMEM((8 * -(-capacity // 8), 128), i32),
            pltpu.VMEM((shard_blocks * heads, 1, BLOCK), i32),
            pltpu.SMEM(table, i32), pltpu.SMEM(table, i32), pltpu.SMEM(table, i32),
            pltpu.SMEM(table, i32),
            pltpu.SMEM((heads, 128), i32), pltpu.SMEM((heads, 128), i32),
            dma((2, parts)), dma((2, parts)), dma((2, parts)),
            dma((seq_count,)), dma((seq_count,)), dma((8,)), dma((8,)),
            dma((2, seq_count)), dma((2, seq_count)),
            dma((seq_count,)), dma((seq_count,)), dma((seq_count,)), dma((seq_count,)),
            pltpu.SemaphoreType.REGULAR((3,)),
        ],
        compiler_params=pltpu.CompilerParams(
            collective_id=1, has_side_effects=True, vmem_limit_bytes=67043328 - 2 * rows * columns - 256 * 1024
        ),
        name="fused",
    )(key_states, value_states, queries, cluster_perm, block_mask)


def attend_kernel(heads, picks, width, capacity, masked, pos_own, pos_far, *refs):
    if masked:
        query_ref, kv_ref, allow_ref, out_ref, stage, sems = refs
    else:
        query_ref, kv_ref, out_ref, stage, sems = refs
    group = lax.axis_index("head")
    scale = math.log2(math.e) / math.sqrt(HEAD_DIM)
    ones = jnp.ones((BLOCK, HEAD_DIM), jnp.bfloat16)
    span = width * HEAD_DIM
    batches = query_ref.shape[1] // span

    def put(batch, buffer):
        return pltpu.make_async_copy(
            stage.at[buffer],
            out_ref.at[:, pl.ds(pl.multiple_of(batch * span, span), span)],
            sems.at[buffer],
        )

    def one(batch, carry):
        where_, scores = [], []
        for w in range(width):
            head = batch * width + w
            away = (head // heads) != group
            local = head % heads
            query = query_ref[:, pl.ds(pl.multiple_of(head * HEAD_DIM, HEAD_DIM), HEAD_DIM)]
            for p in range(picks):
                slot = jnp.where(away, pos_far[local, p], pos_own[local, p])
                spot = (slot // capacity, slot % capacity)
                rel = away.astype(jnp.int32)
                where_.append((rel, spot))
                score = lax.dot_general(
                    query, kv_ref[rel, 0, spot[0], spot[1]], (((1,), (1,)), ((), ())),
                    preferred_element_type=jnp.float32,
                )
                if masked:
                    score = jnp.where(allow_ref[head, :, p : p + 1] > 0, score, -jnp.inf)
                scores.append(score)
        weights = []
        for w in range(width):
            own = scores[w * picks : (w + 1) * picks]
            top = jnp.max(functools.reduce(jnp.maximum, own), axis=1, keepdims=True)
            weights.extend([jnp.exp2((s - top) * scale).astype(jnp.bfloat16) for s in own])
        buffer = batch % 2

        @pl.when(batch >= 2)
        def _():
            put(batch - 2, buffer).wait()

        for w in range(width):
            parts = []
            for p in range(picks):
                rel, spot = where_[w * picks + p]
                parts.append(
                    jnp.dot(
                        weights[w * picks + p],
                        jnp.concatenate([kv_ref[rel, 1, spot[0], spot[1]], ones], axis=1),
                        preferred_element_type=jnp.float32,
                    )
                )
            mixed = functools.reduce(jnp.add, parts)
            stage[buffer, :, w * HEAD_DIM : (w + 1) * HEAD_DIM] = (
                mixed[:, :HEAD_DIM] / mixed[:, HEAD_DIM:]
            ).astype(jnp.bfloat16)
        put(batch, buffer).start()
        return carry

    lax.fori_loop(0, batches, one, 0)
    for batch in range(max(0, batches - 2), batches):
        put(batch, batch % 2).wait()


def token_allow(cluster_perm, block_mask, picks, me, shard_rows):
    needed = jnp.max(block_mask, axis=1)
    prefix = jnp.cumsum(needed, axis=1) - needed
    chosen = (needed[:, :, None] == 1) & (prefix[:, :, None] == jnp.arange(picks)[None, None, :])
    live = jnp.einsum(
        "hqb,hbp->hqp", block_mask.astype(jnp.float32), chosen.astype(jnp.float32)
    )
    group_heads = cluster_perm.shape[0]
    local = cluster_perm - me * shard_rows
    place = jnp.zeros((group_heads, shard_rows), jnp.int32)
    place = place.at[jnp.arange(group_heads)[:, None], local].set(
        jnp.broadcast_to(jnp.arange(shard_rows, dtype=jnp.int32) // BLOCK, local.shape)
    )
    by_token = jnp.take_along_axis(live, place[:, :, None], axis=1).astype(jnp.float32)
    return lax.all_to_all(by_token, "head", split_axis=1, concat_axis=0, tiled=True)


def shards(queries, key_states, value_states, cluster_perm, block_mask):
    group_heads, shard_rows = cluster_perm.shape
    shard_blocks = shard_rows // BLOCK
    seq_count = lax.axis_size("seq")
    block_total = block_mask.shape[2]
    picks = max(1, block_total // 64)
    capacity = max(
        1, min(shard_blocks, (group_heads * picks * 8 + 5 * seq_count - 1) // (5 * seq_count))
    )
    rows, columns = queries.shape
    me = lax.axis_index("seq")
    if picks == 1 and seq_count == 16:
        return fused(
            key_states, value_states, queries, cluster_perm, block_mask, capacity, picks
        )
    vmem = pl.BlockSpec(memory_space=pltpu.VMEM)
    anywhere = pl.BlockSpec(memory_space=pltpu.HBM)
    struct = jax.ShapeDtypeStruct
    bf16, i32 = jnp.bfloat16, jnp.int32

    dma = pltpu.SemaphoreType.DMA
    kv_half = pltpu.VMEM((group_heads, rows, HEAD_DIM), bf16)
    table = struct((group_heads, 128), i32)
    resident = 2 * (4 * seq_count * capacity * BLOCK * HEAD_DIM + rows * columns)
    grant = 67043328 - resident - 256 * 1024
    got, positions, pos_far, near_queries = pl.pallas_call(
        functools.partial(exchange_kernel, seq_count, capacity, shard_blocks, picks),
        out_shape=(
            pltpu.VMEM((2, 2, seq_count, capacity, BLOCK, HEAD_DIM), bf16), table, table,
            pltpu.VMEM((rows, columns), bf16),
        ),
        in_specs=[anywhere, anywhere, anywhere, vmem, vmem],
        out_specs=(vmem, vmem, vmem, vmem),
        scratch_shapes=[
            kv_half, kv_half, kv_half, kv_half,
            pltpu.VMEM((seq_count, 1, 128), i32),
            pltpu.VMEM((seq_count, 1, 128), i32),
            pltpu.SMEM((seq_count, 1, 128), i32),
            pltpu.VMEM((2, seq_count, capacity, BLOCK, HEAD_DIM), bf16),
            pltpu.VMEM((8 * -(-capacity // 8), 128), i32),
            pltpu.VMEM((shard_blocks * group_heads, 1, BLOCK), i32),
            dma((2 * group_heads,)), dma((2 * group_heads,)), dma((2 * group_heads,)),
            dma((seq_count,)), dma((seq_count,)), dma((7,)),
        ] + [dma((2, seq_count)) for _ in range(4)],
        compiler_params=pltpu.CompilerParams(
            collective_id=0, has_side_effects=True, vmem_limit_bytes=grant
        ),
        name="exchange",
    )(key_states, value_states, queries, cluster_perm, block_mask)

    masked = picks > 1
    total_heads = columns // HEAD_DIM
    width = 8 if total_heads % 8 == 0 else 1
    operands = [near_queries, got]
    if masked:
        operands.append(token_allow(cluster_perm, block_mask, picks, me, shard_rows))
    smem = pl.BlockSpec(memory_space=pltpu.SMEM)
    return pl.pallas_call(
        functools.partial(attend_kernel, group_heads, picks, width, capacity, masked),
        out_shape=struct((rows, columns), bf16),
        in_specs=[smem, smem] + [vmem] * len(operands),
        out_specs=anywhere,
        scratch_shapes=[pltpu.VMEM((2, rows, width * HEAD_DIM), bf16), dma((2,))],
        compiler_params=pltpu.CompilerParams(vmem_limit_bytes=24 * 1024 * 1024),
        name="attend",
    )(positions, pos_far, *operands)


def solution(mesh):
    rows = P(("seq", "head"), None)
    placed = (rows, rows, rows, P("head", "seq"), P("head", "seq", None))
    return jax.shard_map(shards, mesh=mesh, in_specs=placed, out_specs=rows, check_vma=False)
```

```python
import functools
import math

import jax
import jax.numpy as jnp
from jax import lax
from jax.experimental import pallas as pl
from jax.experimental.pallas import tpu as pltpu
from jax.sharding import PartitionSpec as P

HEAD_DIM = 128
BLOCK = 128
MESH = pl.DeviceIdType.MESH
HIGHEST = lax.Precision.HIGHEST


def iota(shape, dim):
    return lax.broadcasted_iota(jnp.int32, shape, dim)


def partner_of(me, step, count):
    if count & (count - 1):
        raise ValueError("seq size")
    peer = 0
    bit = 1
    while bit < count:
        peer = peer + bit * (((me // bit) + (step // bit)) % 2)
        bit *= 2
    return peer


def route(shard_blocks, capacity, picks, mask_ref, req_ref, pos_ref):
    heads, _, blocks = mask_ref.shape
    seq_count = blocks // shard_blocks
    needed = jnp.max(mask_ref[...], axis=1).astype(jnp.float32)
    row, col = iota((blocks, blocks), 0), iota((blocks, blocks), 1)
    same = (row // shard_blocks) == (col // shard_blocks)
    dot = functools.partial(jnp.dot, precision=HIGHEST, preferred_element_type=jnp.float32)
    ones = lambda flag: flag.astype(jnp.float32)
    by_owner = dot(needed, ones(same))
    before_in_owner = dot(needed, ones(same & (row < col)))
    before_all = dot(needed, ones(row < col))
    lower = ones(iota((heads, heads), 1) < iota((heads, heads), 0))
    rank = dot(lower, by_owner) + before_in_owner
    head_ids, block_ids = iota((heads, blocks), 0), iota((heads, blocks), 1)
    pair = (block_ids % shard_blocks * heads + head_ids).astype(jnp.float32)
    slot_row = iota((128, blocks), 0)
    sums = jnp.zeros((128, blocks), jnp.float32)
    for c in range(capacity):
        hit = jnp.where((rank == c) & (needed > 0.5), pair, 0.0)
        sums = jnp.where(slot_row == 2 * c, jnp.sum(hit, axis=0, keepdims=True), sums)
        hit = jnp.where((rank == c) & (needed > 0.5), head_ids.astype(jnp.float32), 0.0)
        sums = jnp.where(slot_row == 2 * c + 1, jnp.sum(hit, axis=0, keepdims=True), sums)
    owner_t = ones(iota((seq_count, blocks), 1) // shard_blocks == iota((seq_count, blocks), 0))
    asked = lax.dot_general(
        owner_t, sums, (((1,), (1,)), ((), ())), precision=HIGHEST,
        preferred_element_type=jnp.float32,
    )
    req_ref[...] = (asked + 0.5).astype(jnp.int32)[:, None, :]
    position = (block_ids // shard_blocks * capacity).astype(jnp.float32) + rank
    lane = iota((heads, 128), 1)
    table = jnp.zeros((heads, 128), jnp.float32)
    for p in range(picks):
        here = jnp.where((before_all == p) & (needed > 0.5), position, 0.0)
        table = jnp.where(lane == p, jnp.sum(here, axis=1, keepdims=True), table)
    pos_ref[...] = (table + 0.5).astype(jnp.int32)


def order(i, me, count):
    top, next_bit = (me // (count // 2)) % 2, (me // (count // 4)) % 2
    end = (top + next_bit + 1) % 2
    return end * (1 + (i + count // 4 - 1) % (count - 1)) + (1 - end) * (count - 1 - i)


def exchange_kernel(
    seq_count, capacity, shard_blocks, picks,
    key_ref, value_ref, query_ref, perm_ref, mask_ref, got_ref, pos_ref, pos_out, query_out,
    near_key, near_value, far_key, far_value, req_ref, asked_ref, asked, send_ref, rows_ref, blocks_ref,
    load_sem, swap_send, swap_recv, req_send, req_recv, misc_sem,
    sends, recvs, relay_send, relay_recv,
):
    group, me = lax.axis_index("head"), lax.axis_index("seq")
    other = 1 - group
    near_kv, far_kv = (near_key, near_value), (far_key, far_value)
    heads, rows = near_key.shape[:2]
    barrier = pltpu.get_barrier_semaphore()
    pl.semaphore_signal(barrier, inc=1, device_id={"head": other}, device_id_type=MESH)

    def greet(step, carry):
        pl.semaphore_signal(
            barrier, inc=1, device_id={"seq": partner_of(me, step, seq_count)}, device_id_type=MESH
        )
        return carry

    lax.fori_loop(1, seq_count, greet, 0)
    loads = []
    for number, src in enumerate((key_ref, value_ref)):
        for head in range(heads):
            start_at = pl.multiple_of((group * heads + head) * HEAD_DIM, HEAD_DIM)
            loads.append(
                pltpu.make_async_copy(
                    src.at[:, pl.ds(start_at, HEAD_DIM)], near_kv[number].at[head],
                    load_sem.at[number * heads + head],
                )
            )
    for copy in loads:
        copy.start()
    pl.semaphore_wait(barrier, seq_count)

    swaps = []
    for number, src in enumerate((key_ref, value_ref)):
        for head in range(heads):
            start_at = pl.multiple_of((other * heads + head) * HEAD_DIM, HEAD_DIM)
            at = number * heads + head
            swaps.append(
                pltpu.make_async_remote_copy(
                    src_ref=src.at[:, pl.ds(start_at, HEAD_DIM)], dst_ref=far_kv[number].at[head],
                    send_sem=swap_send.at[at], recv_sem=swap_recv.at[at],
                    device_id={"head": other}, device_id_type=MESH,
                )
            )
    for copy in swaps:
        copy.start()
    route(shard_blocks, capacity, picks, mask_ref, req_ref, pos_ref)
    for b in range(shard_blocks):
        blocks_ref[b * heads : (b + 1) * heads] = perm_ref[:, b * BLOCK : (b + 1) * BLOCK][:, None, :]
    rows_ref[...] = jnp.zeros_like(rows_ref)

    def ask(step, landing):
        peer = partner_of(me, step, seq_count)
        return pltpu.make_async_remote_copy(
            src_ref=req_ref.at[peer], dst_ref=asked_ref.at[peer if landing else me],
            send_sem=req_send.at[step], recv_sem=req_recv.at[step],
            device_id={"seq": peer}, device_id_type=MESH,
        )

    def start_ask(step, carry):
        ask(step, False).start()
        return carry

    lax.fori_loop(1, seq_count, start_ask, 0)
    tell = pltpu.make_async_remote_copy(
        src_ref=pos_ref, dst_ref=pos_out, send_sem=misc_sem.at[0], recv_sem=misc_sem.at[1],
        device_id={"head": other}, device_id_type=MESH,
    )
    tell.start()
    stay = pltpu.make_async_copy(query_ref, query_out, misc_sem.at[6])
    stay.start()
    keep = pltpu.make_async_copy(req_ref.at[me], asked_ref.at[me], misc_sem.at[2])
    keep.start()
    keep.wait()

    def finish_ask(step, carry):
        ask(step, True).wait()
        return carry

    lax.fori_loop(1, seq_count, finish_ask, 0)
    to_scalar = pltpu.make_async_copy(asked_ref, asked, misc_sem.at[3])
    to_scalar.start()
    to_scalar.wait()
    base = me * (2 * rows)
    token = iota((BLOCK, rows), 1)
    near = token + (base + group * rows)
    far = token + (base + other * rows)

    def gather(which, peer):
        chosen = []
        for c in range(capacity):
            pair = jnp.clip(asked[peer, 0, 2 * c], 0, heads * shard_blocks - 1)
            rows_ref[c : c + 1, :] = blocks_ref[pair]
            chosen.append(jnp.clip(asked[peer, 0, 2 * c + 1], 0, heads - 1))
        turned = rows_ref[...].T
        for c, head in enumerate(chosen):
            column = turned[:, c : c + 1]
            near_table = (column == near).astype(jnp.float32).astype(jnp.bfloat16)
            far_table = (column == far).astype(jnp.float32).astype(jnp.bfloat16)
            got = jnp.dot(near_table, near_kv[which][head], preferred_element_type=jnp.float32)
            got += jnp.dot(far_table, far_kv[which][head], preferred_element_type=jnp.float32)
            send_ref[which, peer, c] = got.astype(jnp.bfloat16)

    def deliver(which, step, landing):
        peer = partner_of(me, step, seq_count)
        return pltpu.make_async_remote_copy(
            src_ref=send_ref.at[which, peer],
            dst_ref=got_ref.at[0, which, peer if landing else me],
            send_sem=sends.at[which, step], recv_sem=recvs.at[which, step],
            device_id={"seq": peer}, device_id_type=MESH,
        )

    def relay(which, step):
        peer = partner_of(me, step, seq_count)
        return pltpu.make_async_remote_copy(
            src_ref=got_ref.at[0, which, peer], dst_ref=got_ref.at[1, which, peer],
            send_sem=relay_send.at[which, step], recv_sem=relay_recv.at[which, step],
            device_id={"head": other}, device_id_type=MESH,
        )

    for which in range(2):
        for copy in loads[which * heads : (which + 1) * heads]:
            copy.wait()
        for copy in swaps[which * heads : (which + 1) * heads]:
            copy.wait()
        gather(which, partner_of(me, order(0, me, seq_count), seq_count))

        def produce(i, carry, which=which):
            gather(which, partner_of(me, order(i, me, seq_count), seq_count))
            deliver(which, order(i - 1, me, seq_count), False).start()
            return carry

        lax.fori_loop(1, seq_count - 1, produce, 0)
        gather(which, me)
        deliver(which, order(seq_count - 2, me, seq_count), False).start()

    locals_ = []
    for which in range(2):
        mine = pltpu.make_async_copy(
            send_ref.at[which, me], got_ref.at[0, which, me], misc_sem.at[4 + which]
        )
        share = pltpu.make_async_remote_copy(
            src_ref=send_ref.at[which, me], dst_ref=got_ref.at[1, which, me],
            send_sem=relay_send.at[which, 0], recv_sem=relay_recv.at[which, 0],
            device_id={"head": other}, device_id_type=MESH,
        )
        mine.start()
        share.start()
        locals_.extend((mine, share))

    for which in range(2):

        def pass_on(i, carry, which=which):
            step = order(i, me, seq_count)
            deliver(which, step, True).wait_recv()
            relay(which, step).start()
            return carry

        lax.fori_loop(0, seq_count - 1, pass_on, 0)

    def finish(step, carry):
        for which in range(2):
            deliver(which, step, True).wait_send()
            relay(which, step).wait()
        return carry

    lax.fori_loop(1, seq_count, finish, 0)
    for copy in locals_:
        copy.wait()
    tell.wait()
    stay.wait()


def request(shard_blocks, capacity, mask_ref, tab_ref):
    heads, _, blocks = mask_ref.shape
    seq_count = blocks // shard_blocks
    needed = jnp.max(mask_ref[...], axis=1).astype(jnp.float32)
    row, col = iota((blocks, blocks), 0), iota((blocks, blocks), 1)
    same = (row // shard_blocks) == (col // shard_blocks)
    small = lambda value: value.astype(jnp.float32).astype(jnp.bfloat16)
    dot = functools.partial(jnp.dot, preferred_element_type=jnp.float32)
    by_owner = dot(small(needed), small(same))
    lower = small(iota((heads, heads), 1) < iota((heads, heads), 0))
    rank = dot(lower, small(by_owner)) + dot(small(needed), small(same & (row < col)))
    head_ids, block_ids = iota((heads, blocks), 0), iota((heads, blocks), 1)
    pair = (block_ids % shard_blocks * heads + head_ids).astype(jnp.float32)
    slot_row = iota((128, blocks), 0)
    sums = jnp.zeros((128, blocks), jnp.float32)
    for c in range(capacity):
        taken = (rank == c) & (needed > 0.5)
        for lane, value in ((2 * c, pair), (2 * c + 1, head_ids.astype(jnp.float32))):
            hit = jnp.sum(jnp.where(taken, value, 0.0), axis=0, keepdims=True)
            sums = jnp.where(slot_row == lane, hit, sums)
    owner_t = small(iota((seq_count, blocks), 1) // shard_blocks == iota((seq_count, blocks), 0))
    asked = lax.dot_general(
        owner_t, small(sums), (((1,), (1,)), ((), ())), preferred_element_type=jnp.float32
    )
    tab_ref[:seq_count] = (asked + 0.5).astype(jnp.int32)[:, None, :]
    spot = (block_ids // shard_blocks * capacity).astype(jnp.float32) + rank
    spot = jnp.sum(jnp.where(needed > 0.5, spot, 0.0), axis=1, keepdims=True)
    spot = (jnp.broadcast_to(spot, (heads, 128)) + 0.5).astype(jnp.int32)
    tab_ref[seq_count:] = spot[:, None, :]


def fused_kernel(
    seq_count, capacity, shard_blocks,
    key_ref, value_ref, query_hbm, perm_hbm, mask_hbm, stage_ref, tab_ref, far_tab_ref,
    perm_ref, mask_ref, keys, values, query_ref, send_ref, got_ref, asked_ref, rows_ref, blocks_ref,
    own_tab, far_tab, asked_near, asked,
    near_sem, load_sem, swap_send, swap_recv, ask_send, ask_recv, misc_sem,
    send_sem, recvs, relay_send, relay_recv, step_sem,
):
    group, me = lax.axis_index("head"), lax.axis_index("seq")
    other = 1 - group
    heads = perm_ref.shape[0]
    rows = query_hbm.shape[0]
    half = heads * HEAD_DIM
    spread = seq_count // 4
    peer_of = lambda step: partner_of(me, step, seq_count)
    top, low = (me // (2 * spread)) % 2, (me // spread) % 2
    edge = (top + low + 1) % 2

    def near_peer(i):
        far = (3 - i) // 2
        turn = edge * ((i + 1) // 2) + (1 - edge) * ((i + 1) % 2)
        return peer_of(spread * (2 * far + turn))

    def side_peer(plane, k):
        return peer_of(spread * plane + 1 + k)

    def far_peer(k):
        plane = 2 + edge * ((k + 1) % 2) + (1 - edge) * (k % 2)
        return side_peer(plane, k // 2)

    def times(count, body):
        lax.fori_loop(0, count, lambda i, carry: (body(i), carry)[1], 0)

    beside = spread - 1

    def all_rest(body):
        times(beside, lambda k: body(side_peer(0, k)))
        times(beside, lambda k: body(side_peer(1, k)))
        times(2 * beside, lambda k: body(far_peer(k)))

    barrier = pltpu.get_barrier_semaphore()
    pl.semaphore_signal(barrier, inc=1, device_id={"head": other}, device_id_type=MESH)
    for step in (spread, 2 * spread, 3 * spread, 1, 2):
        pl.semaphore_signal(barrier, inc=1, device_id={"seq": peer_of(step)}, device_id_type=MESH)

    masks = pltpu.make_async_copy(mask_hbm, mask_ref, misc_sem.at[0])
    masks.start()
    perms = pltpu.make_async_copy(perm_hbm, perm_ref, misc_sem.at[1])
    perms.start()
    here = pl.ds(pl.multiple_of(group * rows, rows), rows)
    sides = ((key_ref, keys), (value_ref, values))

    def load(number, start_at, span):
        src, dst = sides[number]
        mine = pl.ds(pl.multiple_of(group * half + start_at, HEAD_DIM), span)
        return pltpu.make_async_copy(
            src.at[:, mine], dst.at[here, pl.ds(start_at, span)], load_sem.at[number]
        )

    def swap(number, start_at, span):
        src, dst = sides[number]
        theirs = pl.ds(pl.multiple_of(other * half + start_at, HEAD_DIM), span)
        return pltpu.make_async_remote_copy(
            src_ref=src.at[:, theirs], dst_ref=dst.at[here, pl.ds(start_at, span)],
            send_sem=swap_send.at[number], recv_sem=swap_recv.at[number],
            device_id={"head": other}, device_id_type=MESH,
        )

    parts = 4
    cuts = [(number, part * (half // parts), half // parts) for number in range(2) for part in range(parts)]
    for cut in cuts[:parts]:
        load(*cut).start()
    take = pltpu.make_async_copy(query_hbm, query_ref, misc_sem.at[2])
    masks.wait()
    request(shard_blocks, capacity, mask_ref, tab_ref)
    pl.semaphore_wait(barrier, 6)

    def ask(peer, landing, near):
        return pltpu.make_async_remote_copy(
            src_ref=tab_ref.at[peer], dst_ref=asked_ref.at[peer if landing else me],
            send_sem=ask_send.at[0],
            recv_sem=ask_recv.at[near * (1 + (peer if landing else me) // spread)],
            device_id={"seq": peer}, device_id_type=MESH,
        )

    def asks(count):
        return pltpu.make_async_remote_copy(
            src_ref=tab_ref.at[pl.ds(0, count)], dst_ref=asked_ref.at[pl.ds(0, count)],
            send_sem=ask_send.at[0], recv_sem=ask_recv.at[0],
            device_id={"head": other}, device_id_type=MESH,
        )

    times(3, lambda i: ask(near_peer(i), False, 1).start())
    for cut in cuts:
        swap(*cut).start()
    for cut in cuts[parts:]:
        load(*cut).start()
    for number, step in enumerate((1, 2)):
        pl.semaphore_signal(
            step_sem.at[number], inc=1, device_id={"seq": peer_of(step)}, device_id_type=MESH
        )
    tell = pltpu.make_async_remote_copy(
        src_ref=tab_ref, dst_ref=far_tab_ref, send_sem=misc_sem.at[3], recv_sem=misc_sem.at[4],
        device_id={"head": other}, device_id_type=MESH,
    )
    tell.start()
    keep = pltpu.make_async_copy(tab_ref.at[me], asked_ref.at[me], misc_sem.at[5])
    keep.start()
    own = pltpu.make_async_copy(tab_ref, own_tab, misc_sem.at[6])
    own.start()
    perms.wait()
    for b in range(shard_blocks):
        blocks_ref[b * heads : (b + 1) * heads] = perm_ref[:, b * BLOCK : (b + 1) * BLOCK][:, None, :]
    rows_ref[...] = jnp.zeros_like(rows_ref)

    def near_scalar(peer):
        return pltpu.make_async_copy(
            asked_ref.at[peer], asked_near.at[peer], near_sem.at[peer // spread]
        )

    pl.semaphore_wait(step_sem.at[0], 1)
    pl.semaphore_wait(step_sem.at[1], 1)
    pl.semaphore_signal(step_sem.at[2], inc=1, device_id={"seq": peer_of(2)}, device_id_type=MESH)

    token = iota((BLOCK, 2 * rows), 1) + me * (2 * rows)

    def gather(table_ref, peer, whiches, put):
        chosen = []
        for c in range(capacity):
            pair = jnp.clip(table_ref[peer, 0, 2 * c], 0, heads * shard_blocks - 1)
            rows_ref[c : c + 1, :] = blocks_ref[pair]
            head = jnp.clip(table_ref[peer, 0, 2 * c + 1], 0, heads - 1)
            chosen.append(head * HEAD_DIM)
        turned = rows_ref[...].T
        for c, start_at in enumerate(chosen):
            table = (turned[:, c : c + 1] == token).astype(jnp.float32).astype(jnp.bfloat16)
            for which in whiches:
                got = jnp.dot(
                    table, sides[which][1][:, pl.ds(start_at, HEAD_DIM)],
                    preferred_element_type=jnp.float32,
                )
                put(which, c, got.astype(jnp.bfloat16))

    def to_send(peer):
        def put(which, c, got):
            send_ref[peer, which, c] = got

        return put

    def near_deliver(which, peer):
        return pltpu.make_async_remote_copy(
            src_ref=send_ref.at[peer, which], dst_ref=got_ref.at[0, me, which],
            send_sem=send_sem.at[0], recv_sem=recvs.at[me],
            device_id={"seq": peer}, device_id_type=MESH,
        )

    def deliver(peer, landing):
        source = peer if landing else me
        return pltpu.make_async_remote_copy(
            src_ref=send_ref.at[peer], dst_ref=got_ref.at[0, source],
            send_sem=send_sem.at[0], recv_sem=recvs.at[source],
            device_id={"seq": peer}, device_id_type=MESH,
        )

    def relay(source):
        return pltpu.make_async_remote_copy(
            src_ref=got_ref.at[0, source], dst_ref=got_ref.at[1, source],
            send_sem=relay_send.at[0], recv_sem=relay_recv.at[source],
            device_id={"head": other}, device_id_type=MESH,
        )

    def serve(i, which):
        peer = near_peer(i)
        if which == 0:
            near_scalar(peer).wait()
        gather(asked_near, peer, (which,), to_send(peer))
        near_deliver(which, peer).start()

    def heed(i):
        peer = near_peer(i)
        ask(peer, True, 1).wait_recv()
        near_scalar(peer).start()

    load(0, 0, half).wait()
    heed(0)
    pl.semaphore_wait(step_sem.at[2], 1)
    all_rest(lambda peer: ask(peer, False, 0).start())
    heed(1)
    swap(0, 0, half).wait_recv()
    serve(0, 0)
    serve(1, 0)
    heed(2)
    serve(2, 0)
    load(1, 0, half).wait()
    swap(1, 0, half).wait_recv()
    times(3, lambda i: serve(i, 1))
    take.start()
    own.wait()
    tell.wait_recv()
    far_scalar = pltpu.make_async_copy(far_tab_ref, far_tab, misc_sem.at[8])
    far_scalar.start()

    def to_got(which, c, got):
        got_ref[0, me, which, c] = got

    gather(own_tab, me, (0, 1), to_got)
    relay(me).start()
    keep.wait()
    asks(seq_count - 4).wait_recv()
    to_scalar = pltpu.make_async_copy(asked_ref, asked, misc_sem.at[7])
    to_scalar.start()
    to_scalar.wait()

    def produce(i):
        far = edge * ((i + 2 * beside) // (3 * beside)) + (1 - edge) * ((5 * beside - 1 - i) // (3 * beside))
        at = i - beside * edge + 3 * beside * (1 - far)
        peer = far * far_peer(at % (3 * beside)) + (1 - far) * side_peer(1, at % beside)
        gather(asked, peer, (0, 1), to_send(peer))
        deliver(peer, False).start()

    def produce_beside(k):
        peer = side_peer(0, k)
        gather(asked, peer, (0, 1), to_send(peer))
        deliver(peer, False).start()

    times(3 * beside, produce)
    times(beside, produce_beside)
    far_scalar.wait()
    take.wait()

    scale = math.log2(math.e) / math.sqrt(HEAD_DIM)
    ones = jnp.ones((BLOCK, HEAD_DIM), jnp.bfloat16)

    def attend(items):
        scores = []
        for rel, source, c in items:
            tab, base = ((own_tab, group), (far_tab, other))[rel]
            head = base * heads + jnp.clip(tab[source, 0, 2 * c + 1], 0, heads - 1)
            query = query_ref[:, pl.ds(head * HEAD_DIM, HEAD_DIM)]
            scores.append(
                lax.dot_general(
                    query, got_ref[rel, source, 0, c], (((1,), (1,)), ((), ())),
                    preferred_element_type=jnp.float32,
                )
            )
        weights = []
        for score in scores:
            peak = jnp.max(score, axis=1, keepdims=True)
            weights.append(jnp.exp2((score - peak) * scale).astype(jnp.bfloat16))
        for (rel, source, c), weight in zip(items, weights):
            mixed = jnp.dot(
                weight, jnp.concatenate([got_ref[rel, source, 1, c], ones], axis=1),
                preferred_element_type=jnp.float32,
            )
            stage_ref[rel, source * capacity + c] = (
                mixed[:, :HEAD_DIM] / mixed[:, HEAD_DIM:]
            ).astype(jnp.bfloat16)

    slots = lambda rel, source: [(rel, source, c) for c in range(capacity)]
    attend(slots(0, me))
    relay(me).wait_recv()
    attend(slots(1, me))

    def near_take(i):
        source = near_peer(i)
        deliver(source, True).wait_recv()
        relay(source).start()

    times(3, near_take)

    def near_use(i):
        source = near_peer(i)
        relay(source).wait_recv()
        attend(slots(0, source) + slots(1, source))

    times(3, near_use)

    def rest_peer(i):
        late = i // (2 * beside)
        plane = (1 - late) * (i // beside) + late * (2 + i % 2)
        return side_peer(plane, (1 - late) * (i % beside) + late * (i % (2 * beside) // 2))

    def use(i, first=False, last=False):
        before = [] if first else [rest_peer(2 * i - 2), rest_peer(2 * i - 1)]
        sources = [] if last else [rest_peer(2 * i), rest_peer(2 * i + 1)]
        for source in sources:
            deliver(source, True).wait_recv()
            relay(source).start()
        for source in before:
            relay(source).wait_recv()
        items = [slots(0, source) for source in sources] + [slots(1, source) for source in before]
        attend(sum(items, []))

    pairs = 2 * beside
    use(0, first=True)
    times(pairs - 1, lambda i: use(i + 1))
    use(pairs, last=True)

    for number in range(2):
        swap(number, 0, half).wait_send()
    asks(seq_count - 1).wait_send()
    tell.wait_send()
    pltpu.make_async_remote_copy(
        src_ref=send_ref.at[pl.ds(0, seq_count - 1)], dst_ref=got_ref.at[0, pl.ds(0, seq_count - 1)],
        send_sem=send_sem.at[0], recv_sem=recvs.at[me],
        device_id={"head": other}, device_id_type=MESH,
    ).wait_send()
    pltpu.make_async_remote_copy(
        src_ref=got_ref.at[0], dst_ref=got_ref.at[1],
        send_sem=relay_send.at[0], recv_sem=relay_recv.at[me],
        device_id={"head": other}, device_id_type=MESH,
    ).wait_send()


def flush_kernel(seq_count, stage_ref, tab_ref, far_tab_ref, out_ref, sem):
    group = lax.axis_index("head")
    heads = tab_ref.shape[0] - seq_count
    last = stage_ref.shape[1] - 1
    for local in range(heads):
        for rel, (tab, base) in enumerate(((tab_ref, group), (far_tab_ref, 1 - group))):
            slot = jnp.clip(tab[seq_count + local, 0, 0], 0, last)
            at = pl.multiple_of((base * heads + local) * HEAD_DIM, HEAD_DIM)
            pltpu.make_async_copy(
                stage_ref.at[rel, slot], out_ref.at[:, pl.ds(at, HEAD_DIM)], sem.at[0]
            ).start()
    pltpu.make_async_copy(out_ref, out_ref, sem.at[0]).wait()


def fused(key_states, value_states, queries, cluster_perm, block_mask, capacity):
    heads, shard_rows = cluster_perm.shape
    shard_blocks = shard_rows // BLOCK
    seq_count = lax.axis_size("seq")
    rows, columns = queries.shape
    vmem = pl.BlockSpec(memory_space=pltpu.VMEM)
    anywhere = pl.BlockSpec(memory_space=pltpu.HBM)
    bf16, i32 = jnp.bfloat16, jnp.int32
    dma = pltpu.SemaphoreType.DMA
    resident = 4 * seq_count * capacity * rows * HEAD_DIM + 8 * 8 * 128 * (seq_count + heads)
    table, asks = (seq_count + heads, 1, 128), (seq_count, 1, 128)
    staged = pl.pallas_call(
        functools.partial(fused_kernel, seq_count, capacity, shard_blocks),
        out_shape=(
            pltpu.VMEM((2, seq_count * capacity, rows, HEAD_DIM), bf16),
            pltpu.VMEM(table, i32), pltpu.VMEM(table, i32),
        ),
        in_specs=[anywhere] * 5,
        out_specs=(vmem, vmem, vmem),
        scratch_shapes=[
            pltpu.VMEM(cluster_perm.shape, i32), pltpu.VMEM(block_mask.shape, i32),
            pltpu.VMEM((shard_rows, heads * HEAD_DIM), bf16),
            pltpu.VMEM((shard_rows, heads * HEAD_DIM), bf16),
            pltpu.VMEM((rows, columns), bf16),
            pltpu.VMEM((seq_count, 2, capacity, BLOCK, HEAD_DIM), bf16),
            pltpu.VMEM((2, seq_count, 2, capacity, BLOCK, HEAD_DIM), bf16),
            pltpu.VMEM(asks, i32),
            pltpu.VMEM((8 * -(-capacity // 8), 128), i32),
            pltpu.VMEM((shard_blocks * heads, 1, BLOCK), i32),
            pltpu.SMEM(table, i32), pltpu.SMEM(table, i32),
            pltpu.SMEM(asks, i32), pltpu.SMEM(asks, i32),
            dma((4,)), dma((2,)), dma((2,)), dma((2,)), dma((1,)), dma((5,)), dma((9,)),
            dma((1,)), dma((seq_count,)), dma((1,)), dma((seq_count,)),
            pltpu.SemaphoreType.REGULAR((3,)),
        ],
        compiler_params=pltpu.CompilerParams(
            collective_id=1, has_side_effects=True,
            vmem_limit_bytes=67043328 - resident - 256 * 1024,
        ),
        name="fused",
    )(key_states, value_states, queries, cluster_perm, block_mask)
    return pl.pallas_call(
        functools.partial(flush_kernel, seq_count),
        out_shape=jax.ShapeDtypeStruct((rows, columns), bf16),
        in_specs=[vmem, vmem, vmem],
        out_specs=anywhere,
        scratch_shapes=[dma((1,))],
        compiler_params=pltpu.CompilerParams(vmem_limit_bytes=8 * 1024 * 1024),
        name="flush",
    )(*staged)


def attend_kernel(heads, picks, width, capacity, masked, pos_own, pos_far, *refs):
    if masked:
        query_ref, kv_ref, allow_ref, out_ref, stage, sems = refs
    else:
        query_ref, kv_ref, out_ref, stage, sems = refs
    group = lax.axis_index("head")
    scale = math.log2(math.e) / math.sqrt(HEAD_DIM)
    ones = jnp.ones((BLOCK, HEAD_DIM), jnp.bfloat16)
    span = width * HEAD_DIM
    batches = query_ref.shape[1] // span

    def put(batch, buffer):
        return pltpu.make_async_copy(
            stage.at[buffer],
            out_ref.at[:, pl.ds(pl.multiple_of(batch * span, span), span)],
            sems.at[buffer],
        )

    def one(batch, carry):
        where_, scores = [], []
        for w in range(width):
            head = batch * width + w
            away = (head // heads) != group
            local = head % heads
            query = query_ref[:, pl.ds(pl.multiple_of(head * HEAD_DIM, HEAD_DIM), HEAD_DIM)]
            for p in range(picks):
                slot = jnp.where(away, pos_far[local, p], pos_own[local, p])
                spot = (slot // capacity, slot % capacity)
                rel = away.astype(jnp.int32)
                where_.append((rel, spot))
                score = lax.dot_general(
                    query, kv_ref[rel, 0, spot[0], spot[1]], (((1,), (1,)), ((), ())),
                    preferred_element_type=jnp.float32,
                )
                if masked:
                    score = jnp.where(allow_ref[head, :, p : p + 1] > 0, score, -jnp.inf)
                scores.append(score)
        weights = []
        for w in range(width):
            own = scores[w * picks : (w + 1) * picks]
            top = jnp.max(functools.reduce(jnp.maximum, own), axis=1, keepdims=True)
            weights.extend([jnp.exp2((s - top) * scale).astype(jnp.bfloat16) for s in own])
        buffer = batch % 2

        @pl.when(batch >= 2)
        def _():
            put(batch - 2, buffer).wait()

        for w in range(width):
            parts = []
            for p in range(picks):
                rel, spot = where_[w * picks + p]
                parts.append(
                    jnp.dot(
                        weights[w * picks + p],
                        jnp.concatenate([kv_ref[rel, 1, spot[0], spot[1]], ones], axis=1),
                        preferred_element_type=jnp.float32,
                    )
                )
            mixed = functools.reduce(jnp.add, parts)
            stage[buffer, :, w * HEAD_DIM : (w + 1) * HEAD_DIM] = (
                mixed[:, :HEAD_DIM] / mixed[:, HEAD_DIM:]
            ).astype(jnp.bfloat16)
        put(batch, buffer).start()
        return carry

    lax.fori_loop(0, batches, one, 0)
    for batch in range(max(0, batches - 2), batches):
        put(batch, batch % 2).wait()


def token_allow(cluster_perm, block_mask, picks, me, shard_rows):
    needed = jnp.max(block_mask, axis=1)
    prefix = jnp.cumsum(needed, axis=1) - needed
    chosen = (needed[:, :, None] == 1) & (prefix[:, :, None] == jnp.arange(picks)[None, None, :])
    live = jnp.einsum(
        "hqb,hbp->hqp", block_mask.astype(jnp.float32), chosen.astype(jnp.float32)
    )
    group_heads = cluster_perm.shape[0]
    local = cluster_perm - me * shard_rows
    place = jnp.zeros((group_heads, shard_rows), jnp.int32)
    place = place.at[jnp.arange(group_heads)[:, None], local].set(
        jnp.broadcast_to(jnp.arange(shard_rows, dtype=jnp.int32) // BLOCK, local.shape)
    )
    by_token = jnp.take_along_axis(live, place[:, :, None], axis=1).astype(jnp.float32)
    return lax.all_to_all(by_token, "head", split_axis=1, concat_axis=0, tiled=True)


def shards(queries, key_states, value_states, cluster_perm, block_mask):
    group_heads, shard_rows = cluster_perm.shape
    shard_blocks = shard_rows // BLOCK
    seq_count = lax.axis_size("seq")
    block_total = block_mask.shape[2]
    picks = max(1, block_total // 64)
    capacity = max(
        1, min(shard_blocks, (group_heads * picks * 8 + 5 * seq_count - 1) // (5 * seq_count))
    )
    rows, columns = queries.shape
    me = lax.axis_index("seq")
    if picks == 1 and seq_count == 16 and shard_blocks * group_heads <= 256:
        return fused(key_states, value_states, queries, cluster_perm, block_mask, capacity)
    vmem = pl.BlockSpec(memory_space=pltpu.VMEM)
    anywhere = pl.BlockSpec(memory_space=pltpu.HBM)
    struct = jax.ShapeDtypeStruct
    bf16, i32 = jnp.bfloat16, jnp.int32

    dma = pltpu.SemaphoreType.DMA
    kv_half = pltpu.VMEM((group_heads, rows, HEAD_DIM), bf16)
    table = struct((group_heads, 128), i32)
    resident = 2 * (4 * seq_count * capacity * BLOCK * HEAD_DIM + rows * columns)
    grant = 67043328 - resident - 256 * 1024
    got, positions, pos_far, near_queries = pl.pallas_call(
        functools.partial(exchange_kernel, seq_count, capacity, shard_blocks, picks),
        out_shape=(
            pltpu.VMEM((2, 2, seq_count, capacity, BLOCK, HEAD_DIM), bf16), table, table,
            pltpu.VMEM((rows, columns), bf16),
        ),
        in_specs=[anywhere, anywhere, anywhere, vmem, vmem],
        out_specs=(vmem, vmem, vmem, vmem),
        scratch_shapes=[
            kv_half, kv_half, kv_half, kv_half,
            pltpu.VMEM((seq_count, 1, 128), i32),
            pltpu.VMEM((seq_count, 1, 128), i32),
            pltpu.SMEM((seq_count, 1, 128), i32),
            pltpu.VMEM((2, seq_count, capacity, BLOCK, HEAD_DIM), bf16),
            pltpu.VMEM((8 * -(-capacity // 8), 128), i32),
            pltpu.VMEM((shard_blocks * group_heads, 1, BLOCK), i32),
            dma((2 * group_heads,)), dma((2 * group_heads,)), dma((2 * group_heads,)),
            dma((seq_count,)), dma((seq_count,)), dma((7,)),
        ] + [dma((2, seq_count)) for _ in range(4)],
        compiler_params=pltpu.CompilerParams(
            collective_id=0, has_side_effects=True, vmem_limit_bytes=grant
        ),
        name="exchange",
    )(key_states, value_states, queries, cluster_perm, block_mask)

    masked = picks > 1
    total_heads = columns // HEAD_DIM
    width = 8 if total_heads % 8 == 0 else 1
    operands = [near_queries, got]
    if masked:
        operands.append(token_allow(cluster_perm, block_mask, picks, me, shard_rows))
    smem = pl.BlockSpec(memory_space=pltpu.SMEM)
    return pl.pallas_call(
        functools.partial(attend_kernel, group_heads, picks, width, capacity, masked),
        out_shape=struct((rows, columns), bf16),
        in_specs=[smem, smem] + [vmem] * len(operands),
        out_specs=anywhere,
        scratch_shapes=[pltpu.VMEM((2, rows, width * HEAD_DIM), bf16), dma((2,))],
        compiler_params=pltpu.CompilerParams(vmem_limit_bytes=24 * 1024 * 1024),
        name="attend",
    )(positions, pos_far, *operands)


def solution(mesh):
    rows = P(("seq", "head"), None)
    placed = (rows, rows, rows, P("head", "seq"), P("head", "seq", None))
    return jax.shard_map(shards, mesh=mesh, in_specs=placed, out_specs=rows, check_vma=False)
```

```python
import functools
import math

import jax
import jax.numpy as jnp
from jax import lax
from jax.experimental import pallas as pl
from jax.experimental.pallas import tpu as pltpu
from jax.sharding import PartitionSpec as P

HEAD_DIM = 128
BLOCK = 128
MESH = pl.DeviceIdType.MESH
HIGHEST = lax.Precision.HIGHEST


def iota(shape, dim):
    return lax.broadcasted_iota(jnp.int32, shape, dim)


def partner_of(me, step, count):
    if count & (count - 1):
        raise ValueError("seq size")
    peer = 0
    bit = 1
    while bit < count:
        peer = peer + bit * (((me // bit) + (step // bit)) % 2)
        bit *= 2
    return peer


def route(shard_blocks, capacity, picks, mask_ref, req_ref, pos_ref):
    heads, _, blocks = mask_ref.shape
    seq_count = blocks // shard_blocks
    needed = jnp.max(mask_ref[...], axis=1).astype(jnp.float32)
    row, col = iota((blocks, blocks), 0), iota((blocks, blocks), 1)
    same = (row // shard_blocks) == (col // shard_blocks)
    dot = functools.partial(jnp.dot, precision=HIGHEST, preferred_element_type=jnp.float32)
    ones = lambda flag: flag.astype(jnp.float32)
    by_owner = dot(needed, ones(same))
    before_in_owner = dot(needed, ones(same & (row < col)))
    before_all = dot(needed, ones(row < col))
    lower = ones(iota((heads, heads), 1) < iota((heads, heads), 0))
    rank = dot(lower, by_owner) + before_in_owner
    head_ids, block_ids = iota((heads, blocks), 0), iota((heads, blocks), 1)
    pair = (block_ids % shard_blocks * heads + head_ids).astype(jnp.float32)
    slot_row = iota((128, blocks), 0)
    sums = jnp.zeros((128, blocks), jnp.float32)
    for c in range(capacity):
        hit = jnp.where((rank == c) & (needed > 0.5), pair, 0.0)
        sums = jnp.where(slot_row == 2 * c, jnp.sum(hit, axis=0, keepdims=True), sums)
        hit = jnp.where((rank == c) & (needed > 0.5), head_ids.astype(jnp.float32), 0.0)
        sums = jnp.where(slot_row == 2 * c + 1, jnp.sum(hit, axis=0, keepdims=True), sums)
    owner_t = ones(iota((seq_count, blocks), 1) // shard_blocks == iota((seq_count, blocks), 0))
    asked = lax.dot_general(
        owner_t, sums, (((1,), (1,)), ((), ())), precision=HIGHEST,
        preferred_element_type=jnp.float32,
    )
    req_ref[...] = (asked + 0.5).astype(jnp.int32)[:, None, :]
    position = (block_ids // shard_blocks * capacity).astype(jnp.float32) + rank
    lane = iota((heads, 128), 1)
    table = jnp.zeros((heads, 128), jnp.float32)
    for p in range(picks):
        here = jnp.where((before_all == p) & (needed > 0.5), position, 0.0)
        table = jnp.where(lane == p, jnp.sum(here, axis=1, keepdims=True), table)
    pos_ref[...] = (table + 0.5).astype(jnp.int32)


def order(i, me, count):
    top, next_bit = (me // (count // 2)) % 2, (me // (count // 4)) % 2
    end = (top + next_bit + 1) % 2
    return end * (1 + (i + count // 4 - 1) % (count - 1)) + (1 - end) * (count - 1 - i)


def exchange_kernel(
    seq_count, capacity, shard_blocks, picks,
    key_ref, value_ref, query_ref, perm_ref, mask_ref, got_ref, pos_ref, pos_out, query_out,
    near_key, near_value, far_key, far_value, req_ref, asked_ref, asked, send_ref, rows_ref, blocks_ref,
    load_sem, swap_send, swap_recv, req_send, req_recv, misc_sem,
    sends, recvs, relay_send, relay_recv,
):
    group, me = lax.axis_index("head"), lax.axis_index("seq")
    other = 1 - group
    near_kv, far_kv = (near_key, near_value), (far_key, far_value)
    heads, rows = near_key.shape[:2]
    barrier = pltpu.get_barrier_semaphore()
    pl.semaphore_signal(barrier, inc=1, device_id={"head": other}, device_id_type=MESH)

    def greet(step, carry):
        pl.semaphore_signal(
            barrier, inc=1, device_id={"seq": partner_of(me, step, seq_count)}, device_id_type=MESH
        )
        return carry

    lax.fori_loop(1, seq_count, greet, 0)
    loads = []
    for number, src in enumerate((key_ref, value_ref)):
        for head in range(heads):
            start_at = pl.multiple_of((group * heads + head) * HEAD_DIM, HEAD_DIM)
            loads.append(
                pltpu.make_async_copy(
                    src.at[:, pl.ds(start_at, HEAD_DIM)], near_kv[number].at[head],
                    load_sem.at[number * heads + head],
                )
            )
    for copy in loads:
        copy.start()
    pl.semaphore_wait(barrier, seq_count)

    swaps = []
    for number, src in enumerate((key_ref, value_ref)):
        for head in range(heads):
            start_at = pl.multiple_of((other * heads + head) * HEAD_DIM, HEAD_DIM)
            at = number * heads + head
            swaps.append(
                pltpu.make_async_remote_copy(
                    src_ref=src.at[:, pl.ds(start_at, HEAD_DIM)], dst_ref=far_kv[number].at[head],
                    send_sem=swap_send.at[at], recv_sem=swap_recv.at[at],
                    device_id={"head": other}, device_id_type=MESH,
                )
            )
    for copy in swaps:
        copy.start()
    route(shard_blocks, capacity, picks, mask_ref, req_ref, pos_ref)
    for b in range(shard_blocks):
        blocks_ref[b * heads : (b + 1) * heads] = perm_ref[:, b * BLOCK : (b + 1) * BLOCK][:, None, :]
    rows_ref[...] = jnp.zeros_like(rows_ref)

    def ask(step, landing):
        peer = partner_of(me, step, seq_count)
        return pltpu.make_async_remote_copy(
            src_ref=req_ref.at[peer], dst_ref=asked_ref.at[peer if landing else me],
            send_sem=req_send.at[step], recv_sem=req_recv.at[step],
            device_id={"seq": peer}, device_id_type=MESH,
        )

    def start_ask(step, carry):
        ask(step, False).start()
        return carry

    lax.fori_loop(1, seq_count, start_ask, 0)
    tell = pltpu.make_async_remote_copy(
        src_ref=pos_ref, dst_ref=pos_out, send_sem=misc_sem.at[0], recv_sem=misc_sem.at[1],
        device_id={"head": other}, device_id_type=MESH,
    )
    tell.start()
    stay = pltpu.make_async_copy(query_ref, query_out, misc_sem.at[6])
    stay.start()
    keep = pltpu.make_async_copy(req_ref.at[me], asked_ref.at[me], misc_sem.at[2])
    keep.start()
    keep.wait()

    def finish_ask(step, carry):
        ask(step, True).wait()
        return carry

    lax.fori_loop(1, seq_count, finish_ask, 0)
    to_scalar = pltpu.make_async_copy(asked_ref, asked, misc_sem.at[3])
    to_scalar.start()
    to_scalar.wait()
    base = me * (2 * rows)
    token = iota((BLOCK, rows), 1)
    near = token + (base + group * rows)
    far = token + (base + other * rows)

    def gather(which, peer):
        chosen = []
        for c in range(capacity):
            pair = jnp.clip(asked[peer, 0, 2 * c], 0, heads * shard_blocks - 1)
            rows_ref[c : c + 1, :] = blocks_ref[pair]
            chosen.append(jnp.clip(asked[peer, 0, 2 * c + 1], 0, heads - 1))
        turned = rows_ref[...].T
        for c, head in enumerate(chosen):
            column = turned[:, c : c + 1]
            near_table = (column == near).astype(jnp.float32).astype(jnp.bfloat16)
            far_table = (column == far).astype(jnp.float32).astype(jnp.bfloat16)
            got = jnp.dot(near_table, near_kv[which][head], preferred_element_type=jnp.float32)
            got += jnp.dot(far_table, far_kv[which][head], preferred_element_type=jnp.float32)
            send_ref[which, peer, c] = got.astype(jnp.bfloat16)

    def deliver(which, step, landing):
        peer = partner_of(me, step, seq_count)
        return pltpu.make_async_remote_copy(
            src_ref=send_ref.at[which, peer],
            dst_ref=got_ref.at[0, which, peer if landing else me],
            send_sem=sends.at[which, step], recv_sem=recvs.at[which, step],
            device_id={"seq": peer}, device_id_type=MESH,
        )

    def relay(which, step):
        peer = partner_of(me, step, seq_count)
        return pltpu.make_async_remote_copy(
            src_ref=got_ref.at[0, which, peer], dst_ref=got_ref.at[1, which, peer],
            send_sem=relay_send.at[which, step], recv_sem=relay_recv.at[which, step],
            device_id={"head": other}, device_id_type=MESH,
        )

    for which in range(2):
        for copy in loads[which * heads : (which + 1) * heads]:
            copy.wait()
        for copy in swaps[which * heads : (which + 1) * heads]:
            copy.wait()
        gather(which, partner_of(me, order(0, me, seq_count), seq_count))

        def produce(i, carry, which=which):
            gather(which, partner_of(me, order(i, me, seq_count), seq_count))
            deliver(which, order(i - 1, me, seq_count), False).start()
            return carry

        lax.fori_loop(1, seq_count - 1, produce, 0)
        gather(which, me)
        deliver(which, order(seq_count - 2, me, seq_count), False).start()

    locals_ = []
    for which in range(2):
        mine = pltpu.make_async_copy(
            send_ref.at[which, me], got_ref.at[0, which, me], misc_sem.at[4 + which]
        )
        share = pltpu.make_async_remote_copy(
            src_ref=send_ref.at[which, me], dst_ref=got_ref.at[1, which, me],
            send_sem=relay_send.at[which, 0], recv_sem=relay_recv.at[which, 0],
            device_id={"head": other}, device_id_type=MESH,
        )
        mine.start()
        share.start()
        locals_.extend((mine, share))

    for which in range(2):

        def pass_on(i, carry, which=which):
            step = order(i, me, seq_count)
            deliver(which, step, True).wait_recv()
            relay(which, step).start()
            return carry

        lax.fori_loop(0, seq_count - 1, pass_on, 0)

    def finish(step, carry):
        for which in range(2):
            deliver(which, step, True).wait_send()
            relay(which, step).wait()
        return carry

    lax.fori_loop(1, seq_count, finish, 0)
    for copy in locals_:
        copy.wait()
    tell.wait()
    stay.wait()


def request(shard_blocks, capacity, mask_ref, tab_ref):
    heads, _, blocks = mask_ref.shape
    seq_count = blocks // shard_blocks
    needed = jnp.max(mask_ref[...], axis=1).astype(jnp.float32)
    row, col = iota((blocks, blocks), 0), iota((blocks, blocks), 1)
    same = (row // shard_blocks) == (col // shard_blocks)
    small = lambda value: value.astype(jnp.float32).astype(jnp.bfloat16)
    dot = functools.partial(jnp.dot, preferred_element_type=jnp.float32)
    by_owner = dot(small(needed), small(same))
    lower = small(iota((heads, heads), 1) < iota((heads, heads), 0))
    rank = dot(lower, small(by_owner)) + dot(small(needed), small(same & (row < col)))
    head_ids, block_ids = iota((heads, blocks), 0), iota((heads, blocks), 1)
    pair = (block_ids % shard_blocks * heads + head_ids).astype(jnp.float32)
    slot_row = iota((128, blocks), 0)
    sums = jnp.zeros((128, blocks), jnp.float32)
    for c in range(capacity):
        taken = (rank == c) & (needed > 0.5)
        for lane, value in ((2 * c, pair), (2 * c + 1, head_ids.astype(jnp.float32))):
            hit = jnp.sum(jnp.where(taken, value, 0.0), axis=0, keepdims=True)
            sums = jnp.where(slot_row == lane, hit, sums)
    owner_t = small(iota((seq_count, blocks), 1) // shard_blocks == iota((seq_count, blocks), 0))
    asked = lax.dot_general(
        owner_t, small(sums), (((1,), (1,)), ((), ())), preferred_element_type=jnp.float32
    )
    tab_ref[:seq_count] = (asked + 0.5).astype(jnp.int32)[:, None, :]
    spot = (block_ids // shard_blocks * capacity).astype(jnp.float32) + rank
    spot = jnp.sum(jnp.where(needed > 0.5, spot, 0.0), axis=1, keepdims=True)
    spot = (jnp.broadcast_to(spot, (heads, 128)) + 0.5).astype(jnp.int32)
    tab_ref[seq_count:] = spot[:, None, :]


def fused_kernel(
    seq_count, capacity, shard_blocks,
    key_ref, value_ref, query_hbm, perm_hbm, mask_hbm, stage_ref, tab_ref, far_tab_ref,
    perm_ref, mask_ref, keys, values, query_ref, send_ref, got_ref, asked_ref, rows_ref, blocks_ref,
    own_tab, far_tab, asked_near, asked,
    near_sem, load_sem, swap_send, swap_recv, ask_send, ask_recv, misc_sem,
    send_sem, recvs, relay_send, relay_recv, step_sem,
):
    group, me = lax.axis_index("head"), lax.axis_index("seq")
    other = 1 - group
    heads = perm_ref.shape[0]
    rows = query_hbm.shape[0]
    half = heads * HEAD_DIM
    spread = seq_count // 4
    peer_of = lambda step: partner_of(me, step, seq_count)
    top, low = (me // (2 * spread)) % 2, (me // spread) % 2
    edge = (top + low + 1) % 2

    def near_peer(i):
        far = (3 - i) // 2
        turn = edge * ((i + 1) // 2) + (1 - edge) * ((i + 1) % 2)
        return peer_of(spread * (2 * far + turn))

    def side_peer(plane, k):
        return peer_of(spread * plane + 1 + k)

    def far_peer(k):
        return side_peer(2 + (edge + (1 - top) * (1 - group) + k) % 2, k // 2)

    def times(count, body):
        lax.fori_loop(0, count, lambda i, carry: (body(i), carry)[1], 0)

    beside = spread - 1

    def all_rest(body):
        times(beside, lambda k: body(side_peer(0, k)))
        times(beside, lambda k: body(side_peer(1, k)))
        times(2 * beside, lambda k: body(far_peer(k)))

    barrier = pltpu.get_barrier_semaphore()
    pl.semaphore_signal(barrier, inc=1, device_id={"head": other}, device_id_type=MESH)
    for step in (spread, 2 * spread, 3 * spread, 1, 2):
        pl.semaphore_signal(barrier, inc=1, device_id={"seq": peer_of(step)}, device_id_type=MESH)

    masks = pltpu.make_async_copy(mask_hbm, mask_ref, misc_sem.at[0])
    masks.start()
    perms = pltpu.make_async_copy(perm_hbm, perm_ref, misc_sem.at[1])
    perms.start()
    here = pl.ds(pl.multiple_of(group * rows, rows), rows)
    sides = ((key_ref, keys), (value_ref, values))

    def load(number, start_at, span):
        src, dst = sides[number]
        mine = pl.ds(pl.multiple_of(group * half + start_at, HEAD_DIM), span)
        return pltpu.make_async_copy(
            src.at[:, mine], dst.at[here, pl.ds(start_at, span)], load_sem.at[number]
        )

    def swap(number, start_at, span):
        src, dst = sides[number]
        theirs = pl.ds(pl.multiple_of(other * half + start_at, HEAD_DIM), span)
        return pltpu.make_async_remote_copy(
            src_ref=src.at[:, theirs], dst_ref=dst.at[here, pl.ds(start_at, span)],
            send_sem=swap_send.at[number], recv_sem=swap_recv.at[number],
            device_id={"head": other}, device_id_type=MESH,
        )

    parts = 4
    cuts = [(number, part * (half // parts), half // parts) for number in range(2) for part in range(parts)]
    for cut in cuts[:parts]:
        load(*cut).start()
    take = pltpu.make_async_copy(query_hbm, query_ref, misc_sem.at[2])
    masks.wait()
    request(shard_blocks, capacity, mask_ref, tab_ref)
    pl.semaphore_wait(barrier, 6)

    def ask(peer, landing, near):
        return pltpu.make_async_remote_copy(
            src_ref=tab_ref.at[peer], dst_ref=asked_ref.at[peer if landing else me],
            send_sem=ask_send.at[0],
            recv_sem=ask_recv.at[near * (1 + (peer if landing else me) // spread)],
            device_id={"seq": peer}, device_id_type=MESH,
        )

    def asks(count):
        return pltpu.make_async_remote_copy(
            src_ref=tab_ref.at[pl.ds(0, count)], dst_ref=asked_ref.at[pl.ds(0, count)],
            send_sem=ask_send.at[0], recv_sem=ask_recv.at[0],
            device_id={"head": other}, device_id_type=MESH,
        )

    times(3, lambda i: ask(near_peer(i), False, 1).start())
    for cut in cuts:
        swap(*cut).start()
    for cut in cuts[parts:]:
        load(*cut).start()
    for number, step in enumerate((1, 2)):
        pl.semaphore_signal(
            step_sem.at[number], inc=1, device_id={"seq": peer_of(step)}, device_id_type=MESH
        )
    tell = pltpu.make_async_remote_copy(
        src_ref=tab_ref, dst_ref=far_tab_ref, send_sem=misc_sem.at[3], recv_sem=misc_sem.at[4],
        device_id={"head": other}, device_id_type=MESH,
    )
    tell.start()
    keep = pltpu.make_async_copy(tab_ref.at[me], asked_ref.at[me], misc_sem.at[5])
    keep.start()
    own = pltpu.make_async_copy(tab_ref, own_tab, misc_sem.at[6])
    own.start()
    perms.wait()
    for b in range(shard_blocks):
        blocks_ref[b * heads : (b + 1) * heads] = perm_ref[:, b * BLOCK : (b + 1) * BLOCK][:, None, :]
    rows_ref[...] = jnp.zeros_like(rows_ref)

    def near_scalar(peer):
        return pltpu.make_async_copy(
            asked_ref.at[peer], asked_near.at[peer], near_sem.at[peer // spread]
        )

    pl.semaphore_wait(step_sem.at[0], 1)
    pl.semaphore_wait(step_sem.at[1], 1)
    pl.semaphore_signal(step_sem.at[2], inc=1, device_id={"seq": peer_of(2)}, device_id_type=MESH)

    token = iota((BLOCK, 2 * rows), 1) + me * (2 * rows)

    def gather(table_ref, peer, whiches, put):
        chosen = []
        for c in range(capacity):
            pair = jnp.clip(table_ref[peer, 0, 2 * c], 0, heads * shard_blocks - 1)
            rows_ref[c : c + 1, :] = blocks_ref[pair]
            head = jnp.clip(table_ref[peer, 0, 2 * c + 1], 0, heads - 1)
            chosen.append(head * HEAD_DIM)
        turned = rows_ref[...].T
        for c, start_at in enumerate(chosen):
            table = (turned[:, c : c + 1] == token).astype(jnp.float32).astype(jnp.bfloat16)
            for which in whiches:
                got = jnp.dot(
                    table, sides[which][1][:, pl.ds(start_at, HEAD_DIM)],
                    preferred_element_type=jnp.float32,
                )
                put(which, c, got.astype(jnp.bfloat16))

    def to_send(peer):
        def put(which, c, got):
            send_ref[peer, which, c] = got

        return put

    def near_deliver(which, peer):
        return pltpu.make_async_remote_copy(
            src_ref=send_ref.at[peer, which], dst_ref=got_ref.at[0, me, which],
            send_sem=send_sem.at[0], recv_sem=recvs.at[me],
            device_id={"seq": peer}, device_id_type=MESH,
        )

    def deliver(peer, landing):
        source = peer if landing else me
        return pltpu.make_async_remote_copy(
            src_ref=send_ref.at[peer], dst_ref=got_ref.at[0, source],
            send_sem=send_sem.at[0], recv_sem=recvs.at[source],
            device_id={"seq": peer}, device_id_type=MESH,
        )

    def relay(source):
        return pltpu.make_async_remote_copy(
            src_ref=got_ref.at[0, source], dst_ref=got_ref.at[1, source],
            send_sem=relay_send.at[0], recv_sem=relay_recv.at[source],
            device_id={"head": other}, device_id_type=MESH,
        )

    def serve(i, which):
        peer = near_peer(i)
        if which == 0:
            near_scalar(peer).wait()
        gather(asked_near, peer, (which,), to_send(peer))
        near_deliver(which, peer).start()

    def heed(i):
        peer = near_peer(i)
        ask(peer, True, 1).wait_recv()
        near_scalar(peer).start()

    load(0, 0, half).wait()
    heed(0)
    pl.semaphore_wait(step_sem.at[2], 1)
    all_rest(lambda peer: ask(peer, False, 0).start())
    heed(1)
    swap(0, 0, half).wait_recv()
    serve(0, 0)
    serve(1, 0)
    heed(2)
    serve(2, 0)
    load(1, 0, half).wait()
    swap(1, 0, half).wait_recv()
    times(3, lambda i: serve(i, 1))
    take.start()
    own.wait()
    tell.wait_recv()
    far_scalar = pltpu.make_async_copy(far_tab_ref, far_tab, misc_sem.at[8])
    far_scalar.start()

    def to_got(which, c, got):
        got_ref[0, me, which, c] = got

    gather(own_tab, me, (0, 1), to_got)
    relay(me).start()
    keep.wait()
    asks(seq_count - 4).wait_recv()
    to_scalar = pltpu.make_async_copy(asked_ref, asked, misc_sem.at[7])
    to_scalar.start()
    to_scalar.wait()

    def produce(i):
        far = edge * ((i + 2 * beside) // (3 * beside)) + (1 - edge) * ((5 * beside - 1 - i) // (3 * beside))
        at = i - beside * edge + 3 * beside * (1 - far)
        peer = far * far_peer(at % (3 * beside)) + (1 - far) * side_peer(1, at % beside)
        gather(asked, peer, (0, 1), to_send(peer))
        deliver(peer, False).start()

    def produce_beside(k):
        peer = side_peer(0, k)
        gather(asked, peer, (0, 1), to_send(peer))
        deliver(peer, False).start()

    times(3 * beside, produce)
    times(beside, produce_beside)
    far_scalar.wait()
    take.wait()

    scale = math.log2(math.e) / math.sqrt(HEAD_DIM)
    ones = jnp.ones((BLOCK, HEAD_DIM), jnp.bfloat16)

    def attend(items):
        scores = []
        for rel, source, c in items:
            tab, base = ((own_tab, group), (far_tab, other))[rel]
            head = base * heads + jnp.clip(tab[source, 0, 2 * c + 1], 0, heads - 1)
            query = query_ref[:, pl.ds(head * HEAD_DIM, HEAD_DIM)]
            scores.append(
                lax.dot_general(
                    query, got_ref[rel, source, 0, c], (((1,), (1,)), ((), ())),
                    preferred_element_type=jnp.float32,
                )
            )
        weights = []
        for score in scores:
            peak = jnp.max(score, axis=1, keepdims=True)
            weights.append(jnp.exp2((score - peak) * scale).astype(jnp.bfloat16))
        for (rel, source, c), weight in zip(items, weights):
            mixed = jnp.dot(
                weight, jnp.concatenate([got_ref[rel, source, 1, c], ones], axis=1),
                preferred_element_type=jnp.float32,
            )
            stage_ref[rel, source * capacity + c] = (
                mixed[:, :HEAD_DIM] / mixed[:, HEAD_DIM:]
            ).astype(jnp.bfloat16)

    slots = lambda rel, source: [(rel, source, c) for c in range(capacity)]
    attend(slots(0, me))
    relay(me).wait_recv()
    attend(slots(1, me))

    def near_take(i):
        source = near_peer(i)
        deliver(source, True).wait_recv()
        relay(source).start()

    times(3, near_take)

    def near_use(i):
        source = near_peer(i)
        relay(source).wait_recv()
        attend(slots(0, source) + slots(1, source))

    times(3, near_use)

    def rest_peer(i):
        late = i // (2 * beside)
        plane = (1 - late) * (i // beside) + late * (2 + i % 2)
        return side_peer(plane, (1 - late) * (i % beside) + late * (i % (2 * beside) // 2))

    def use(i, first=False, last=False):
        before = [] if first else [rest_peer(2 * i - 2), rest_peer(2 * i - 1)]
        sources = [] if last else [rest_peer(2 * i), rest_peer(2 * i + 1)]
        for source in sources:
            deliver(source, True).wait_recv()
            relay(source).start()
        for source in before:
            relay(source).wait_recv()
        items = [slots(0, source) for source in sources] + [slots(1, source) for source in before]
        attend(sum(items, []))

    pairs = 2 * beside
    use(0, first=True)
    times(pairs - 1, lambda i: use(i + 1))
    use(pairs, last=True)

    for number in range(2):
        swap(number, 0, half).wait_send()
    asks(seq_count - 1).wait_send()
    tell.wait_send()
    pltpu.make_async_remote_copy(
        src_ref=send_ref.at[pl.ds(0, seq_count - 1)], dst_ref=got_ref.at[0, pl.ds(0, seq_count - 1)],
        send_sem=send_sem.at[0], recv_sem=recvs.at[me],
        device_id={"head": other}, device_id_type=MESH,
    ).wait_send()
    pltpu.make_async_remote_copy(
        src_ref=got_ref.at[0], dst_ref=got_ref.at[1],
        send_sem=relay_send.at[0], recv_sem=relay_recv.at[me],
        device_id={"head": other}, device_id_type=MESH,
    ).wait_send()


def flush_kernel(seq_count, stage_ref, tab_ref, far_tab_ref, out_ref, sem):
    group = lax.axis_index("head")
    heads = tab_ref.shape[0] - seq_count
    last = stage_ref.shape[1] - 1
    for local in range(heads):
        for rel, (tab, base) in enumerate(((tab_ref, group), (far_tab_ref, 1 - group))):
            slot = jnp.clip(tab[seq_count + local, 0, 0], 0, last)
            at = pl.multiple_of((base * heads + local) * HEAD_DIM, HEAD_DIM)
            pltpu.make_async_copy(
                stage_ref.at[rel, slot], out_ref.at[:, pl.ds(at, HEAD_DIM)], sem.at[0]
            ).start()
    pltpu.make_async_copy(out_ref, out_ref, sem.at[0]).wait()


def fused(key_states, value_states, queries, cluster_perm, block_mask, capacity):
    heads, shard_rows = cluster_perm.shape
    shard_blocks = shard_rows // BLOCK
    seq_count = lax.axis_size("seq")
    rows, columns = queries.shape
    vmem = pl.BlockSpec(memory_space=pltpu.VMEM)
    anywhere = pl.BlockSpec(memory_space=pltpu.HBM)
    bf16, i32 = jnp.bfloat16, jnp.int32
    dma = pltpu.SemaphoreType.DMA
    resident = 4 * seq_count * capacity * rows * HEAD_DIM + 8 * 8 * 128 * (seq_count + heads)
    table, asks = (seq_count + heads, 1, 128), (seq_count, 1, 128)
    staged = pl.pallas_call(
        functools.partial(fused_kernel, seq_count, capacity, shard_blocks),
        out_shape=(
            pltpu.VMEM((2, seq_count * capacity, rows, HEAD_DIM), bf16),
            pltpu.VMEM(table, i32), pltpu.VMEM(table, i32),
        ),
        in_specs=[anywhere] * 5,
        out_specs=(vmem, vmem, vmem),
        scratch_shapes=[
            pltpu.VMEM(cluster_perm.shape, i32), pltpu.VMEM(block_mask.shape, i32),
            pltpu.VMEM((shard_rows, heads * HEAD_DIM), bf16),
            pltpu.VMEM((shard_rows, heads * HEAD_DIM), bf16),
            pltpu.VMEM((rows, columns), bf16),
            pltpu.VMEM((seq_count, 2, capacity, BLOCK, HEAD_DIM), bf16),
            pltpu.VMEM((2, seq_count, 2, capacity, BLOCK, HEAD_DIM), bf16),
            pltpu.VMEM(asks, i32),
            pltpu.VMEM((8 * -(-capacity // 8), 128), i32),
            pltpu.VMEM((shard_blocks * heads, 1, BLOCK), i32),
            pltpu.SMEM(table, i32), pltpu.SMEM(table, i32),
            pltpu.SMEM(asks, i32), pltpu.SMEM(asks, i32),
            dma((4,)), dma((2,)), dma((2,)), dma((2,)), dma((1,)), dma((5,)), dma((9,)),
            dma((1,)), dma((seq_count,)), dma((1,)), dma((seq_count,)),
            pltpu.SemaphoreType.REGULAR((3,)),
        ],
        compiler_params=pltpu.CompilerParams(
            collective_id=1, has_side_effects=True,
            vmem_limit_bytes=67043328 - resident - 256 * 1024,
        ),
        name="fused",
    )(key_states, value_states, queries, cluster_perm, block_mask)
    return pl.pallas_call(
        functools.partial(flush_kernel, seq_count),
        out_shape=jax.ShapeDtypeStruct((rows, columns), bf16),
        in_specs=[vmem, vmem, vmem],
        out_specs=anywhere,
        scratch_shapes=[dma((1,))],
        compiler_params=pltpu.CompilerParams(vmem_limit_bytes=8 * 1024 * 1024),
        name="flush",
    )(*staged)


def attend_kernel(heads, picks, width, capacity, masked, pos_own, pos_far, *refs):
    if masked:
        query_ref, kv_ref, allow_ref, out_ref, stage, sems = refs
    else:
        query_ref, kv_ref, out_ref, stage, sems = refs
    group = lax.axis_index("head")
    scale = math.log2(math.e) / math.sqrt(HEAD_DIM)
    ones = jnp.ones((BLOCK, HEAD_DIM), jnp.bfloat16)
    span = width * HEAD_DIM
    batches = query_ref.shape[1] // span

    def put(batch, buffer):
        return pltpu.make_async_copy(
            stage.at[buffer],
            out_ref.at[:, pl.ds(pl.multiple_of(batch * span, span), span)],
            sems.at[buffer],
        )

    def one(batch, carry):
        where_, scores = [], []
        for w in range(width):
            head = batch * width + w
            away = (head // heads) != group
            local = head % heads
            query = query_ref[:, pl.ds(pl.multiple_of(head * HEAD_DIM, HEAD_DIM), HEAD_DIM)]
            for p in range(picks):
                slot = jnp.where(away, pos_far[local, p], pos_own[local, p])
                spot = (slot // capacity, slot % capacity)
                rel = away.astype(jnp.int32)
                where_.append((rel, spot))
                score = lax.dot_general(
                    query, kv_ref[rel, 0, spot[0], spot[1]], (((1,), (1,)), ((), ())),
                    preferred_element_type=jnp.float32,
                )
                if masked:
                    score = jnp.where(allow_ref[head, :, p : p + 1] > 0, score, -jnp.inf)
                scores.append(score)
        weights = []
        for w in range(width):
            own = scores[w * picks : (w + 1) * picks]
            top = jnp.max(functools.reduce(jnp.maximum, own), axis=1, keepdims=True)
            weights.extend([jnp.exp2((s - top) * scale).astype(jnp.bfloat16) for s in own])
        buffer = batch % 2

        @pl.when(batch >= 2)
        def _():
            put(batch - 2, buffer).wait()

        for w in range(width):
            parts = []
            for p in range(picks):
                rel, spot = where_[w * picks + p]
                parts.append(
                    jnp.dot(
                        weights[w * picks + p],
                        jnp.concatenate([kv_ref[rel, 1, spot[0], spot[1]], ones], axis=1),
                        preferred_element_type=jnp.float32,
                    )
                )
            mixed = functools.reduce(jnp.add, parts)
            stage[buffer, :, w * HEAD_DIM : (w + 1) * HEAD_DIM] = (
                mixed[:, :HEAD_DIM] / mixed[:, HEAD_DIM:]
            ).astype(jnp.bfloat16)
        put(batch, buffer).start()
        return carry

    lax.fori_loop(0, batches, one, 0)
    for batch in range(max(0, batches - 2), batches):
        put(batch, batch % 2).wait()


def token_allow(cluster_perm, block_mask, picks, me, shard_rows):
    needed = jnp.max(block_mask, axis=1)
    prefix = jnp.cumsum(needed, axis=1) - needed
    chosen = (needed[:, :, None] == 1) & (prefix[:, :, None] == jnp.arange(picks)[None, None, :])
    live = jnp.einsum(
        "hqb,hbp->hqp", block_mask.astype(jnp.float32), chosen.astype(jnp.float32)
    )
    group_heads = cluster_perm.shape[0]
    local = cluster_perm - me * shard_rows
    place = jnp.zeros((group_heads, shard_rows), jnp.int32)
    place = place.at[jnp.arange(group_heads)[:, None], local].set(
        jnp.broadcast_to(jnp.arange(shard_rows, dtype=jnp.int32) // BLOCK, local.shape)
    )
    by_token = jnp.take_along_axis(live, place[:, :, None], axis=1).astype(jnp.float32)
    return lax.all_to_all(by_token, "head", split_axis=1, concat_axis=0, tiled=True)


def shards(queries, key_states, value_states, cluster_perm, block_mask):
    group_heads, shard_rows = cluster_perm.shape
    shard_blocks = shard_rows // BLOCK
    seq_count = lax.axis_size("seq")
    block_total = block_mask.shape[2]
    picks = max(1, block_total // 64)
    capacity = max(
        1, min(shard_blocks, (group_heads * picks * 8 + 5 * seq_count - 1) // (5 * seq_count))
    )
    rows, columns = queries.shape
    me = lax.axis_index("seq")
    if picks == 1 and seq_count == 16 and shard_blocks * group_heads <= 256:
        return fused(key_states, value_states, queries, cluster_perm, block_mask, capacity)
    vmem = pl.BlockSpec(memory_space=pltpu.VMEM)
    anywhere = pl.BlockSpec(memory_space=pltpu.HBM)
    struct = jax.ShapeDtypeStruct
    bf16, i32 = jnp.bfloat16, jnp.int32

    dma = pltpu.SemaphoreType.DMA
    kv_half = pltpu.VMEM((group_heads, rows, HEAD_DIM), bf16)
    table = struct((group_heads, 128), i32)
    resident = 2 * (4 * seq_count * capacity * BLOCK * HEAD_DIM + rows * columns)
    grant = 67043328 - resident - 256 * 1024
    got, positions, pos_far, near_queries = pl.pallas_call(
        functools.partial(exchange_kernel, seq_count, capacity, shard_blocks, picks),
        out_shape=(
            pltpu.VMEM((2, 2, seq_count, capacity, BLOCK, HEAD_DIM), bf16), table, table,
            pltpu.VMEM((rows, columns), bf16),
        ),
        in_specs=[anywhere, anywhere, anywhere, vmem, vmem],
        out_specs=(vmem, vmem, vmem, vmem),
        scratch_shapes=[
            kv_half, kv_half, kv_half, kv_half,
            pltpu.VMEM((seq_count, 1, 128), i32),
            pltpu.VMEM((seq_count, 1, 128), i32),
            pltpu.SMEM((seq_count, 1, 128), i32),
            pltpu.VMEM((2, seq_count, capacity, BLOCK, HEAD_DIM), bf16),
            pltpu.VMEM((8 * -(-capacity // 8), 128), i32),
            pltpu.VMEM((shard_blocks * group_heads, 1, BLOCK), i32),
            dma((2 * group_heads,)), dma((2 * group_heads,)), dma((2 * group_heads,)),
            dma((seq_count,)), dma((seq_count,)), dma((7,)),
        ] + [dma((2, seq_count)) for _ in range(4)],
        compiler_params=pltpu.CompilerParams(
            collective_id=0, has_side_effects=True, vmem_limit_bytes=grant
        ),
        name="exchange",
    )(key_states, value_states, queries, cluster_perm, block_mask)

    masked = picks > 1
    total_heads = columns // HEAD_DIM
    width = 8 if total_heads % 8 == 0 else 1
    operands = [near_queries, got]
    if masked:
        operands.append(token_allow(cluster_perm, block_mask, picks, me, shard_rows))
    smem = pl.BlockSpec(memory_space=pltpu.SMEM)
    return pl.pallas_call(
        functools.partial(attend_kernel, group_heads, picks, width, capacity, masked),
        out_shape=struct((rows, columns), bf16),
        in_specs=[smem, smem] + [vmem] * len(operands),
        out_specs=anywhere,
        scratch_shapes=[pltpu.VMEM((2, rows, width * HEAD_DIM), bf16), dma((2,))],
        compiler_params=pltpu.CompilerParams(vmem_limit_bytes=24 * 1024 * 1024),
        name="attend",
    )(positions, pos_far, *operands)


def solution(mesh):
    rows = P(("seq", "head"), None)
    placed = (rows, rows, rows, P("head", "seq"), P("head", "seq", None))
    return jax.shard_map(shards, mesh=mesh, in_specs=placed, out_specs=rows, check_vma=False)
```

```python
import functools
import math

import jax
import jax.numpy as jnp
from jax import lax
from jax.experimental import pallas as pl
from jax.experimental.pallas import tpu as pltpu
from jax.sharding import PartitionSpec as P

HEAD_DIM = 128
BLOCK = 128
MESH = pl.DeviceIdType.MESH
HIGHEST = lax.Precision.HIGHEST


def iota(shape, dim):
    return lax.broadcasted_iota(jnp.int32, shape, dim)


def partner_of(me, step, count):
    if count & (count - 1):
        raise ValueError("seq size")
    peer = 0
    bit = 1
    while bit < count:
        peer = peer + bit * (((me // bit) + (step // bit)) % 2)
        bit *= 2
    return peer


def route(shard_blocks, capacity, picks, mask_ref, req_ref, pos_ref):
    heads, _, blocks = mask_ref.shape
    seq_count = blocks // shard_blocks
    needed = jnp.max(mask_ref[...], axis=1).astype(jnp.float32)
    row, col = iota((blocks, blocks), 0), iota((blocks, blocks), 1)
    same = (row // shard_blocks) == (col // shard_blocks)
    dot = functools.partial(jnp.dot, precision=HIGHEST, preferred_element_type=jnp.float32)
    ones = lambda flag: flag.astype(jnp.float32)
    by_owner = dot(needed, ones(same))
    before_in_owner = dot(needed, ones(same & (row < col)))
    before_all = dot(needed, ones(row < col))
    lower = ones(iota((heads, heads), 1) < iota((heads, heads), 0))
    rank = dot(lower, by_owner) + before_in_owner
    head_ids, block_ids = iota((heads, blocks), 0), iota((heads, blocks), 1)
    pair = (block_ids % shard_blocks * heads + head_ids).astype(jnp.float32)
    slot_row = iota((128, blocks), 0)
    sums = jnp.zeros((128, blocks), jnp.float32)
    for c in range(capacity):
        hit = jnp.where((rank == c) & (needed > 0.5), pair, 0.0)
        sums = jnp.where(slot_row == 2 * c, jnp.sum(hit, axis=0, keepdims=True), sums)
        hit = jnp.where((rank == c) & (needed > 0.5), head_ids.astype(jnp.float32), 0.0)
        sums = jnp.where(slot_row == 2 * c + 1, jnp.sum(hit, axis=0, keepdims=True), sums)
    owner_t = ones(iota((seq_count, blocks), 1) // shard_blocks == iota((seq_count, blocks), 0))
    asked = lax.dot_general(
        owner_t, sums, (((1,), (1,)), ((), ())), precision=HIGHEST,
        preferred_element_type=jnp.float32,
    )
    req_ref[...] = (asked + 0.5).astype(jnp.int32)[:, None, :]
    position = (block_ids // shard_blocks * capacity).astype(jnp.float32) + rank
    lane = iota((heads, 128), 1)
    table = jnp.zeros((heads, 128), jnp.float32)
    for p in range(picks):
        here = jnp.where((before_all == p) & (needed > 0.5), position, 0.0)
        table = jnp.where(lane == p, jnp.sum(here, axis=1, keepdims=True), table)
    pos_ref[...] = (table + 0.5).astype(jnp.int32)


def order(i, me, count):
    top, next_bit = (me // (count // 2)) % 2, (me // (count // 4)) % 2
    end = (top + next_bit + 1) % 2
    return end * (1 + (i + count // 4 - 1) % (count - 1)) + (1 - end) * (count - 1 - i)


def exchange_kernel(
    seq_count, capacity, shard_blocks, picks,
    key_ref, value_ref, query_ref, perm_ref, mask_ref, got_ref, pos_ref, pos_out, query_out,
    near_key, near_value, far_key, far_value, req_ref, asked_ref, asked, send_ref, rows_ref, blocks_ref,
    load_sem, swap_send, swap_recv, req_send, req_recv, misc_sem,
    sends, recvs, relay_send, relay_recv,
):
    group, me = lax.axis_index("head"), lax.axis_index("seq")
    other = 1 - group
    near_kv, far_kv = (near_key, near_value), (far_key, far_value)
    heads, rows = near_key.shape[:2]
    barrier = pltpu.get_barrier_semaphore()
    pl.semaphore_signal(barrier, inc=1, device_id={"head": other}, device_id_type=MESH)

    def greet(step, carry):
        pl.semaphore_signal(
            barrier, inc=1, device_id={"seq": partner_of(me, step, seq_count)}, device_id_type=MESH
        )
        return carry

    lax.fori_loop(1, seq_count, greet, 0)
    loads = []
    for number, src in enumerate((key_ref, value_ref)):
        for head in range(heads):
            start_at = pl.multiple_of((group * heads + head) * HEAD_DIM, HEAD_DIM)
            loads.append(
                pltpu.make_async_copy(
                    src.at[:, pl.ds(start_at, HEAD_DIM)], near_kv[number].at[head],
                    load_sem.at[number * heads + head],
                )
            )
    for copy in loads:
        copy.start()
    pl.semaphore_wait(barrier, seq_count)

    swaps = []
    for number, src in enumerate((key_ref, value_ref)):
        for head in range(heads):
            start_at = pl.multiple_of((other * heads + head) * HEAD_DIM, HEAD_DIM)
            at = number * heads + head
            swaps.append(
                pltpu.make_async_remote_copy(
                    src_ref=src.at[:, pl.ds(start_at, HEAD_DIM)], dst_ref=far_kv[number].at[head],
                    send_sem=swap_send.at[at], recv_sem=swap_recv.at[at],
                    device_id={"head": other}, device_id_type=MESH,
                )
            )
    for copy in swaps:
        copy.start()
    route(shard_blocks, capacity, picks, mask_ref, req_ref, pos_ref)
    for b in range(shard_blocks):
        blocks_ref[b * heads : (b + 1) * heads] = perm_ref[:, b * BLOCK : (b + 1) * BLOCK][:, None, :]
    rows_ref[...] = jnp.zeros_like(rows_ref)

    def ask(step, landing):
        peer = partner_of(me, step, seq_count)
        return pltpu.make_async_remote_copy(
            src_ref=req_ref.at[peer], dst_ref=asked_ref.at[peer if landing else me],
            send_sem=req_send.at[step], recv_sem=req_recv.at[step],
            device_id={"seq": peer}, device_id_type=MESH,
        )

    def start_ask(step, carry):
        ask(step, False).start()
        return carry

    lax.fori_loop(1, seq_count, start_ask, 0)
    tell = pltpu.make_async_remote_copy(
        src_ref=pos_ref, dst_ref=pos_out, send_sem=misc_sem.at[0], recv_sem=misc_sem.at[1],
        device_id={"head": other}, device_id_type=MESH,
    )
    tell.start()
    stay = pltpu.make_async_copy(query_ref, query_out, misc_sem.at[6])
    stay.start()
    keep = pltpu.make_async_copy(req_ref.at[me], asked_ref.at[me], misc_sem.at[2])
    keep.start()
    keep.wait()

    def finish_ask(step, carry):
        ask(step, True).wait()
        return carry

    lax.fori_loop(1, seq_count, finish_ask, 0)
    to_scalar = pltpu.make_async_copy(asked_ref, asked, misc_sem.at[3])
    to_scalar.start()
    to_scalar.wait()
    base = me * (2 * rows)
    token = iota((BLOCK, rows), 1)
    near = token + (base + group * rows)
    far = token + (base + other * rows)

    def gather(which, peer):
        chosen = []
        for c in range(capacity):
            pair = jnp.clip(asked[peer, 0, 2 * c], 0, heads * shard_blocks - 1)
            rows_ref[c : c + 1, :] = blocks_ref[pair]
            chosen.append(jnp.clip(asked[peer, 0, 2 * c + 1], 0, heads - 1))
        turned = rows_ref[...].T
        for c, head in enumerate(chosen):
            column = turned[:, c : c + 1]
            near_table = (column == near).astype(jnp.float32).astype(jnp.bfloat16)
            far_table = (column == far).astype(jnp.float32).astype(jnp.bfloat16)
            got = jnp.dot(near_table, near_kv[which][head], preferred_element_type=jnp.float32)
            got += jnp.dot(far_table, far_kv[which][head], preferred_element_type=jnp.float32)
            send_ref[which, peer, c] = got.astype(jnp.bfloat16)

    def deliver(which, step, landing):
        peer = partner_of(me, step, seq_count)
        return pltpu.make_async_remote_copy(
            src_ref=send_ref.at[which, peer],
            dst_ref=got_ref.at[0, which, peer if landing else me],
            send_sem=sends.at[which, step], recv_sem=recvs.at[which, step],
            device_id={"seq": peer}, device_id_type=MESH,
        )

    def relay(which, step):
        peer = partner_of(me, step, seq_count)
        return pltpu.make_async_remote_copy(
            src_ref=got_ref.at[0, which, peer], dst_ref=got_ref.at[1, which, peer],
            send_sem=relay_send.at[which, step], recv_sem=relay_recv.at[which, step],
            device_id={"head": other}, device_id_type=MESH,
        )

    for which in range(2):
        for copy in loads[which * heads : (which + 1) * heads]:
            copy.wait()
        for copy in swaps[which * heads : (which + 1) * heads]:
            copy.wait()
        gather(which, partner_of(me, order(0, me, seq_count), seq_count))

        def produce(i, carry, which=which):
            gather(which, partner_of(me, order(i, me, seq_count), seq_count))
            deliver(which, order(i - 1, me, seq_count), False).start()
            return carry

        lax.fori_loop(1, seq_count - 1, produce, 0)
        gather(which, me)
        deliver(which, order(seq_count - 2, me, seq_count), False).start()

    locals_ = []
    for which in range(2):
        mine = pltpu.make_async_copy(
            send_ref.at[which, me], got_ref.at[0, which, me], misc_sem.at[4 + which]
        )
        share = pltpu.make_async_remote_copy(
            src_ref=send_ref.at[which, me], dst_ref=got_ref.at[1, which, me],
            send_sem=relay_send.at[which, 0], recv_sem=relay_recv.at[which, 0],
            device_id={"head": other}, device_id_type=MESH,
        )
        mine.start()
        share.start()
        locals_.extend((mine, share))

    for which in range(2):

        def pass_on(i, carry, which=which):
            step = order(i, me, seq_count)
            deliver(which, step, True).wait_recv()
            relay(which, step).start()
            return carry

        lax.fori_loop(0, seq_count - 1, pass_on, 0)

    def finish(step, carry):
        for which in range(2):
            deliver(which, step, True).wait_send()
            relay(which, step).wait()
        return carry

    lax.fori_loop(1, seq_count, finish, 0)
    for copy in locals_:
        copy.wait()
    tell.wait()
    stay.wait()


def request(shard_blocks, capacity, mask_ref, tab_ref):
    heads, _, blocks = mask_ref.shape
    seq_count = blocks // shard_blocks
    needed = jnp.max(mask_ref[...], axis=1).astype(jnp.float32)
    row, col = iota((blocks, blocks), 0), iota((blocks, blocks), 1)
    same = (row // shard_blocks) == (col // shard_blocks)
    small = lambda value: value.astype(jnp.float32).astype(jnp.bfloat16)
    dot = functools.partial(jnp.dot, preferred_element_type=jnp.float32)
    by_owner = dot(small(needed), small(same))
    lower = small(iota((heads, heads), 1) < iota((heads, heads), 0))
    rank = dot(lower, small(by_owner)) + dot(small(needed), small(same & (row < col)))
    head_ids, block_ids = iota((heads, blocks), 0), iota((heads, blocks), 1)
    pair = (block_ids % shard_blocks * heads + head_ids).astype(jnp.float32)
    slot_row = iota((128, blocks), 0)
    sums = jnp.zeros((128, blocks), jnp.float32)
    for c in range(capacity):
        taken = (rank == c) & (needed > 0.5)
        for lane, value in ((2 * c, pair), (2 * c + 1, head_ids.astype(jnp.float32))):
            hit = jnp.sum(jnp.where(taken, value, 0.0), axis=0, keepdims=True)
            sums = jnp.where(slot_row == lane, hit, sums)
    owner_t = small(iota((seq_count, blocks), 1) // shard_blocks == iota((seq_count, blocks), 0))
    asked = lax.dot_general(
        owner_t, small(sums), (((1,), (1,)), ((), ())), preferred_element_type=jnp.float32
    )
    tab_ref[:seq_count] = (asked + 0.5).astype(jnp.int32)[:, None, :]
    spot = (block_ids // shard_blocks * capacity).astype(jnp.float32) + rank
    spot = jnp.sum(jnp.where(needed > 0.5, spot, 0.0), axis=1, keepdims=True)
    spot = (jnp.broadcast_to(spot, (heads, 128)) + 0.5).astype(jnp.int32)
    tab_ref[seq_count:] = spot[:, None, :]


def fused_kernel(
    seq_count, capacity, shard_blocks,
    key_ref, value_ref, query_hbm, perm_hbm, mask_hbm, stage_ref, tab_ref, far_tab_ref,
    perm_ref, mask_ref, keys, values, query_ref, send_ref, got_ref, asked_ref, rows_ref, blocks_ref,
    own_tab, far_tab, asked_near, asked,
    near_sem, load_sem, swap_send, swap_recv, ask_send, ask_recv, misc_sem,
    send_sem, recvs, relay_send, relay_recv, step_sem,
):
    group, me = lax.axis_index("head"), lax.axis_index("seq")
    other = 1 - group
    heads = perm_ref.shape[0]
    rows = query_hbm.shape[0]
    half = heads * HEAD_DIM
    spread = seq_count // 4
    peer_of = lambda step: partner_of(me, step, seq_count)
    top, low = (me // (2 * spread)) % 2, (me // spread) % 2
    edge = (top + low + 1) % 2

    def near_peer(i):
        far = (3 - i) // 2
        turn = edge * ((i + 1) // 2) + (1 - edge) * ((i + 1) % 2)
        return peer_of(spread * (2 * far + turn))

    def side_peer(plane, k):
        return peer_of(spread * plane + 1 + k)

    def turn_of(k):
        return 3 + k * (2 - 3) + k * (k - 1) // 2 * (1 - 2 * 2 + 3) - 1

    def far_peer(k):
        return side_peer(2 + (edge + (1 - top) * (1 - group) + k) % 2, turn_of(k // 2))

    def times(count, body):
        lax.fori_loop(0, count, lambda i, carry: (body(i), carry)[1], 0)

    beside = spread - 1

    def all_rest(body):
        times(beside, lambda k: body(side_peer(0, k)))
        times(beside, lambda k: body(side_peer(1, k)))
        times(2 * beside, lambda k: body(far_peer(k)))

    barrier = pltpu.get_barrier_semaphore()
    pl.semaphore_signal(barrier, inc=1, device_id={"head": other}, device_id_type=MESH)
    for step in (spread, 2 * spread, 3 * spread, 1, 2):
        pl.semaphore_signal(barrier, inc=1, device_id={"seq": peer_of(step)}, device_id_type=MESH)

    masks = pltpu.make_async_copy(mask_hbm, mask_ref, misc_sem.at[0])
    masks.start()
    perms = pltpu.make_async_copy(perm_hbm, perm_ref, misc_sem.at[1])
    perms.start()
    here = pl.ds(pl.multiple_of(group * rows, rows), rows)
    sides = ((key_ref, keys), (value_ref, values))

    def load(number, start_at, span):
        src, dst = sides[number]
        mine = pl.ds(pl.multiple_of(group * half + start_at, HEAD_DIM), span)
        return pltpu.make_async_copy(
            src.at[:, mine], dst.at[here, pl.ds(start_at, span)], load_sem.at[number]
        )

    def swap(number, start_at, span):
        src, dst = sides[number]
        theirs = pl.ds(pl.multiple_of(other * half + start_at, HEAD_DIM), span)
        return pltpu.make_async_remote_copy(
            src_ref=src.at[:, theirs], dst_ref=dst.at[here, pl.ds(start_at, span)],
            send_sem=swap_send.at[number], recv_sem=swap_recv.at[number],
            device_id={"head": other}, device_id_type=MESH,
        )

    parts = 4
    cuts = [(number, part * (half // parts), half // parts) for number in range(2) for part in range(parts)]
    for cut in cuts[:parts]:
        load(*cut).start()
    take = pltpu.make_async_copy(query_hbm, query_ref, misc_sem.at[2])
    masks.wait()
    request(shard_blocks, capacity, mask_ref, tab_ref)
    pl.semaphore_wait(barrier, 6)

    def ask(peer, landing, near):
        return pltpu.make_async_remote_copy(
            src_ref=tab_ref.at[peer], dst_ref=asked_ref.at[peer if landing else me],
            send_sem=ask_send.at[0],
            recv_sem=ask_recv.at[near * (1 + (peer if landing else me) // spread)],
            device_id={"seq": peer}, device_id_type=MESH,
        )

    def asks(count):
        return pltpu.make_async_remote_copy(
            src_ref=tab_ref.at[pl.ds(0, count)], dst_ref=asked_ref.at[pl.ds(0, count)],
            send_sem=ask_send.at[0], recv_sem=ask_recv.at[0],
            device_id={"head": other}, device_id_type=MESH,
        )

    times(3, lambda i: ask(near_peer(i), False, 1).start())
    for cut in cuts:
        swap(*cut).start()
    for cut in cuts[parts:]:
        load(*cut).start()
    for number, step in enumerate((1, 2)):
        pl.semaphore_signal(
            step_sem.at[number], inc=1, device_id={"seq": peer_of(step)}, device_id_type=MESH
        )
    tell = pltpu.make_async_remote_copy(
        src_ref=tab_ref, dst_ref=far_tab_ref, send_sem=misc_sem.at[3], recv_sem=misc_sem.at[4],
        device_id={"head": other}, device_id_type=MESH,
    )
    tell.start()
    keep = pltpu.make_async_copy(tab_ref.at[me], asked_ref.at[me], misc_sem.at[5])
    keep.start()
    own = pltpu.make_async_copy(tab_ref, own_tab, misc_sem.at[6])
    own.start()
    perms.wait()
    for b in range(shard_blocks):
        blocks_ref[b * heads : (b + 1) * heads] = perm_ref[:, b * BLOCK : (b + 1) * BLOCK][:, None, :]
    rows_ref[...] = jnp.zeros_like(rows_ref)

    def near_scalar(peer):
        return pltpu.make_async_copy(
            asked_ref.at[peer], asked_near.at[peer], near_sem.at[peer // spread]
        )

    pl.semaphore_wait(step_sem.at[0], 1)
    pl.semaphore_wait(step_sem.at[1], 1)
    pl.semaphore_signal(step_sem.at[2], inc=1, device_id={"seq": peer_of(2)}, device_id_type=MESH)

    token = iota((BLOCK, 2 * rows), 1) + me * (2 * rows)

    def gather(table_ref, peer, whiches, put):
        chosen = []
        for c in range(capacity):
            pair = jnp.clip(table_ref[peer, 0, 2 * c], 0, heads * shard_blocks - 1)
            rows_ref[c : c + 1, :] = blocks_ref[pair]
            head = jnp.clip(table_ref[peer, 0, 2 * c + 1], 0, heads - 1)
            chosen.append(head * HEAD_DIM)
        turned = rows_ref[...].T
        for c, start_at in enumerate(chosen):
            table = (turned[:, c : c + 1] == token).astype(jnp.float32).astype(jnp.bfloat16)
            for which in whiches:
                got = jnp.dot(
                    table, sides[which][1][:, pl.ds(start_at, HEAD_DIM)],
                    preferred_element_type=jnp.float32,
                )
                put(which, c, got.astype(jnp.bfloat16))

    def to_send(peer):
        def put(which, c, got):
            send_ref[peer, which, c] = got

        return put

    def near_deliver(which, peer):
        return pltpu.make_async_remote_copy(
            src_ref=send_ref.at[peer, which], dst_ref=got_ref.at[0, me, which],
            send_sem=send_sem.at[0], recv_sem=recvs.at[me],
            device_id={"seq": peer}, device_id_type=MESH,
        )

    def deliver(peer, landing):
        source = peer if landing else me
        return pltpu.make_async_remote_copy(
            src_ref=send_ref.at[peer], dst_ref=got_ref.at[0, source],
            send_sem=send_sem.at[0], recv_sem=recvs.at[source],
            device_id={"seq": peer}, device_id_type=MESH,
        )

    def relay(source):
        return pltpu.make_async_remote_copy(
            src_ref=got_ref.at[0, source], dst_ref=got_ref.at[1, source],
            send_sem=relay_send.at[0], recv_sem=relay_recv.at[source],
            device_id={"head": other}, device_id_type=MESH,
        )

    def serve(i, which):
        peer = near_peer(i)
        if which == 0:
            near_scalar(peer).wait()
        gather(asked_near, peer, (which,), to_send(peer))
        near_deliver(which, peer).start()

    def heed(i):
        peer = near_peer(i)
        ask(peer, True, 1).wait_recv()
        near_scalar(peer).start()

    load(0, 0, half).wait()
    heed(0)
    pl.semaphore_wait(step_sem.at[2], 1)
    all_rest(lambda peer: ask(peer, False, 0).start())
    heed(1)
    swap(0, 0, half).wait_recv()
    serve(0, 0)
    serve(1, 0)
    heed(2)
    serve(2, 0)
    load(1, 0, half).wait()
    swap(1, 0, half).wait_recv()
    times(3, lambda i: serve(i, 1))
    take.start()
    own.wait()
    tell.wait_recv()
    far_scalar = pltpu.make_async_copy(far_tab_ref, far_tab, misc_sem.at[8])
    far_scalar.start()

    def to_got(which, c, got):
        got_ref[0, me, which, c] = got

    gather(own_tab, me, (0, 1), to_got)
    relay(me).start()
    keep.wait()
    asks(seq_count - 4).wait_recv()
    to_scalar = pltpu.make_async_copy(asked_ref, asked, misc_sem.at[7])
    to_scalar.start()
    to_scalar.wait()

    def produce(i):
        far = edge * ((i + 2 * beside) // (3 * beside)) + (1 - edge) * ((5 * beside - 1 - i) // (3 * beside))
        at = i - beside * edge + 3 * beside * (1 - far)
        peer = far * far_peer(at % (3 * beside)) + (1 - far) * side_peer(1, at % beside)
        gather(asked, peer, (0, 1), to_send(peer))
        deliver(peer, False).start()

    def produce_beside(k):
        peer = side_peer(0, k)
        gather(asked, peer, (0, 1), to_send(peer))
        deliver(peer, False).start()

    times(beside, produce_beside)
    times(3 * beside, produce)
    far_scalar.wait()
    take.wait()

    scale = math.log2(math.e) / math.sqrt(HEAD_DIM)
    ones = jnp.ones((BLOCK, HEAD_DIM), jnp.bfloat16)

    def attend(items):
        scores = []
        for rel, source, c in items:
            tab, base = ((own_tab, group), (far_tab, other))[rel]
            head = base * heads + jnp.clip(tab[source, 0, 2 * c + 1], 0, heads - 1)
            query = query_ref[:, pl.ds(head * HEAD_DIM, HEAD_DIM)]
            scores.append(
                lax.dot_general(
                    query, got_ref[rel, source, 0, c], (((1,), (1,)), ((), ())),
                    preferred_element_type=jnp.float32,
                )
            )
        weights = []
        for score in scores:
            peak = jnp.max(score, axis=1, keepdims=True)
            weights.append(jnp.exp2((score - peak) * scale).astype(jnp.bfloat16))
        for (rel, source, c), weight in zip(items, weights):
            mixed = jnp.dot(
                weight, jnp.concatenate([got_ref[rel, source, 1, c], ones], axis=1),
                preferred_element_type=jnp.float32,
            )
            stage_ref[rel, source * capacity + c] = (
                mixed[:, :HEAD_DIM] / mixed[:, HEAD_DIM:]
            ).astype(jnp.bfloat16)

    slots = lambda rel, source: [(rel, source, c) for c in range(capacity)]
    attend(slots(0, me))
    relay(me).wait_recv()
    attend(slots(1, me))

    def near_take(i):
        source = near_peer(i)
        deliver(source, True).wait_recv()
        relay(source).start()

    times(3, near_take)

    def near_use(i):
        source = near_peer(i)
        relay(source).wait_recv()
        attend(slots(0, source) + slots(1, source))

    times(3, near_use)

    def rest_peer(i):
        late = i // (2 * beside)
        plane = (1 - late) * (i // beside) + late * (2 + i % 2)
        return side_peer(plane, (1 - late) * (i % beside) + late * turn_of(i % (2 * beside) // 2))

    def use(i, first=False, last=False):
        before = [] if first else [rest_peer(2 * i - 2), rest_peer(2 * i - 1)]
        sources = [] if last else [rest_peer(2 * i), rest_peer(2 * i + 1)]
        for source in sources:
            deliver(source, True).wait_recv()
            relay(source).start()
        for source in before:
            relay(source).wait_recv()
        items = [slots(0, source) for source in sources] + [slots(1, source) for source in before]
        attend(sum(items, []))

    pairs = 2 * beside
    use(0, first=True)
    times(pairs - 1, lambda i: use(i + 1))
    use(pairs, last=True)

    for number in range(2):
        swap(number, 0, half).wait_send()
    asks(seq_count - 1).wait_send()
    tell.wait_send()
    pltpu.make_async_remote_copy(
        src_ref=send_ref.at[pl.ds(0, seq_count - 1)], dst_ref=got_ref.at[0, pl.ds(0, seq_count - 1)],
        send_sem=send_sem.at[0], recv_sem=recvs.at[me],
        device_id={"head": other}, device_id_type=MESH,
    ).wait_send()
    pltpu.make_async_remote_copy(
        src_ref=got_ref.at[0], dst_ref=got_ref.at[1],
        send_sem=relay_send.at[0], recv_sem=relay_recv.at[me],
        device_id={"head": other}, device_id_type=MESH,
    ).wait_send()


def flush_kernel(seq_count, stage_ref, tab_ref, far_tab_ref, out_ref, sem):
    group = lax.axis_index("head")
    heads = tab_ref.shape[0] - seq_count
    last = stage_ref.shape[1] - 1
    for local in range(heads):
        for rel, (tab, base) in enumerate(((tab_ref, group), (far_tab_ref, 1 - group))):
            slot = jnp.clip(tab[seq_count + local, 0, 0], 0, last)
            at = pl.multiple_of((base * heads + local) * HEAD_DIM, HEAD_DIM)
            pltpu.make_async_copy(
                stage_ref.at[rel, slot], out_ref.at[:, pl.ds(at, HEAD_DIM)], sem.at[0]
            ).start()
    pltpu.make_async_copy(out_ref, out_ref, sem.at[0]).wait()


def fused(key_states, value_states, queries, cluster_perm, block_mask, capacity):
    heads, shard_rows = cluster_perm.shape
    shard_blocks = shard_rows // BLOCK
    seq_count = lax.axis_size("seq")
    rows, columns = queries.shape
    vmem = pl.BlockSpec(memory_space=pltpu.VMEM)
    anywhere = pl.BlockSpec(memory_space=pltpu.HBM)
    bf16, i32 = jnp.bfloat16, jnp.int32
    dma = pltpu.SemaphoreType.DMA
    resident = 4 * seq_count * capacity * rows * HEAD_DIM + 8 * 8 * 128 * (seq_count + heads)
    table, asks = (seq_count + heads, 1, 128), (seq_count, 1, 128)
    staged = pl.pallas_call(
        functools.partial(fused_kernel, seq_count, capacity, shard_blocks),
        out_shape=(
            pltpu.VMEM((2, seq_count * capacity, rows, HEAD_DIM), bf16),
            pltpu.VMEM(table, i32), pltpu.VMEM(table, i32),
        ),
        in_specs=[anywhere] * 5,
        out_specs=(vmem, vmem, vmem),
        scratch_shapes=[
            pltpu.VMEM(cluster_perm.shape, i32), pltpu.VMEM(block_mask.shape, i32),
            pltpu.VMEM((shard_rows, heads * HEAD_DIM), bf16),
            pltpu.VMEM((shard_rows, heads * HEAD_DIM), bf16),
            pltpu.VMEM((rows, columns), bf16),
            pltpu.VMEM((seq_count, 2, capacity, BLOCK, HEAD_DIM), bf16),
            pltpu.VMEM((2, seq_count, 2, capacity, BLOCK, HEAD_DIM), bf16),
            pltpu.VMEM(asks, i32),
            pltpu.VMEM((8 * -(-capacity // 8), 128), i32),
            pltpu.VMEM((shard_blocks * heads, 1, BLOCK), i32),
            pltpu.SMEM(table, i32), pltpu.SMEM(table, i32),
            pltpu.SMEM(asks, i32), pltpu.SMEM(asks, i32),
            dma((4,)), dma((2,)), dma((2,)), dma((2,)), dma((1,)), dma((5,)), dma((9,)),
            dma((1,)), dma((seq_count,)), dma((1,)), dma((seq_count,)),
            pltpu.SemaphoreType.REGULAR((3,)),
        ],
        compiler_params=pltpu.CompilerParams(
            collective_id=1, has_side_effects=True,
            vmem_limit_bytes=67043328 - resident - 256 * 1024,
        ),
        name="fused",
    )(key_states, value_states, queries, cluster_perm, block_mask)
    return pl.pallas_call(
        functools.partial(flush_kernel, seq_count),
        out_shape=jax.ShapeDtypeStruct((rows, columns), bf16),
        in_specs=[vmem, vmem, vmem],
        out_specs=anywhere,
        scratch_shapes=[dma((1,))],
        compiler_params=pltpu.CompilerParams(vmem_limit_bytes=8 * 1024 * 1024),
        name="flush",
    )(*staged)


def attend_kernel(heads, picks, width, capacity, masked, pos_own, pos_far, *refs):
    if masked:
        query_ref, kv_ref, allow_ref, out_ref, stage, sems = refs
    else:
        query_ref, kv_ref, out_ref, stage, sems = refs
    group = lax.axis_index("head")
    scale = math.log2(math.e) / math.sqrt(HEAD_DIM)
    ones = jnp.ones((BLOCK, HEAD_DIM), jnp.bfloat16)
    span = width * HEAD_DIM
    batches = query_ref.shape[1] // span

    def put(batch, buffer):
        return pltpu.make_async_copy(
            stage.at[buffer],
            out_ref.at[:, pl.ds(pl.multiple_of(batch * span, span), span)],
            sems.at[buffer],
        )

    def one(batch, carry):
        where_, scores = [], []
        for w in range(width):
            head = batch * width + w
            away = (head // heads) != group
            local = head % heads
            query = query_ref[:, pl.ds(pl.multiple_of(head * HEAD_DIM, HEAD_DIM), HEAD_DIM)]
            for p in range(picks):
                slot = jnp.where(away, pos_far[local, p], pos_own[local, p])
                spot = (slot // capacity, slot % capacity)
                rel = away.astype(jnp.int32)
                where_.append((rel, spot))
                score = lax.dot_general(
                    query, kv_ref[rel, 0, spot[0], spot[1]], (((1,), (1,)), ((), ())),
                    preferred_element_type=jnp.float32,
                )
                if masked:
                    score = jnp.where(allow_ref[head, :, p : p + 1] > 0, score, -jnp.inf)
                scores.append(score)
        weights = []
        for w in range(width):
            own = scores[w * picks : (w + 1) * picks]
            top = jnp.max(functools.reduce(jnp.maximum, own), axis=1, keepdims=True)
            weights.extend([jnp.exp2((s - top) * scale).astype(jnp.bfloat16) for s in own])
        buffer = batch % 2

        @pl.when(batch >= 2)
        def _():
            put(batch - 2, buffer).wait()

        for w in range(width):
            parts = []
            for p in range(picks):
                rel, spot = where_[w * picks + p]
                parts.append(
                    jnp.dot(
                        weights[w * picks + p],
                        jnp.concatenate([kv_ref[rel, 1, spot[0], spot[1]], ones], axis=1),
                        preferred_element_type=jnp.float32,
                    )
                )
            mixed = functools.reduce(jnp.add, parts)
            stage[buffer, :, w * HEAD_DIM : (w + 1) * HEAD_DIM] = (
                mixed[:, :HEAD_DIM] / mixed[:, HEAD_DIM:]
            ).astype(jnp.bfloat16)
        put(batch, buffer).start()
        return carry

    lax.fori_loop(0, batches, one, 0)
    for batch in range(max(0, batches - 2), batches):
        put(batch, batch % 2).wait()


def token_allow(cluster_perm, block_mask, picks, me, shard_rows):
    needed = jnp.max(block_mask, axis=1)
    prefix = jnp.cumsum(needed, axis=1) - needed
    chosen = (needed[:, :, None] == 1) & (prefix[:, :, None] == jnp.arange(picks)[None, None, :])
    live = jnp.einsum(
        "hqb,hbp->hqp", block_mask.astype(jnp.float32), chosen.astype(jnp.float32)
    )
    group_heads = cluster_perm.shape[0]
    local = cluster_perm - me * shard_rows
    place = jnp.zeros((group_heads, shard_rows), jnp.int32)
    place = place.at[jnp.arange(group_heads)[:, None], local].set(
        jnp.broadcast_to(jnp.arange(shard_rows, dtype=jnp.int32) // BLOCK, local.shape)
    )
    by_token = jnp.take_along_axis(live, place[:, :, None], axis=1).astype(jnp.float32)
    return lax.all_to_all(by_token, "head", split_axis=1, concat_axis=0, tiled=True)


def shards(queries, key_states, value_states, cluster_perm, block_mask):
    group_heads, shard_rows = cluster_perm.shape
    shard_blocks = shard_rows // BLOCK
    seq_count = lax.axis_size("seq")
    block_total = block_mask.shape[2]
    picks = max(1, block_total // 64)
    capacity = max(
        1, min(shard_blocks, (group_heads * picks * 8 + 5 * seq_count - 1) // (5 * seq_count))
    )
    rows, columns = queries.shape
    me = lax.axis_index("seq")
    if picks == 1 and seq_count == 16 and shard_blocks * group_heads <= 256:
        return fused(key_states, value_states, queries, cluster_perm, block_mask, capacity)
    vmem = pl.BlockSpec(memory_space=pltpu.VMEM)
    anywhere = pl.BlockSpec(memory_space=pltpu.HBM)
    struct = jax.ShapeDtypeStruct
    bf16, i32 = jnp.bfloat16, jnp.int32

    dma = pltpu.SemaphoreType.DMA
    kv_half = pltpu.VMEM((group_heads, rows, HEAD_DIM), bf16)
    table = struct((group_heads, 128), i32)
    resident = 2 * (4 * seq_count * capacity * BLOCK * HEAD_DIM + rows * columns)
    grant = 67043328 - resident - 256 * 1024
    got, positions, pos_far, near_queries = pl.pallas_call(
        functools.partial(exchange_kernel, seq_count, capacity, shard_blocks, picks),
        out_shape=(
            pltpu.VMEM((2, 2, seq_count, capacity, BLOCK, HEAD_DIM), bf16), table, table,
            pltpu.VMEM((rows, columns), bf16),
        ),
        in_specs=[anywhere, anywhere, anywhere, vmem, vmem],
        out_specs=(vmem, vmem, vmem, vmem),
        scratch_shapes=[
            kv_half, kv_half, kv_half, kv_half,
            pltpu.VMEM((seq_count, 1, 128), i32),
            pltpu.VMEM((seq_count, 1, 128), i32),
            pltpu.SMEM((seq_count, 1, 128), i32),
            pltpu.VMEM((2, seq_count, capacity, BLOCK, HEAD_DIM), bf16),
            pltpu.VMEM((8 * -(-capacity // 8), 128), i32),
            pltpu.VMEM((shard_blocks * group_heads, 1, BLOCK), i32),
            dma((2 * group_heads,)), dma((2 * group_heads,)), dma((2 * group_heads,)),
            dma((seq_count,)), dma((seq_count,)), dma((7,)),
        ] + [dma((2, seq_count)) for _ in range(4)],
        compiler_params=pltpu.CompilerParams(
            collective_id=0, has_side_effects=True, vmem_limit_bytes=grant
        ),
        name="exchange",
    )(key_states, value_states, queries, cluster_perm, block_mask)

    masked = picks > 1
    total_heads = columns // HEAD_DIM
    width = 8 if total_heads % 8 == 0 else 1
    operands = [near_queries, got]
    if masked:
        operands.append(token_allow(cluster_perm, block_mask, picks, me, shard_rows))
    smem = pl.BlockSpec(memory_space=pltpu.SMEM)
    return pl.pallas_call(
        functools.partial(attend_kernel, group_heads, picks, width, capacity, masked),
        out_shape=struct((rows, columns), bf16),
        in_specs=[smem, smem] + [vmem] * len(operands),
        out_specs=anywhere,
        scratch_shapes=[pltpu.VMEM((2, rows, width * HEAD_DIM), bf16), dma((2,))],
        compiler_params=pltpu.CompilerParams(vmem_limit_bytes=24 * 1024 * 1024),
        name="attend",
    )(positions, pos_far, *operands)


def solution(mesh):
    rows = P(("seq", "head"), None)
    placed = (rows, rows, rows, P("head", "seq"), P("head", "seq", None))
    return jax.shard_map(shards, mesh=mesh, in_specs=placed, out_specs=rows, check_vma=False)
```

```python
import functools
import math

import jax
import jax.numpy as jnp
from jax import lax
from jax.experimental import pallas as pl
from jax.experimental.pallas import tpu as pltpu
from jax.sharding import PartitionSpec as P

HEAD_DIM = 128
BLOCK = 128
MESH = pl.DeviceIdType.MESH
HIGHEST = lax.Precision.HIGHEST


def iota(shape, dim):
    return lax.broadcasted_iota(jnp.int32, shape, dim)


def partner_of(me, step, count):
    if count & (count - 1):
        raise ValueError("seq size")
    peer = 0
    bit = 1
    while bit < count:
        peer = peer + bit * (((me // bit) + (step // bit)) % 2)
        bit *= 2
    return peer


def route(shard_blocks, capacity, picks, mask_ref, req_ref, pos_ref):
    heads, _, blocks = mask_ref.shape
    seq_count = blocks // shard_blocks
    needed = jnp.max(mask_ref[...], axis=1).astype(jnp.float32)
    row, col = iota((blocks, blocks), 0), iota((blocks, blocks), 1)
    same = (row // shard_blocks) == (col // shard_blocks)
    dot = functools.partial(jnp.dot, precision=HIGHEST, preferred_element_type=jnp.float32)
    ones = lambda flag: flag.astype(jnp.float32)
    by_owner = dot(needed, ones(same))
    before_in_owner = dot(needed, ones(same & (row < col)))
    before_all = dot(needed, ones(row < col))
    lower = ones(iota((heads, heads), 1) < iota((heads, heads), 0))
    rank = dot(lower, by_owner) + before_in_owner
    head_ids, block_ids = iota((heads, blocks), 0), iota((heads, blocks), 1)
    pair = (block_ids % shard_blocks * heads + head_ids).astype(jnp.float32)
    slot_row = iota((128, blocks), 0)
    sums = jnp.zeros((128, blocks), jnp.float32)
    for c in range(capacity):
        hit = jnp.where((rank == c) & (needed > 0.5), pair, 0.0)
        sums = jnp.where(slot_row == 2 * c, jnp.sum(hit, axis=0, keepdims=True), sums)
        hit = jnp.where((rank == c) & (needed > 0.5), head_ids.astype(jnp.float32), 0.0)
        sums = jnp.where(slot_row == 2 * c + 1, jnp.sum(hit, axis=0, keepdims=True), sums)
    owner_t = ones(iota((seq_count, blocks), 1) // shard_blocks == iota((seq_count, blocks), 0))
    asked = lax.dot_general(
        owner_t, sums, (((1,), (1,)), ((), ())), precision=HIGHEST,
        preferred_element_type=jnp.float32,
    )
    req_ref[...] = (asked + 0.5).astype(jnp.int32)[:, None, :]
    position = (block_ids // shard_blocks * capacity).astype(jnp.float32) + rank
    lane = iota((heads, 128), 1)
    table = jnp.zeros((heads, 128), jnp.float32)
    for p in range(picks):
        here = jnp.where((before_all == p) & (needed > 0.5), position, 0.0)
        table = jnp.where(lane == p, jnp.sum(here, axis=1, keepdims=True), table)
    pos_ref[...] = (table + 0.5).astype(jnp.int32)


def order(i, me, count):
    top, next_bit = (me // (count // 2)) % 2, (me // (count // 4)) % 2
    end = (top + next_bit + 1) % 2
    return end * (1 + (i + count // 4 - 1) % (count - 1)) + (1 - end) * (count - 1 - i)


def exchange_kernel(
    seq_count, capacity, shard_blocks, picks,
    key_ref, value_ref, query_ref, perm_ref, mask_ref, got_ref, pos_ref, pos_out, query_out,
    near_key, near_value, far_key, far_value, req_ref, asked_ref, asked, send_ref, rows_ref, blocks_ref,
    load_sem, swap_send, swap_recv, req_send, req_recv, misc_sem,
    sends, recvs, relay_send, relay_recv,
):
    group, me = lax.axis_index("head"), lax.axis_index("seq")
    other = 1 - group
    near_kv, far_kv = (near_key, near_value), (far_key, far_value)
    heads, rows = near_key.shape[:2]
    barrier = pltpu.get_barrier_semaphore()
    pl.semaphore_signal(barrier, inc=1, device_id={"head": other}, device_id_type=MESH)

    def greet(step, carry):
        pl.semaphore_signal(
            barrier, inc=1, device_id={"seq": partner_of(me, step, seq_count)}, device_id_type=MESH
        )
        return carry

    lax.fori_loop(1, seq_count, greet, 0)
    loads = []
    for number, src in enumerate((key_ref, value_ref)):
        for head in range(heads):
            start_at = pl.multiple_of((group * heads + head) * HEAD_DIM, HEAD_DIM)
            loads.append(
                pltpu.make_async_copy(
                    src.at[:, pl.ds(start_at, HEAD_DIM)], near_kv[number].at[head],
                    load_sem.at[number * heads + head],
                )
            )
    for copy in loads:
        copy.start()
    pl.semaphore_wait(barrier, seq_count)

    swaps = []
    for number, src in enumerate((key_ref, value_ref)):
        for head in range(heads):
            start_at = pl.multiple_of((other * heads + head) * HEAD_DIM, HEAD_DIM)
            at = number * heads + head
            swaps.append(
                pltpu.make_async_remote_copy(
                    src_ref=src.at[:, pl.ds(start_at, HEAD_DIM)], dst_ref=far_kv[number].at[head],
                    send_sem=swap_send.at[at], recv_sem=swap_recv.at[at],
                    device_id={"head": other}, device_id_type=MESH,
                )
            )
    for copy in swaps:
        copy.start()
    route(shard_blocks, capacity, picks, mask_ref, req_ref, pos_ref)
    for b in range(shard_blocks):
        blocks_ref[b * heads : (b + 1) * heads] = perm_ref[:, b * BLOCK : (b + 1) * BLOCK][:, None, :]
    rows_ref[...] = jnp.zeros_like(rows_ref)

    def ask(step, landing):
        peer = partner_of(me, step, seq_count)
        return pltpu.make_async_remote_copy(
            src_ref=req_ref.at[peer], dst_ref=asked_ref.at[peer if landing else me],
            send_sem=req_send.at[step], recv_sem=req_recv.at[step],
            device_id={"seq": peer}, device_id_type=MESH,
        )

    def start_ask(step, carry):
        ask(step, False).start()
        return carry

    lax.fori_loop(1, seq_count, start_ask, 0)
    tell = pltpu.make_async_remote_copy(
        src_ref=pos_ref, dst_ref=pos_out, send_sem=misc_sem.at[0], recv_sem=misc_sem.at[1],
        device_id={"head": other}, device_id_type=MESH,
    )
    tell.start()
    stay = pltpu.make_async_copy(query_ref, query_out, misc_sem.at[6])
    stay.start()
    keep = pltpu.make_async_copy(req_ref.at[me], asked_ref.at[me], misc_sem.at[2])
    keep.start()
    keep.wait()

    def finish_ask(step, carry):
        ask(step, True).wait()
        return carry

    lax.fori_loop(1, seq_count, finish_ask, 0)
    to_scalar = pltpu.make_async_copy(asked_ref, asked, misc_sem.at[3])
    to_scalar.start()
    to_scalar.wait()
    base = me * (2 * rows)
    token = iota((BLOCK, rows), 1)
    near = token + (base + group * rows)
    far = token + (base + other * rows)

    def gather(which, peer):
        chosen = []
        for c in range(capacity):
            pair = jnp.clip(asked[peer, 0, 2 * c], 0, heads * shard_blocks - 1)
            rows_ref[c : c + 1, :] = blocks_ref[pair]
            chosen.append(jnp.clip(asked[peer, 0, 2 * c + 1], 0, heads - 1))
        turned = rows_ref[...].T
        for c, head in enumerate(chosen):
            column = turned[:, c : c + 1]
            near_table = (column == near).astype(jnp.float32).astype(jnp.bfloat16)
            far_table = (column == far).astype(jnp.float32).astype(jnp.bfloat16)
            got = jnp.dot(near_table, near_kv[which][head], preferred_element_type=jnp.float32)
            got += jnp.dot(far_table, far_kv[which][head], preferred_element_type=jnp.float32)
            send_ref[which, peer, c] = got.astype(jnp.bfloat16)

    def deliver(which, step, landing):
        peer = partner_of(me, step, seq_count)
        return pltpu.make_async_remote_copy(
            src_ref=send_ref.at[which, peer],
            dst_ref=got_ref.at[0, which, peer if landing else me],
            send_sem=sends.at[which, step], recv_sem=recvs.at[which, step],
            device_id={"seq": peer}, device_id_type=MESH,
        )

    def relay(which, step):
        peer = partner_of(me, step, seq_count)
        return pltpu.make_async_remote_copy(
            src_ref=got_ref.at[0, which, peer], dst_ref=got_ref.at[1, which, peer],
            send_sem=relay_send.at[which, step], recv_sem=relay_recv.at[which, step],
            device_id={"head": other}, device_id_type=MESH,
        )

    for which in range(2):
        for copy in loads[which * heads : (which + 1) * heads]:
            copy.wait()
        for copy in swaps[which * heads : (which + 1) * heads]:
            copy.wait()
        gather(which, partner_of(me, order(0, me, seq_count), seq_count))

        def produce(i, carry, which=which):
            gather(which, partner_of(me, order(i, me, seq_count), seq_count))
            deliver(which, order(i - 1, me, seq_count), False).start()
            return carry

        lax.fori_loop(1, seq_count - 1, produce, 0)
        gather(which, me)
        deliver(which, order(seq_count - 2, me, seq_count), False).start()

    locals_ = []
    for which in range(2):
        mine = pltpu.make_async_copy(
            send_ref.at[which, me], got_ref.at[0, which, me], misc_sem.at[4 + which]
        )
        share = pltpu.make_async_remote_copy(
            src_ref=send_ref.at[which, me], dst_ref=got_ref.at[1, which, me],
            send_sem=relay_send.at[which, 0], recv_sem=relay_recv.at[which, 0],
            device_id={"head": other}, device_id_type=MESH,
        )
        mine.start()
        share.start()
        locals_.extend((mine, share))

    for which in range(2):

        def pass_on(i, carry, which=which):
            step = order(i, me, seq_count)
            deliver(which, step, True).wait_recv()
            relay(which, step).start()
            return carry

        lax.fori_loop(0, seq_count - 1, pass_on, 0)

    def finish(step, carry):
        for which in range(2):
            deliver(which, step, True).wait_send()
            relay(which, step).wait()
        return carry

    lax.fori_loop(1, seq_count, finish, 0)
    for copy in locals_:
        copy.wait()
    tell.wait()
    stay.wait()


def request(shard_blocks, capacity, mask_ref, tab_ref):
    heads, _, blocks = mask_ref.shape
    seq_count = blocks // shard_blocks
    needed = jnp.max(mask_ref[...], axis=1).astype(jnp.float32)
    row, col = iota((blocks, blocks), 0), iota((blocks, blocks), 1)
    same = (row // shard_blocks) == (col // shard_blocks)
    small = lambda value: value.astype(jnp.float32).astype(jnp.bfloat16)
    dot = functools.partial(jnp.dot, preferred_element_type=jnp.float32)
    by_owner = dot(small(needed), small(same))
    lower = small(iota((heads, heads), 1) < iota((heads, heads), 0))
    rank = dot(lower, small(by_owner)) + dot(small(needed), small(same & (row < col)))
    head_ids, block_ids = iota((heads, blocks), 0), iota((heads, blocks), 1)
    pair = (block_ids % shard_blocks * heads + head_ids).astype(jnp.float32)
    slot_row = iota((128, blocks), 0)
    sums = jnp.zeros((128, blocks), jnp.float32)
    for c in range(capacity):
        taken = (rank == c) & (needed > 0.5)
        for lane, value in ((2 * c, pair), (2 * c + 1, head_ids.astype(jnp.float32))):
            hit = jnp.sum(jnp.where(taken, value, 0.0), axis=0, keepdims=True)
            sums = jnp.where(slot_row == lane, hit, sums)
    owner_t = small(iota((seq_count, blocks), 1) // shard_blocks == iota((seq_count, blocks), 0))
    asked = lax.dot_general(
        owner_t, small(sums), (((1,), (1,)), ((), ())), preferred_element_type=jnp.float32
    )
    tab_ref[:seq_count] = (asked + 0.5).astype(jnp.int32)[:, None, :]
    spot = (block_ids // shard_blocks * capacity).astype(jnp.float32) + rank
    spot = jnp.sum(jnp.where(needed > 0.5, spot, 0.0), axis=1, keepdims=True)
    spot = (jnp.broadcast_to(spot, (heads, 128)) + 0.5).astype(jnp.int32)
    tab_ref[seq_count:] = spot[:, None, :]


def fused_kernel(
    seq_count, capacity, shard_blocks,
    key_ref, value_ref, query_hbm, perm_hbm, mask_hbm, stage_ref, tab_ref, far_tab_ref,
    perm_ref, mask_ref, keys, values, query_ref, send_ref, got_ref, rows_ref, blocks_ref,
    own_tab, far_tab, asked,
    load_sem, swap_send, swap_recv, ask_send, ask_recv, misc_sem,
    send_sem, recvs, relay_send, relay_recv, step_sem,
):
    group, me = lax.axis_index("head"), lax.axis_index("seq")
    other = 1 - group
    heads = perm_ref.shape[0]
    rows = query_hbm.shape[0]
    half = heads * HEAD_DIM
    spread = seq_count // 4
    peer_of = lambda step: partner_of(me, step, seq_count)
    top, low = (me // (2 * spread)) % 2, (me // spread) % 2
    edge = (top + low + 1) % 2

    def near_peer(i):
        far = (3 - i) // 2
        turn = edge * ((i + 1) // 2) + (1 - edge) * ((i + 1) % 2)
        return peer_of(spread * (2 * far + turn))

    def side_peer(plane, k):
        return peer_of(spread * plane + 1 + k)

    def turn_of(k):
        return 3 + k * (2 - 3) + k * (k - 1) // 2 * (1 - 2 * 2 + 3) - 1

    def far_peer(k):
        return side_peer(2 + (edge + (1 - top) * (1 - group) + k) % 2, turn_of(k // 2))

    def times(count, body):
        lax.fori_loop(0, count, lambda i, carry: (body(i), carry)[1], 0)

    beside = spread - 1

    barrier = pltpu.get_barrier_semaphore()
    pl.semaphore_signal(barrier, inc=1, device_id={"head": other}, device_id_type=MESH)

    def signal(sem, step):
        pl.semaphore_signal(sem, inc=1, device_id={"seq": peer_of(step)}, device_id_type=MESH)

    for step in (spread, 2 * spread, 1, 2):
        signal(barrier, step)

    @pl.when(edge == 0)
    def _():
        signal(barrier, 3 * spread)

    masks = pltpu.make_async_copy(mask_hbm, mask_ref, misc_sem.at[0])
    masks.start()
    perms = pltpu.make_async_copy(perm_hbm, perm_ref, misc_sem.at[1])
    perms.start()
    here = pl.ds(pl.multiple_of(group * rows, rows), rows)
    sides = ((key_ref, keys), (value_ref, values))

    def load(number, start_at, span):
        src, dst = sides[number]
        mine = pl.ds(pl.multiple_of(group * half + start_at, HEAD_DIM), span)
        return pltpu.make_async_copy(
            src.at[:, mine], dst.at[here, pl.ds(start_at, span)], load_sem.at[number]
        )

    def swap(number, start_at, span):
        src, dst = sides[number]
        theirs = pl.ds(pl.multiple_of(other * half + start_at, HEAD_DIM), span)
        return pltpu.make_async_remote_copy(
            src_ref=src.at[:, theirs], dst_ref=dst.at[here, pl.ds(start_at, span)],
            send_sem=swap_send.at[number], recv_sem=swap_recv.at[number],
            device_id={"head": other}, device_id_type=MESH,
        )

    parts = 4
    cuts = [(number, part * (half // parts), half // parts) for number in range(2) for part in range(parts)]
    for cut in cuts[:parts]:
        load(*cut).start()
    take = pltpu.make_async_copy(query_hbm, query_ref, misc_sem.at[2])
    masks.wait()
    request(shard_blocks, capacity, mask_ref, tab_ref)
    pl.semaphore_wait(barrier, 6 - edge)

    def ask(peer, landing, near, last=0):
        return pltpu.make_async_remote_copy(
            src_ref=tab_ref.at[peer], dst_ref=asked.at[peer if landing else me],
            send_sem=ask_send.at[0],
            recv_sem=ask_recv.at[near * (1 + (peer if landing else me) // spread) + last * 5],
            device_id={"seq": peer}, device_id_type=MESH,
        )

    def asks(count):
        return pltpu.make_async_remote_copy(
            src_ref=tab_ref.at[pl.ds(0, count)], dst_ref=asked.at[pl.ds(0, count)],
            send_sem=ask_send.at[0], recv_sem=ask_recv.at[0],
            device_id={"head": other}, device_id_type=MESH,
        )

    ask(peer_of(2 * spread), False, 1).start()
    ask(peer_of(spread), False, 1).start()

    @pl.when(edge == 0)
    def _():
        ask(peer_of(3 * spread), False, 1).start()

    for cut in cuts:
        swap(*cut).start()
    for cut in cuts[parts:]:
        load(*cut).start()
    for number, step in enumerate((1, 2, spread)):
        signal(step_sem.at[number], step)
    tell = pltpu.make_async_remote_copy(
        src_ref=tab_ref, dst_ref=far_tab_ref, send_sem=misc_sem.at[3], recv_sem=misc_sem.at[4],
        device_id={"head": other}, device_id_type=MESH,
    )
    tell.start()
    own = pltpu.make_async_copy(tab_ref, own_tab, misc_sem.at[6])
    own.start()
    perms.wait()
    for b in range(shard_blocks):
        blocks_ref[b * heads : (b + 1) * heads] = perm_ref[:, b * BLOCK : (b + 1) * BLOCK][:, None, :]
    rows_ref[...] = jnp.zeros_like(rows_ref)

    def ask_far(*places):
        for plane, turn in places:
            ask(peer_of(spread * plane + turn), False, 0).start()

    for number in range(3):
        pl.semaphore_wait(step_sem.at[number], 1)
    for number, step in enumerate((1, 2)):
        signal(step_sem.at[3 + number], step)

    @pl.when(edge == 1)
    def _():
        ask(peer_of(3 * spread), False, 1).start()

    ask_far((2, 1), (2, 2), (1, 1), (1, 2), (0, 1), (0, 2), (0, 3))

    token = iota((BLOCK, 2 * rows), 1) + me * (2 * rows)

    def gather(table_ref, peer, whiches, put):
        chosen = []
        for c in range(capacity):
            pair = jnp.clip(table_ref[peer, 0, 2 * c], 0, heads * shard_blocks - 1)
            rows_ref[c : c + 1, :] = blocks_ref[pair]
            head = jnp.clip(table_ref[peer, 0, 2 * c + 1], 0, heads - 1)
            chosen.append(head * HEAD_DIM)
        turned = rows_ref[...].T
        for c, start_at in enumerate(chosen):
            table = (turned[:, c : c + 1] == token).astype(jnp.float32).astype(jnp.bfloat16)
            for which in whiches:
                got = jnp.dot(
                    table, sides[which][1][:, pl.ds(start_at, HEAD_DIM)],
                    preferred_element_type=jnp.float32,
                )
                put(which, c, got.astype(jnp.bfloat16))

    def to_send(peer):
        def put(which, c, got):
            send_ref[peer, which, c] = got

        return put

    def near_deliver(which, peer):
        return pltpu.make_async_remote_copy(
            src_ref=send_ref.at[peer, which], dst_ref=got_ref.at[0, me, which],
            send_sem=send_sem.at[0], recv_sem=recvs.at[me],
            device_id={"seq": peer}, device_id_type=MESH,
        )

    def deliver(peer, landing):
        source = peer if landing else me
        return pltpu.make_async_remote_copy(
            src_ref=send_ref.at[peer], dst_ref=got_ref.at[0, source],
            send_sem=send_sem.at[0], recv_sem=recvs.at[source],
            device_id={"seq": peer}, device_id_type=MESH,
        )

    def relay(source):
        return pltpu.make_async_remote_copy(
            src_ref=got_ref.at[0, source], dst_ref=got_ref.at[1, source],
            send_sem=relay_send.at[0], recv_sem=relay_recv.at[source],
            device_id={"head": other}, device_id_type=MESH,
        )

    def serve(i, which):
        peer = near_peer(i)
        gather(asked, peer, (which,), to_send(peer))
        near_deliver(which, peer).start()

    def heed(i):
        peer = near_peer(i)
        ask(peer, True, 1).wait_recv()

    load(0, 0, half).wait()
    heed(0)
    pl.semaphore_wait(step_sem.at[3], 1)
    pl.semaphore_wait(step_sem.at[4], 1)
    signal(step_sem.at[5], 2)
    ask_far((2, 3), (3, 1), (3, 2), (1, 3))
    remotest = peer_of(3 * spread + 3)

    @pl.when(edge == 0)
    def _():
        ask(remotest, False, 0, 1).start()

    swap(0, 0, half).wait_recv()
    serve(0, 0)
    pl.semaphore_wait(step_sem.at[5], 1)

    @pl.when(edge == 1)
    def _():
        ask(remotest, False, 0, 1).start()

    heed(1)
    serve(1, 0)
    heed(2)
    serve(2, 0)
    load(1, 0, half).wait()
    swap(1, 0, half).wait_recv()
    times(3, lambda i: serve(i, 1))
    take.start()
    own.wait()
    tell.wait_recv()
    far_scalar = pltpu.make_async_copy(far_tab_ref, far_tab, misc_sem.at[8])
    far_scalar.start()

    def to_got(which, c, got):
        got_ref[0, me, which, c] = got

    gather(own_tab, me, (0, 1), to_got)
    relay(me).start()
    asks(seq_count - 5).wait_recv()

    def produce(i):
        far = edge * ((i + 2 * beside) // (3 * beside)) + (1 - edge) * ((5 * beside - 1 - i) // (3 * beside))
        at = i - beside * edge + 3 * beside * (1 - far)
        peer = far * far_peer(at % (3 * beside)) + (1 - far) * side_peer(1, turn_of(at % beside))
        gather(asked, peer, (0, 1), to_send(peer))
        deliver(peer, False).start()

    def produce_beside(k):
        peer = side_peer(0, turn_of(k))
        gather(asked, peer, (0, 1), to_send(peer))
        deliver(peer, False).start()

    @pl.when(edge == 0)
    def _():
        ask(remotest, True, 0, 1).wait_recv()

    times(beside, produce_beside)
    times(beside, produce)

    @pl.when(edge == 1)
    def _():
        ask(remotest, True, 0, 1).wait_recv()

    times(2 * beside, lambda i: produce(i + beside))
    far_scalar.wait()
    take.wait()

    scale = math.log2(math.e) / math.sqrt(HEAD_DIM)
    ones = jnp.ones((BLOCK, HEAD_DIM), jnp.bfloat16)

    def attend(items):
        scores = []
        for rel, source, c in items:
            tab, base = ((own_tab, group), (far_tab, other))[rel]
            head = base * heads + jnp.clip(tab[source, 0, 2 * c + 1], 0, heads - 1)
            query = query_ref[:, pl.ds(head * HEAD_DIM, HEAD_DIM)]
            scores.append(
                lax.dot_general(
                    query, got_ref[rel, source, 0, c], (((1,), (1,)), ((), ())),
                    preferred_element_type=jnp.float32,
                )
            )
        weights = []
        for score in scores:
            peak = jnp.max(score, axis=1, keepdims=True)
            weights.append(jnp.exp2((score - peak) * scale).astype(jnp.bfloat16))
        for (rel, source, c), weight in zip(items, weights):
            mixed = jnp.dot(
                weight, jnp.concatenate([got_ref[rel, source, 1, c], ones], axis=1),
                preferred_element_type=jnp.float32,
            )
            stage_ref[rel, source * capacity + c] = (
                mixed[:, :HEAD_DIM] / mixed[:, HEAD_DIM:]
            ).astype(jnp.bfloat16)

    slots = lambda rel, source: [(rel, source, c) for c in range(capacity)]
    attend(slots(0, me))
    relay(me).wait_recv()
    attend(slots(1, me))

    def near_take(i):
        source = near_peer(i)
        deliver(source, True).wait_recv()
        relay(source).start()

    times(3, near_take)

    def near_use(i):
        source = near_peer(i)
        relay(source).wait_recv()
        attend(slots(0, source) + slots(1, source))

    times(3, near_use)

    def rest_peer(i):
        late = i // (2 * beside)
        plane = (1 - late) * (i // beside) + late * (2 + i % 2)
        return side_peer(plane, turn_of((1 - late) * (i % beside) + late * (i % (2 * beside) // 2)))

    def use(i, first=False, last=False):
        before = [] if first else [rest_peer(2 * i - 2), rest_peer(2 * i - 1)]
        sources = [] if last else [rest_peer(2 * i), rest_peer(2 * i + 1)]
        for source in sources:
            deliver(source, True).wait_recv()
            relay(source).start()
        for source in before:
            relay(source).wait_recv()
        items = [slots(0, source) for source in sources] + [slots(1, source) for source in before]
        attend(sum(items, []))

    pairs = 2 * beside
    use(0, first=True)
    times(pairs - 1, lambda i: use(i + 1))
    use(pairs, last=True)

    for number in range(2):
        swap(number, 0, half).wait_send()
    asks(seq_count - 1).wait_send()
    tell.wait_send()
    pltpu.make_async_remote_copy(
        src_ref=send_ref.at[pl.ds(0, seq_count - 1)], dst_ref=got_ref.at[0, pl.ds(0, seq_count - 1)],
        send_sem=send_sem.at[0], recv_sem=recvs.at[me],
        device_id={"head": other}, device_id_type=MESH,
    ).wait_send()
    pltpu.make_async_remote_copy(
        src_ref=got_ref.at[0], dst_ref=got_ref.at[1],
        send_sem=relay_send.at[0], recv_sem=relay_recv.at[me],
        device_id={"head": other}, device_id_type=MESH,
    ).wait_send()


def flush_kernel(seq_count, stage_ref, tab_ref, far_tab_ref, out_ref, sem):
    group = lax.axis_index("head")
    heads = tab_ref.shape[0] - seq_count
    last = stage_ref.shape[1] - 1
    for local in range(heads):
        for rel, (tab, base) in enumerate(((tab_ref, group), (far_tab_ref, 1 - group))):
            slot = jnp.clip(tab[seq_count + local, 0, 0], 0, last)
            at = pl.multiple_of((base * heads + local) * HEAD_DIM, HEAD_DIM)
            pltpu.make_async_copy(
                stage_ref.at[rel, slot], out_ref.at[:, pl.ds(at, HEAD_DIM)], sem.at[0]
            ).start()
    pltpu.make_async_copy(out_ref, out_ref, sem.at[0]).wait()


def fused(key_states, value_states, queries, cluster_perm, block_mask, capacity):
    heads, shard_rows = cluster_perm.shape
    shard_blocks = shard_rows // BLOCK
    seq_count = lax.axis_size("seq")
    rows, columns = queries.shape
    vmem = pl.BlockSpec(memory_space=pltpu.VMEM)
    anywhere = pl.BlockSpec(memory_space=pltpu.HBM)
    bf16, i32 = jnp.bfloat16, jnp.int32
    dma = pltpu.SemaphoreType.DMA
    resident = 4 * seq_count * capacity * rows * HEAD_DIM + 8 * 8 * 128 * (seq_count + heads)
    table, asks = (seq_count + heads, 1, 128), (seq_count, 1, 128)
    staged = pl.pallas_call(
        functools.partial(fused_kernel, seq_count, capacity, shard_blocks),
        out_shape=(
            pltpu.VMEM((2, seq_count * capacity, rows, HEAD_DIM), bf16),
            pltpu.VMEM(table, i32), pltpu.VMEM(table, i32),
        ),
        in_specs=[anywhere] * 5,
        out_specs=(vmem, vmem, vmem),
        scratch_shapes=[
            pltpu.VMEM(cluster_perm.shape, i32), pltpu.VMEM(block_mask.shape, i32),
            pltpu.VMEM((shard_rows, heads * HEAD_DIM), bf16),
            pltpu.VMEM((shard_rows, heads * HEAD_DIM), bf16),
            pltpu.VMEM((rows, columns), bf16),
            pltpu.VMEM((seq_count, 2, capacity, BLOCK, HEAD_DIM), bf16),
            pltpu.VMEM((2, seq_count, 2, capacity, BLOCK, HEAD_DIM), bf16),
            pltpu.VMEM((8 * -(-capacity // 8), 128), i32),
            pltpu.VMEM((shard_blocks * heads, 1, BLOCK), i32),
            pltpu.SMEM(table, i32), pltpu.SMEM(table, i32),
            pltpu.SMEM(asks, i32),
            dma((2,)), dma((2,)), dma((2,)), dma((1,)), dma((6,)), dma((9,)),
            dma((1,)), dma((seq_count,)), dma((1,)), dma((seq_count,)),
            pltpu.SemaphoreType.REGULAR((6,)),
        ],
        compiler_params=pltpu.CompilerParams(
            collective_id=1, has_side_effects=True,
            vmem_limit_bytes=67043328 - resident - 256 * 1024,
        ),
        name="fused",
    )(key_states, value_states, queries, cluster_perm, block_mask)
    return pl.pallas_call(
        functools.partial(flush_kernel, seq_count),
        out_shape=jax.ShapeDtypeStruct((rows, columns), bf16),
        in_specs=[vmem, vmem, vmem],
        out_specs=anywhere,
        scratch_shapes=[dma((1,))],
        compiler_params=pltpu.CompilerParams(vmem_limit_bytes=8 * 1024 * 1024),
        name="flush",
    )(*staged)


def attend_kernel(heads, picks, width, capacity, masked, pos_own, pos_far, *refs):
    if masked:
        query_ref, kv_ref, allow_ref, out_ref, stage, sems = refs
    else:
        query_ref, kv_ref, out_ref, stage, sems = refs
    group = lax.axis_index("head")
    scale = math.log2(math.e) / math.sqrt(HEAD_DIM)
    ones = jnp.ones((BLOCK, HEAD_DIM), jnp.bfloat16)
    span = width * HEAD_DIM
    batches = query_ref.shape[1] // span

    def put(batch, buffer):
        return pltpu.make_async_copy(
            stage.at[buffer],
            out_ref.at[:, pl.ds(pl.multiple_of(batch * span, span), span)],
            sems.at[buffer],
        )

    def one(batch, carry):
        where_, scores = [], []
        for w in range(width):
            head = batch * width + w
            away = (head // heads) != group
            local = head % heads
            query = query_ref[:, pl.ds(pl.multiple_of(head * HEAD_DIM, HEAD_DIM), HEAD_DIM)]
            for p in range(picks):
                slot = jnp.where(away, pos_far[local, p], pos_own[local, p])
                spot = (slot // capacity, slot % capacity)
                rel = away.astype(jnp.int32)
                where_.append((rel, spot))
                score = lax.dot_general(
                    query, kv_ref[rel, 0, spot[0], spot[1]], (((1,), (1,)), ((), ())),
                    preferred_element_type=jnp.float32,
                )
                if masked:
                    score = jnp.where(allow_ref[head, :, p : p + 1] > 0, score, -jnp.inf)
                scores.append(score)
        weights = []
        for w in range(width):
            own = scores[w * picks : (w + 1) * picks]
            top = jnp.max(functools.reduce(jnp.maximum, own), axis=1, keepdims=True)
            weights.extend([jnp.exp2((s - top) * scale).astype(jnp.bfloat16) for s in own])
        buffer = batch % 2

        @pl.when(batch >= 2)
        def _():
            put(batch - 2, buffer).wait()

        for w in range(width):
            parts = []
            for p in range(picks):
                rel, spot = where_[w * picks + p]
                parts.append(
                    jnp.dot(
                        weights[w * picks + p],
                        jnp.concatenate([kv_ref[rel, 1, spot[0], spot[1]], ones], axis=1),
                        preferred_element_type=jnp.float32,
                    )
                )
            mixed = functools.reduce(jnp.add, parts)
            stage[buffer, :, w * HEAD_DIM : (w + 1) * HEAD_DIM] = (
                mixed[:, :HEAD_DIM] / mixed[:, HEAD_DIM:]
            ).astype(jnp.bfloat16)
        put(batch, buffer).start()
        return carry

    lax.fori_loop(0, batches, one, 0)
    for batch in range(max(0, batches - 2), batches):
        put(batch, batch % 2).wait()


def token_allow(cluster_perm, block_mask, picks, me, shard_rows):
    needed = jnp.max(block_mask, axis=1)
    prefix = jnp.cumsum(needed, axis=1) - needed
    chosen = (needed[:, :, None] == 1) & (prefix[:, :, None] == jnp.arange(picks)[None, None, :])
    live = jnp.einsum(
        "hqb,hbp->hqp", block_mask.astype(jnp.float32), chosen.astype(jnp.float32)
    )
    group_heads = cluster_perm.shape[0]
    local = cluster_perm - me * shard_rows
    place = jnp.zeros((group_heads, shard_rows), jnp.int32)
    place = place.at[jnp.arange(group_heads)[:, None], local].set(
        jnp.broadcast_to(jnp.arange(shard_rows, dtype=jnp.int32) // BLOCK, local.shape)
    )
    by_token = jnp.take_along_axis(live, place[:, :, None], axis=1).astype(jnp.float32)
    return lax.all_to_all(by_token, "head", split_axis=1, concat_axis=0, tiled=True)


def shards(queries, key_states, value_states, cluster_perm, block_mask):
    group_heads, shard_rows = cluster_perm.shape
    shard_blocks = shard_rows // BLOCK
    seq_count = lax.axis_size("seq")
    block_total = block_mask.shape[2]
    picks = max(1, block_total // 64)
    capacity = max(
        1, min(shard_blocks, (group_heads * picks * 8 + 5 * seq_count - 1) // (5 * seq_count))
    )
    rows, columns = queries.shape
    me = lax.axis_index("seq")
    if picks == 1 and seq_count == 16 and shard_blocks * group_heads <= 256:
        return fused(key_states, value_states, queries, cluster_perm, block_mask, capacity)
    vmem = pl.BlockSpec(memory_space=pltpu.VMEM)
    anywhere = pl.BlockSpec(memory_space=pltpu.HBM)
    struct = jax.ShapeDtypeStruct
    bf16, i32 = jnp.bfloat16, jnp.int32

    dma = pltpu.SemaphoreType.DMA
    kv_half = pltpu.VMEM((group_heads, rows, HEAD_DIM), bf16)
    table = struct((group_heads, 128), i32)
    resident = 2 * (4 * seq_count * capacity * BLOCK * HEAD_DIM + rows * columns)
    grant = 67043328 - resident - 256 * 1024
    got, positions, pos_far, near_queries = pl.pallas_call(
        functools.partial(exchange_kernel, seq_count, capacity, shard_blocks, picks),
        out_shape=(
            pltpu.VMEM((2, 2, seq_count, capacity, BLOCK, HEAD_DIM), bf16), table, table,
            pltpu.VMEM((rows, columns), bf16),
        ),
        in_specs=[anywhere, anywhere, anywhere, vmem, vmem],
        out_specs=(vmem, vmem, vmem, vmem),
        scratch_shapes=[
            kv_half, kv_half, kv_half, kv_half,
            pltpu.VMEM((seq_count, 1, 128), i32),
            pltpu.VMEM((seq_count, 1, 128), i32),
            pltpu.SMEM((seq_count, 1, 128), i32),
            pltpu.VMEM((2, seq_count, capacity, BLOCK, HEAD_DIM), bf16),
            pltpu.VMEM((8 * -(-capacity // 8), 128), i32),
            pltpu.VMEM((shard_blocks * group_heads, 1, BLOCK), i32),
            dma((2 * group_heads,)), dma((2 * group_heads,)), dma((2 * group_heads,)),
            dma((seq_count,)), dma((seq_count,)), dma((7,)),
        ] + [dma((2, seq_count)) for _ in range(4)],
        compiler_params=pltpu.CompilerParams(
            collective_id=0, has_side_effects=True, vmem_limit_bytes=grant
        ),
        name="exchange",
    )(key_states, value_states, queries, cluster_perm, block_mask)

    masked = picks > 1
    total_heads = columns // HEAD_DIM
    width = 8 if total_heads % 8 == 0 else 1
    operands = [near_queries, got]
    if masked:
        operands.append(token_allow(cluster_perm, block_mask, picks, me, shard_rows))
    smem = pl.BlockSpec(memory_space=pltpu.SMEM)
    return pl.pallas_call(
        functools.partial(attend_kernel, group_heads, picks, width, capacity, masked),
        out_shape=struct((rows, columns), bf16),
        in_specs=[smem, smem] + [vmem] * len(operands),
        out_specs=anywhere,
        scratch_shapes=[pltpu.VMEM((2, rows, width * HEAD_DIM), bf16), dma((2,))],
        compiler_params=pltpu.CompilerParams(vmem_limit_bytes=24 * 1024 * 1024),
        name="attend",
    )(positions, pos_far, *operands)


def solution(mesh):
    rows = P(("seq", "head"), None)
    placed = (rows, rows, rows, P("head", "seq"), P("head", "seq", None))
    return jax.shard_map(shards, mesh=mesh, in_specs=placed, out_specs=rows, check_vma=False)
```

```python
import functools
import math

import jax
import jax.numpy as jnp
from jax import lax
from jax.experimental import pallas as pl
from jax.experimental.pallas import tpu as pltpu
from jax.sharding import PartitionSpec as P

HEAD_DIM = 128
BLOCK = 128
MESH = pl.DeviceIdType.MESH
HIGHEST = lax.Precision.HIGHEST


def iota(shape, dim):
    return lax.broadcasted_iota(jnp.int32, shape, dim)


def partner_of(me, step, count):
    if count & (count - 1):
        raise ValueError("seq size")
    peer = 0
    bit = 1
    while bit < count:
        peer = peer + bit * (((me // bit) + (step // bit)) % 2)
        bit *= 2
    return peer


def route(shard_blocks, capacity, picks, mask_ref, req_ref, pos_ref):
    heads, _, blocks = mask_ref.shape
    seq_count = blocks // shard_blocks
    needed = jnp.max(mask_ref[...], axis=1).astype(jnp.float32)
    row, col = iota((blocks, blocks), 0), iota((blocks, blocks), 1)
    same = (row // shard_blocks) == (col // shard_blocks)
    dot = functools.partial(jnp.dot, precision=HIGHEST, preferred_element_type=jnp.float32)
    ones = lambda flag: flag.astype(jnp.float32)
    by_owner = dot(needed, ones(same))
    before_in_owner = dot(needed, ones(same & (row < col)))
    before_all = dot(needed, ones(row < col))
    lower = ones(iota((heads, heads), 1) < iota((heads, heads), 0))
    rank = dot(lower, by_owner) + before_in_owner
    head_ids, block_ids = iota((heads, blocks), 0), iota((heads, blocks), 1)
    pair = (block_ids % shard_blocks * heads + head_ids).astype(jnp.float32)
    slot_row = iota((128, blocks), 0)
    sums = jnp.zeros((128, blocks), jnp.float32)
    for c in range(capacity):
        hit = jnp.where((rank == c) & (needed > 0.5), pair, 0.0)
        sums = jnp.where(slot_row == 2 * c, jnp.sum(hit, axis=0, keepdims=True), sums)
        hit = jnp.where((rank == c) & (needed > 0.5), head_ids.astype(jnp.float32), 0.0)
        sums = jnp.where(slot_row == 2 * c + 1, jnp.sum(hit, axis=0, keepdims=True), sums)
    owner_t = ones(iota((seq_count, blocks), 1) // shard_blocks == iota((seq_count, blocks), 0))
    asked = lax.dot_general(
        owner_t, sums, (((1,), (1,)), ((), ())), precision=HIGHEST,
        preferred_element_type=jnp.float32,
    )
    req_ref[...] = (asked + 0.5).astype(jnp.int32)[:, None, :]
    position = (block_ids // shard_blocks * capacity).astype(jnp.float32) + rank
    lane = iota((heads, 128), 1)
    table = jnp.zeros((heads, 128), jnp.float32)
    for p in range(picks):
        here = jnp.where((before_all == p) & (needed > 0.5), position, 0.0)
        table = jnp.where(lane == p, jnp.sum(here, axis=1, keepdims=True), table)
    pos_ref[...] = (table + 0.5).astype(jnp.int32)


def order(i, me, count):
    top, next_bit = (me // (count // 2)) % 2, (me // (count // 4)) % 2
    end = (top + next_bit + 1) % 2
    return end * (1 + (i + count // 4 - 1) % (count - 1)) + (1 - end) * (count - 1 - i)


def exchange_kernel(
    seq_count, capacity, shard_blocks, picks,
    key_ref, value_ref, query_ref, perm_ref, mask_ref, got_ref, pos_ref, pos_out, query_out,
    near_key, near_value, far_key, far_value, req_ref, asked_ref, asked, send_ref, rows_ref, blocks_ref,
    load_sem, swap_send, swap_recv, req_send, req_recv, misc_sem,
    sends, recvs, relay_send, relay_recv,
):
    group, me = lax.axis_index("head"), lax.axis_index("seq")
    other = 1 - group
    near_kv, far_kv = (near_key, near_value), (far_key, far_value)
    heads, rows = near_key.shape[:2]
    barrier = pltpu.get_barrier_semaphore()
    pl.semaphore_signal(barrier, inc=1, device_id={"head": other}, device_id_type=MESH)

    def greet(step, carry):
        pl.semaphore_signal(
            barrier, inc=1, device_id={"seq": partner_of(me, step, seq_count)}, device_id_type=MESH
        )
        return carry

    lax.fori_loop(1, seq_count, greet, 0)
    loads = []
    for number, src in enumerate((key_ref, value_ref)):
        for head in range(heads):
            start_at = pl.multiple_of((group * heads + head) * HEAD_DIM, HEAD_DIM)
            loads.append(
                pltpu.make_async_copy(
                    src.at[:, pl.ds(start_at, HEAD_DIM)], near_kv[number].at[head],
                    load_sem.at[number * heads + head],
                )
            )
    for copy in loads:
        copy.start()
    pl.semaphore_wait(barrier, seq_count)

    swaps = []
    for number, src in enumerate((key_ref, value_ref)):
        for head in range(heads):
            start_at = pl.multiple_of((other * heads + head) * HEAD_DIM, HEAD_DIM)
            at = number * heads + head
            swaps.append(
                pltpu.make_async_remote_copy(
                    src_ref=src.at[:, pl.ds(start_at, HEAD_DIM)], dst_ref=far_kv[number].at[head],
                    send_sem=swap_send.at[at], recv_sem=swap_recv.at[at],
                    device_id={"head": other}, device_id_type=MESH,
                )
            )
    for copy in swaps:
        copy.start()
    route(shard_blocks, capacity, picks, mask_ref, req_ref, pos_ref)
    for b in range(shard_blocks):
        blocks_ref[b * heads : (b + 1) * heads] = perm_ref[:, b * BLOCK : (b + 1) * BLOCK][:, None, :]
    rows_ref[...] = jnp.zeros_like(rows_ref)

    def ask(step, landing):
        peer = partner_of(me, step, seq_count)
        return pltpu.make_async_remote_copy(
            src_ref=req_ref.at[peer], dst_ref=asked_ref.at[peer if landing else me],
            send_sem=req_send.at[step], recv_sem=req_recv.at[step],
            device_id={"seq": peer}, device_id_type=MESH,
        )

    def start_ask(step, carry):
        ask(step, False).start()
        return carry

    lax.fori_loop(1, seq_count, start_ask, 0)
    tell = pltpu.make_async_remote_copy(
        src_ref=pos_ref, dst_ref=pos_out, send_sem=misc_sem.at[0], recv_sem=misc_sem.at[1],
        device_id={"head": other}, device_id_type=MESH,
    )
    tell.start()
    stay = pltpu.make_async_copy(query_ref, query_out, misc_sem.at[6])
    stay.start()
    keep = pltpu.make_async_copy(req_ref.at[me], asked_ref.at[me], misc_sem.at[2])
    keep.start()
    keep.wait()

    def finish_ask(step, carry):
        ask(step, True).wait()
        return carry

    lax.fori_loop(1, seq_count, finish_ask, 0)
    to_scalar = pltpu.make_async_copy(asked_ref, asked, misc_sem.at[3])
    to_scalar.start()
    to_scalar.wait()
    base = me * (2 * rows)
    token = iota((BLOCK, rows), 1)
    near = token + (base + group * rows)
    far = token + (base + other * rows)

    def gather(which, peer):
        chosen = []
        for c in range(capacity):
            pair = jnp.clip(asked[peer, 0, 2 * c], 0, heads * shard_blocks - 1)
            rows_ref[c : c + 1, :] = blocks_ref[pair]
            chosen.append(jnp.clip(asked[peer, 0, 2 * c + 1], 0, heads - 1))
        turned = rows_ref[...].T
        for c, head in enumerate(chosen):
            column = turned[:, c : c + 1]
            near_table = (column == near).astype(jnp.float32).astype(jnp.bfloat16)
            far_table = (column == far).astype(jnp.float32).astype(jnp.bfloat16)
            got = jnp.dot(near_table, near_kv[which][head], preferred_element_type=jnp.float32)
            got += jnp.dot(far_table, far_kv[which][head], preferred_element_type=jnp.float32)
            send_ref[which, peer, c] = got.astype(jnp.bfloat16)

    def deliver(which, step, landing):
        peer = partner_of(me, step, seq_count)
        return pltpu.make_async_remote_copy(
            src_ref=send_ref.at[which, peer],
            dst_ref=got_ref.at[0, which, peer if landing else me],
            send_sem=sends.at[which, step], recv_sem=recvs.at[which, step],
            device_id={"seq": peer}, device_id_type=MESH,
        )

    def relay(which, step):
        peer = partner_of(me, step, seq_count)
        return pltpu.make_async_remote_copy(
            src_ref=got_ref.at[0, which, peer], dst_ref=got_ref.at[1, which, peer],
            send_sem=relay_send.at[which, step], recv_sem=relay_recv.at[which, step],
            device_id={"head": other}, device_id_type=MESH,
        )

    for which in range(2):
        for copy in loads[which * heads : (which + 1) * heads]:
            copy.wait()
        for copy in swaps[which * heads : (which + 1) * heads]:
            copy.wait()
        gather(which, partner_of(me, order(0, me, seq_count), seq_count))

        def produce(i, carry, which=which):
            gather(which, partner_of(me, order(i, me, seq_count), seq_count))
            deliver(which, order(i - 1, me, seq_count), False).start()
            return carry

        lax.fori_loop(1, seq_count - 1, produce, 0)
        gather(which, me)
        deliver(which, order(seq_count - 2, me, seq_count), False).start()

    locals_ = []
    for which in range(2):
        mine = pltpu.make_async_copy(
            send_ref.at[which, me], got_ref.at[0, which, me], misc_sem.at[4 + which]
        )
        share = pltpu.make_async_remote_copy(
            src_ref=send_ref.at[which, me], dst_ref=got_ref.at[1, which, me],
            send_sem=relay_send.at[which, 0], recv_sem=relay_recv.at[which, 0],
            device_id={"head": other}, device_id_type=MESH,
        )
        mine.start()
        share.start()
        locals_.extend((mine, share))

    for which in range(2):

        def pass_on(i, carry, which=which):
            step = order(i, me, seq_count)
            deliver(which, step, True).wait_recv()
            relay(which, step).start()
            return carry

        lax.fori_loop(0, seq_count - 1, pass_on, 0)

    def finish(step, carry):
        for which in range(2):
            deliver(which, step, True).wait_send()
            relay(which, step).wait()
        return carry

    lax.fori_loop(1, seq_count, finish, 0)
    for copy in locals_:
        copy.wait()
    tell.wait()
    stay.wait()


def request(shard_blocks, capacity, mask_ref, tab_ref):
    heads, _, blocks = mask_ref.shape
    seq_count = blocks // shard_blocks
    needed = jnp.max(mask_ref[...], axis=1).astype(jnp.float32)
    row, col = iota((blocks, blocks), 0), iota((blocks, blocks), 1)
    same = (row // shard_blocks) == (col // shard_blocks)
    small = lambda value: value.astype(jnp.float32).astype(jnp.bfloat16)
    dot = functools.partial(jnp.dot, preferred_element_type=jnp.float32)
    by_owner = dot(small(needed), small(same))
    lower = small(iota((heads, heads), 1) < iota((heads, heads), 0))
    rank = dot(lower, small(by_owner)) + dot(small(needed), small(same & (row < col)))
    head_ids, block_ids = iota((heads, blocks), 0), iota((heads, blocks), 1)
    pair = (block_ids % shard_blocks * heads + head_ids).astype(jnp.float32)
    slot_row = iota((128, blocks), 0)
    sums = jnp.zeros((128, blocks), jnp.float32)
    for c in range(capacity):
        taken = (rank == c) & (needed > 0.5)
        for lane, value in ((2 * c, pair), (2 * c + 1, head_ids.astype(jnp.float32))):
            hit = jnp.sum(jnp.where(taken, value, 0.0), axis=0, keepdims=True)
            sums = jnp.where(slot_row == lane, hit, sums)
    owner_t = small(iota((seq_count, blocks), 1) // shard_blocks == iota((seq_count, blocks), 0))
    asked = lax.dot_general(
        owner_t, small(sums), (((1,), (1,)), ((), ())), preferred_element_type=jnp.float32
    )
    tab_ref[:seq_count] = (asked + 0.5).astype(jnp.int32)[:, None, :]
    spot = (block_ids // shard_blocks * capacity).astype(jnp.float32) + rank
    spot = jnp.sum(jnp.where(needed > 0.5, spot, 0.0), axis=1, keepdims=True)
    spot = (jnp.broadcast_to(spot, (heads, 128)) + 0.5).astype(jnp.int32)
    tab_ref[seq_count:] = spot[:, None, :]


def fused_kernel(
    seq_count, capacity, shard_blocks,
    key_ref, value_ref, query_hbm, perm_hbm, mask_hbm, stage_ref, tab_ref, far_tab_ref,
    perm_ref, mask_ref, keys, values, query_ref, send_ref, got_ref, rows_ref, blocks_ref,
    own_tab, far_tab, asked,
    load_sem, swap_send, swap_recv, ask_send, ask_recv, misc_sem,
    send_sem, recvs, relay_send, relay_recv, step_sem,
):
    group, me = lax.axis_index("head"), lax.axis_index("seq")
    other = 1 - group
    heads = perm_ref.shape[0]
    rows = query_hbm.shape[0]
    half = heads * HEAD_DIM
    spread = seq_count // 4
    peer_of = lambda step: partner_of(me, step, seq_count)
    top, low = (me // (2 * spread)) % 2, (me // spread) % 2
    edge = (top + low + 1) % 2

    def near_peer(i):
        far = (3 - i) // 2
        turn = edge * ((i + 1) // 2) + (1 - edge) * ((i + 1) % 2)
        return peer_of(spread * (2 * far + turn))

    def side_peer(plane, k):
        return peer_of(spread * plane + 1 + k)

    def turn_of(k):
        return 3 + k * (2 - 3) + k * (k - 1) // 2 * (1 - 2 * 2 + 3) - 1

    def far_peer(k):
        return side_peer(2 + (edge + (1 - top) * (1 - group) + k) % 2, turn_of(k // 2))

    def times(count, body):
        lax.fori_loop(0, count, lambda i, carry: (body(i), carry)[1], 0)

    beside = spread - 1

    barrier = pltpu.get_barrier_semaphore()
    pl.semaphore_signal(barrier, inc=1, device_id={"head": other}, device_id_type=MESH)

    def signal(sem, step):
        pl.semaphore_signal(sem, inc=1, device_id={"seq": peer_of(step)}, device_id_type=MESH)

    for step in (spread, 2 * spread, 1, 2):
        signal(barrier, step)

    @pl.when(edge == 0)
    def _():
        signal(barrier, 3 * spread)

    masks = pltpu.make_async_copy(mask_hbm, mask_ref, misc_sem.at[0])
    masks.start()
    perms = pltpu.make_async_copy(perm_hbm, perm_ref, misc_sem.at[1])
    perms.start()
    here = pl.ds(pl.multiple_of(group * rows, rows), rows)
    sides = ((key_ref, keys), (value_ref, values))

    def load(number, start_at, span):
        src, dst = sides[number]
        mine = pl.ds(pl.multiple_of(group * half + start_at, HEAD_DIM), span)
        return pltpu.make_async_copy(
            src.at[:, mine], dst.at[here, pl.ds(start_at, span)], load_sem.at[number]
        )

    def swap(number, start_at, span):
        src, dst = sides[number]
        theirs = pl.ds(pl.multiple_of(other * half + start_at, HEAD_DIM), span)
        return pltpu.make_async_remote_copy(
            src_ref=src.at[:, theirs], dst_ref=dst.at[here, pl.ds(start_at, span)],
            send_sem=swap_send.at[number], recv_sem=swap_recv.at[number],
            device_id={"head": other}, device_id_type=MESH,
        )

    parts = 1
    cuts = [(number, part * (half // parts), half // parts) for number in range(2) for part in range(parts)]
    for cut in cuts[:parts]:
        load(*cut).start()
    take = pltpu.make_async_copy(query_hbm, query_ref, misc_sem.at[2])
    masks.wait()
    request(shard_blocks, capacity, mask_ref, tab_ref)
    pl.semaphore_wait(barrier, 6 - edge)

    def ask(peer, landing, near, last=0):
        return pltpu.make_async_remote_copy(
            src_ref=tab_ref.at[peer], dst_ref=asked.at[peer if landing else me],
            send_sem=ask_send.at[0],
            recv_sem=ask_recv.at[near * (1 + (peer if landing else me) // spread) + last * 5],
            device_id={"seq": peer}, device_id_type=MESH,
        )

    def asks(count):
        return pltpu.make_async_remote_copy(
            src_ref=tab_ref.at[pl.ds(0, count)], dst_ref=asked.at[pl.ds(0, count)],
            send_sem=ask_send.at[0], recv_sem=ask_recv.at[0],
            device_id={"head": other}, device_id_type=MESH,
        )

    ask(peer_of(2 * spread), False, 1).start()
    ask(peer_of(spread), False, 1).start()

    @pl.when(edge == 0)
    def _():
        ask(peer_of(3 * spread), False, 1).start()

    for cut in cuts:
        swap(*cut).start()
    for cut in cuts[parts:]:
        load(*cut).start()
    for number, step in enumerate((1, 2, spread)):
        signal(step_sem.at[number], step)
    tell = pltpu.make_async_remote_copy(
        src_ref=tab_ref, dst_ref=far_tab_ref, send_sem=misc_sem.at[3], recv_sem=misc_sem.at[4],
        device_id={"head": other}, device_id_type=MESH,
    )
    tell.start()
    own = pltpu.make_async_copy(tab_ref, own_tab, misc_sem.at[6])
    own.start()
    perms.wait()
    for b in range(shard_blocks):
        blocks_ref[b * heads : (b + 1) * heads] = perm_ref[:, b * BLOCK : (b + 1) * BLOCK][:, None, :]
    rows_ref[...] = jnp.zeros_like(rows_ref)

    def ask_far(*places):
        for plane, turn in places:
            ask(peer_of(spread * plane + turn), False, 0).start()

    for number in range(3):
        pl.semaphore_wait(step_sem.at[number], 1)
    for number, step in enumerate((1, 2)):
        signal(step_sem.at[3 + number], step)

    @pl.when(edge == 1)
    def _():
        ask(peer_of(3 * spread), False, 1).start()

    ask_far((2, 1), (2, 2), (1, 1), (1, 2), (0, 1), (0, 2), (0, 3))

    token = iota((BLOCK, 2 * rows), 1) + me * (2 * rows)

    def gather(table_ref, peer, whiches, put):
        chosen = []
        for c in range(capacity):
            pair = jnp.clip(table_ref[peer, 0, 2 * c], 0, heads * shard_blocks - 1)
            rows_ref[c : c + 1, :] = blocks_ref[pair]
            head = jnp.clip(table_ref[peer, 0, 2 * c + 1], 0, heads - 1)
            chosen.append(head * HEAD_DIM)
        turned = rows_ref[...].T
        for c, start_at in enumerate(chosen):
            table = (turned[:, c : c + 1] == token).astype(jnp.float32).astype(jnp.bfloat16)
            for which in whiches:
                got = jnp.dot(
                    table, sides[which][1][:, pl.ds(start_at, HEAD_DIM)],
                    preferred_element_type=jnp.float32,
                )
                put(which, c, got.astype(jnp.bfloat16))

    def to_send(peer):
        def put(which, c, got):
            send_ref[peer, which, c] = got

        return put

    def near_deliver(which, peer):
        return pltpu.make_async_remote_copy(
            src_ref=send_ref.at[peer, which], dst_ref=got_ref.at[0, me, which],
            send_sem=send_sem.at[0], recv_sem=recvs.at[me],
            device_id={"seq": peer}, device_id_type=MESH,
        )

    def deliver(peer, landing):
        source = peer if landing else me
        return pltpu.make_async_remote_copy(
            src_ref=send_ref.at[peer], dst_ref=got_ref.at[0, source],
            send_sem=send_sem.at[0], recv_sem=recvs.at[source],
            device_id={"seq": peer}, device_id_type=MESH,
        )

    def relay(source):
        return pltpu.make_async_remote_copy(
            src_ref=got_ref.at[0, source], dst_ref=got_ref.at[1, source],
            send_sem=relay_send.at[0], recv_sem=relay_recv.at[source],
            device_id={"head": other}, device_id_type=MESH,
        )

    def serve(i, which):
        peer = near_peer(i)
        gather(asked, peer, (which,), to_send(peer))
        near_deliver(which, peer).start()

    def heed(i):
        peer = near_peer(i)
        ask(peer, True, 1).wait_recv()

    load(0, 0, half).wait()
    heed(0)
    pl.semaphore_wait(step_sem.at[3], 1)
    pl.semaphore_wait(step_sem.at[4], 1)
    signal(step_sem.at[5], 2)
    ask_far((2, 3), (3, 1), (3, 2), (1, 3))
    remotest = peer_of(3 * spread + 3)

    @pl.when(edge == 0)
    def _():
        ask(remotest, False, 0, 1).start()

    swap(0, 0, half).wait_recv()
    serve(0, 0)
    pl.semaphore_wait(step_sem.at[5], 1)

    @pl.when(edge == 1)
    def _():
        ask(remotest, False, 0, 1).start()

    heed(1)
    serve(1, 0)
    heed(2)
    serve(2, 0)
    load(1, 0, half).wait()
    swap(1, 0, half).wait_recv()
    times(3, lambda i: serve(i, 1))
    take.start()
    own.wait()
    tell.wait_recv()
    far_scalar = pltpu.make_async_copy(far_tab_ref, far_tab, misc_sem.at[5])
    far_scalar.start()

    def to_got(which, c, got):
        got_ref[0, me, which, c] = got

    gather(own_tab, me, (0, 1), to_got)
    relay(me).start()
    asks(seq_count - 5).wait_recv()

    def produce(i):
        far = edge * ((i + 2 * beside) // (3 * beside)) + (1 - edge) * ((5 * beside - 1 - i) // (3 * beside))
        at = i - beside * edge + 3 * beside * (1 - far)
        peer = far * far_peer(at % (3 * beside)) + (1 - far) * side_peer(1, turn_of(at % beside))
        gather(asked, peer, (0, 1), to_send(peer))
        deliver(peer, False).start()

    def produce_beside(k):
        peer = side_peer(0, turn_of(k))
        gather(asked, peer, (0, 1), to_send(peer))
        deliver(peer, False).start()

    @pl.when(edge == 0)
    def _():
        ask(remotest, True, 0, 1).wait_recv()

    times(beside, produce_beside)
    times(beside, produce)

    @pl.when(edge == 1)
    def _():
        ask(remotest, True, 0, 1).wait_recv()

    times(2 * beside, lambda i: produce(i + beside))
    far_scalar.wait()
    take.wait()

    scale = math.log2(math.e) / math.sqrt(HEAD_DIM)
    ones = jnp.ones((BLOCK, HEAD_DIM), jnp.bfloat16)

    def attend(items):
        scores = []
        for rel, source, c in items:
            tab, base = ((own_tab, group), (far_tab, other))[rel]
            head = base * heads + jnp.clip(tab[source, 0, 2 * c + 1], 0, heads - 1)
            query = query_ref[:, pl.ds(head * HEAD_DIM, HEAD_DIM)]
            scores.append(
                lax.dot_general(
                    query, got_ref[rel, source, 0, c], (((1,), (1,)), ((), ())),
                    preferred_element_type=jnp.float32,
                )
            )
        weights = []
        for score in scores:
            peak = jnp.max(score, axis=1, keepdims=True)
            weights.append(jnp.exp2((score - peak) * scale).astype(jnp.bfloat16))
        for (rel, source, c), weight in zip(items, weights):
            mixed = jnp.dot(
                weight, jnp.concatenate([got_ref[rel, source, 1, c], ones], axis=1),
                preferred_element_type=jnp.float32,
            )
            stage_ref[rel, source * capacity + c] = (
                mixed[:, :HEAD_DIM] / mixed[:, HEAD_DIM:]
            ).astype(jnp.bfloat16)

    slots = lambda rel, source: [(rel, source, c) for c in range(capacity)]
    attend(slots(0, me))
    relay(me).wait_recv()
    attend(slots(1, me))

    def near_take(i):
        source = near_peer(i)
        deliver(source, True).wait_recv()
        relay(source).start()

    times(3, near_take)

    def near_use(i):
        source = near_peer(i)
        relay(source).wait_recv()
        attend(slots(0, source) + slots(1, source))

    times(3, near_use)

    def rest_peer(i):
        late = i // (2 * beside)
        plane = (1 - late) * (i // beside) + late * (2 + i % 2)
        return side_peer(plane, turn_of((1 - late) * (i % beside) + late * (i % (2 * beside) // 2)))

    def use(i, first=False, last=False):
        before = [] if first else [rest_peer(2 * i - 2), rest_peer(2 * i - 1)]
        sources = [] if last else [rest_peer(2 * i), rest_peer(2 * i + 1)]
        for source in sources:
            deliver(source, True).wait_recv()
            relay(source).start()
        for source in before:
            relay(source).wait_recv()
        items = [slots(0, source) for source in sources] + [slots(1, source) for source in before]
        attend(sum(items, []))

    pairs = 2 * beside
    use(0, first=True)
    times(pairs - 1, lambda i: use(i + 1))
    use(pairs, last=True)

    for number in range(2):
        swap(number, 0, half).wait_send()
    asks(seq_count - 1).wait_send()
    tell.wait_send()
    pltpu.make_async_remote_copy(
        src_ref=send_ref.at[pl.ds(0, seq_count - 1)], dst_ref=got_ref.at[0, pl.ds(0, seq_count - 1)],
        send_sem=send_sem.at[0], recv_sem=recvs.at[me],
        device_id={"head": other}, device_id_type=MESH,
    ).wait_send()
    pltpu.make_async_remote_copy(
        src_ref=got_ref.at[0], dst_ref=got_ref.at[1],
        send_sem=relay_send.at[0], recv_sem=relay_recv.at[me],
        device_id={"head": other}, device_id_type=MESH,
    ).wait_send()


def flush_kernel(seq_count, stage_ref, tab_ref, far_tab_ref, out_ref, sem):
    group = lax.axis_index("head")
    heads = tab_ref.shape[0] - seq_count
    last = stage_ref.shape[1] - 1
    for local in range(heads):
        for rel, (tab, base) in enumerate(((tab_ref, group), (far_tab_ref, 1 - group))):
            slot = jnp.clip(tab[seq_count + local, 0, 0], 0, last)
            at = pl.multiple_of((base * heads + local) * HEAD_DIM, HEAD_DIM)
            pltpu.make_async_copy(
                stage_ref.at[rel, slot], out_ref.at[:, pl.ds(at, HEAD_DIM)], sem.at[0]
            ).start()
    pltpu.make_async_copy(out_ref, out_ref, sem.at[0]).wait()


def fused(key_states, value_states, queries, cluster_perm, block_mask, capacity):
    heads, shard_rows = cluster_perm.shape
    shard_blocks = shard_rows // BLOCK
    seq_count = lax.axis_size("seq")
    rows, columns = queries.shape
    vmem = pl.BlockSpec(memory_space=pltpu.VMEM)
    anywhere = pl.BlockSpec(memory_space=pltpu.HBM)
    bf16, i32 = jnp.bfloat16, jnp.int32
    dma = pltpu.SemaphoreType.DMA
    resident = 4 * seq_count * capacity * rows * HEAD_DIM + 8 * 8 * 128 * (seq_count + heads)
    table, asks = (seq_count + heads, 1, 128), (seq_count, 1, 128)
    staged = pl.pallas_call(
        functools.partial(fused_kernel, seq_count, capacity, shard_blocks),
        out_shape=(
            pltpu.VMEM((2, seq_count * capacity, rows, HEAD_DIM), bf16),
            pltpu.VMEM(table, i32), pltpu.VMEM(table, i32),
        ),
        in_specs=[anywhere] * 5,
        out_specs=(vmem, vmem, vmem),
        scratch_shapes=[
            pltpu.VMEM(cluster_perm.shape, i32), pltpu.VMEM(block_mask.shape, i32),
            pltpu.VMEM((shard_rows, heads * HEAD_DIM), bf16),
            pltpu.VMEM((shard_rows, heads * HEAD_DIM), bf16),
            pltpu.VMEM((rows, columns), bf16),
            pltpu.VMEM((seq_count, 2, capacity, BLOCK, HEAD_DIM), bf16),
            pltpu.VMEM((2, seq_count, 2, capacity, BLOCK, HEAD_DIM), bf16),
            pltpu.VMEM((8 * -(-capacity // 8), 128), i32),
            pltpu.VMEM((shard_blocks * heads, 1, BLOCK), i32),
            pltpu.SMEM(table, i32), pltpu.SMEM(table, i32),
            pltpu.SMEM(asks, i32),
            dma((2,)), dma((2,)), dma((2,)), dma((1,)), dma((6,)), dma((7,)),
            dma((1,)), dma((seq_count,)), dma((1,)), dma((seq_count,)),
            pltpu.SemaphoreType.REGULAR((6,)),
        ],
        compiler_params=pltpu.CompilerParams(
            collective_id=1, has_side_effects=True,
            vmem_limit_bytes=67043328 - resident - 256 * 1024,
        ),
        name="fused",
    )(key_states, value_states, queries, cluster_perm, block_mask)
    return pl.pallas_call(
        functools.partial(flush_kernel, seq_count),
        out_shape=jax.ShapeDtypeStruct((rows, columns), bf16),
        in_specs=[vmem, vmem, vmem],
        out_specs=anywhere,
        scratch_shapes=[dma((1,))],
        compiler_params=pltpu.CompilerParams(vmem_limit_bytes=8 * 1024 * 1024),
        name="flush",
    )(*staged)


def attend_kernel(heads, picks, width, capacity, masked, pos_own, pos_far, *refs):
    if masked:
        query_ref, kv_ref, allow_ref, out_ref, stage, sems = refs
    else:
        query_ref, kv_ref, out_ref, stage, sems = refs
    group = lax.axis_index("head")
    scale = math.log2(math.e) / math.sqrt(HEAD_DIM)
    ones = jnp.ones((BLOCK, HEAD_DIM), jnp.bfloat16)
    span = width * HEAD_DIM
    batches = query_ref.shape[1] // span

    def put(batch, buffer):
        return pltpu.make_async_copy(
            stage.at[buffer],
            out_ref.at[:, pl.ds(pl.multiple_of(batch * span, span), span)],
            sems.at[buffer],
        )

    def one(batch, carry):
        where_, scores = [], []
        for w in range(width):
            head = batch * width + w
            away = (head // heads) != group
            local = head % heads
            query = query_ref[:, pl.ds(pl.multiple_of(head * HEAD_DIM, HEAD_DIM), HEAD_DIM)]
            for p in range(picks):
                slot = jnp.where(away, pos_far[local, p], pos_own[local, p])
                spot = (slot // capacity, slot % capacity)
                rel = away.astype(jnp.int32)
                where_.append((rel, spot))
                score = lax.dot_general(
                    query, kv_ref[rel, 0, spot[0], spot[1]], (((1,), (1,)), ((), ())),
                    preferred_element_type=jnp.float32,
                )
                if masked:
                    score = jnp.where(allow_ref[head, :, p : p + 1] > 0, score, -jnp.inf)
                scores.append(score)
        weights = []
        for w in range(width):
            own = scores[w * picks : (w + 1) * picks]
            top = jnp.max(functools.reduce(jnp.maximum, own), axis=1, keepdims=True)
            weights.extend([jnp.exp2((s - top) * scale).astype(jnp.bfloat16) for s in own])
        buffer = batch % 2

        @pl.when(batch >= 2)
        def _():
            put(batch - 2, buffer).wait()

        for w in range(width):
            parts = []
            for p in range(picks):
                rel, spot = where_[w * picks + p]
                parts.append(
                    jnp.dot(
                        weights[w * picks + p],
                        jnp.concatenate([kv_ref[rel, 1, spot[0], spot[1]], ones], axis=1),
                        preferred_element_type=jnp.float32,
                    )
                )
            mixed = functools.reduce(jnp.add, parts)
            stage[buffer, :, w * HEAD_DIM : (w + 1) * HEAD_DIM] = (
                mixed[:, :HEAD_DIM] / mixed[:, HEAD_DIM:]
            ).astype(jnp.bfloat16)
        put(batch, buffer).start()
        return carry

    lax.fori_loop(0, batches, one, 0)
    for batch in range(max(0, batches - 2), batches):
        put(batch, batch % 2).wait()


def token_allow(cluster_perm, block_mask, picks, me, shard_rows):
    needed = jnp.max(block_mask, axis=1)
    prefix = jnp.cumsum(needed, axis=1) - needed
    chosen = (needed[:, :, None] == 1) & (prefix[:, :, None] == jnp.arange(picks)[None, None, :])
    live = jnp.einsum(
        "hqb,hbp->hqp", block_mask.astype(jnp.float32), chosen.astype(jnp.float32)
    )
    group_heads = cluster_perm.shape[0]
    local = cluster_perm - me * shard_rows
    place = jnp.zeros((group_heads, shard_rows), jnp.int32)
    place = place.at[jnp.arange(group_heads)[:, None], local].set(
        jnp.broadcast_to(jnp.arange(shard_rows, dtype=jnp.int32) // BLOCK, local.shape)
    )
    by_token = jnp.take_along_axis(live, place[:, :, None], axis=1).astype(jnp.float32)
    return lax.all_to_all(by_token, "head", split_axis=1, concat_axis=0, tiled=True)


def shards(queries, key_states, value_states, cluster_perm, block_mask):
    group_heads, shard_rows = cluster_perm.shape
    shard_blocks = shard_rows // BLOCK
    seq_count = lax.axis_size("seq")
    block_total = block_mask.shape[2]
    picks = max(1, block_total // 64)
    capacity = max(
        1, min(shard_blocks, (group_heads * picks * 8 + 5 * seq_count - 1) // (5 * seq_count))
    )
    rows, columns = queries.shape
    me = lax.axis_index("seq")
    if picks == 1 and seq_count == 16 and shard_blocks * group_heads <= 256:
        return fused(key_states, value_states, queries, cluster_perm, block_mask, capacity)
    vmem = pl.BlockSpec(memory_space=pltpu.VMEM)
    anywhere = pl.BlockSpec(memory_space=pltpu.HBM)
    struct = jax.ShapeDtypeStruct
    bf16, i32 = jnp.bfloat16, jnp.int32

    dma = pltpu.SemaphoreType.DMA
    kv_half = pltpu.VMEM((group_heads, rows, HEAD_DIM), bf16)
    table = struct((group_heads, 128), i32)
    resident = 2 * (4 * seq_count * capacity * BLOCK * HEAD_DIM + rows * columns)
    grant = 67043328 - resident - 256 * 1024
    got, positions, pos_far, near_queries = pl.pallas_call(
        functools.partial(exchange_kernel, seq_count, capacity, shard_blocks, picks),
        out_shape=(
            pltpu.VMEM((2, 2, seq_count, capacity, BLOCK, HEAD_DIM), bf16), table, table,
            pltpu.VMEM((rows, columns), bf16),
        ),
        in_specs=[anywhere, anywhere, anywhere, vmem, vmem],
        out_specs=(vmem, vmem, vmem, vmem),
        scratch_shapes=[
            kv_half, kv_half, kv_half, kv_half,
            pltpu.VMEM((seq_count, 1, 128), i32),
            pltpu.VMEM((seq_count, 1, 128), i32),
            pltpu.SMEM((seq_count, 1, 128), i32),
            pltpu.VMEM((2, seq_count, capacity, BLOCK, HEAD_DIM), bf16),
            pltpu.VMEM((8 * -(-capacity // 8), 128), i32),
            pltpu.VMEM((shard_blocks * group_heads, 1, BLOCK), i32),
            dma((2 * group_heads,)), dma((2 * group_heads,)), dma((2 * group_heads,)),
            dma((seq_count,)), dma((seq_count,)), dma((7,)),
        ] + [dma((2, seq_count)) for _ in range(4)],
        compiler_params=pltpu.CompilerParams(
            collective_id=0, has_side_effects=True, vmem_limit_bytes=grant
        ),
        name="exchange",
    )(key_states, value_states, queries, cluster_perm, block_mask)

    masked = picks > 1
    total_heads = columns // HEAD_DIM
    width = 8 if total_heads % 8 == 0 else 1
    operands = [near_queries, got]
    if masked:
        operands.append(token_allow(cluster_perm, block_mask, picks, me, shard_rows))
    smem = pl.BlockSpec(memory_space=pltpu.SMEM)
    return pl.pallas_call(
        functools.partial(attend_kernel, group_heads, picks, width, capacity, masked),
        out_shape=struct((rows, columns), bf16),
        in_specs=[smem, smem] + [vmem] * len(operands),
        out_specs=anywhere,
        scratch_shapes=[pltpu.VMEM((2, rows, width * HEAD_DIM), bf16), dma((2,))],
        compiler_params=pltpu.CompilerParams(vmem_limit_bytes=24 * 1024 * 1024),
        name="attend",
    )(positions, pos_far, *operands)


def solution(mesh):
    rows = P(("seq", "head"), None)
    placed = (rows, rows, rows, P("head", "seq"), P("head", "seq", None))
    return jax.shard_map(shards, mesh=mesh, in_specs=placed, out_specs=rows, check_vma=False)
```
